32 devices in a mesh: replica: 2 (over x), shard: 16 (over z, y, core).
Axes of the slice: x: 2, y: 2, z: 4, core: 2. Of those that a mesh axis runs over, the one named last changes fastest.
Arguments:
- tokens: bfloat16 [32, 197, 768], P(('replica', 'shard')), may hold values from -6 to 6
- cotangent: bfloat16 [32, 197, 768], P(('replica', 'shard')), may hold values from -6 to 6
- norm1_gain: bfloat16 [768], P('shard'), may hold values from 0.5 to 1.5
- norm1_bias: bfloat16 [768], P('shard'), may hold values from -3 to 3
- proj_in: bfloat16 [768, 2304], P('shard'), may hold values from -0.21875 to 0.21875
- query_bias: bfloat16 [768], P('shard'), may hold values from -6 to 6
- value_bias: bfloat16 [768], P('shard'), may hold values from -3 to 3
- proj_out: bfloat16 [768, 768], P('shard'), may hold values from -0.625 to 0.625
- out_bias: bfloat16 [768], P('shard'), may hold values from -3 to 3
- norm2_gain: bfloat16 [768], P('shard'), may hold values from 0.5 to 1.5
- norm2_bias: bfloat16 [768], P('shard'), may hold values from -3 to 3
- router: bfloat16 [768, 16], P('shard'), may hold values from -0.21875 to 0.21875
- up_weight: bfloat16 [16, 768, 3072], P('shard'), may hold values from -0.21875 to 0.21875
- up_bias: bfloat16 [16, 3072], P('shard'), may hold values from -3 to 3
- down_weight: bfloat16 [16, 3072, 768], P('shard'), may hold values from -1.75 to 1.75
- down_bias: bfloat16 [16, 768], P('shard'), may hold values from -24 to 24
- expert_ids: int32 [6304, 2], P(('replica', 'shard')), may hold values from 0 to 15, as said below
- slot_ids: int32 [6304, 2], P(('replica', 'shard')), may hold values from 0 to 24, as said below
Outputs:
- block_out: bfloat16 [32, 197, 768], P(('replica', 'shard'))
- tokens_grad: bfloat16 [32, 197, 768], P(('replica', 'shard'))
- norm1_gain_grad: float32 [768], P('shard')
- norm1_bias_grad: float32 [768], P('shard')
- proj_in_grad: float32 [768, 2304], P('shard')
- query_bias_grad: float32 [768], P('shard')
- value_bias_grad: float32 [768], P('shard')
- proj_out_grad: float32 [768, 768], P('shard')
- out_bias_grad: float32 [768], P('shard')
- norm2_gain_grad: float32 [768], P('shard')
- norm2_bias_grad: float32 [768], P('shard')
- router_grad: float32 [768, 16], P('shard')
- up_weight_grad: float32 [16, 768, 3072], P('shard', None, 'replica')
- up_bias_grad: float32 [16, 3072], P('shard', 'replica')
- down_weight_grad: float32 [16, 3072, 768], P('shard', 'replica')
- down_bias_grad: float32 [16, 768], P('shard', 'replica')
The draws below stay inside these ranges and needn't reach their ends.
Inputs may be any that keep to these rules, and one draw needn't show every extreme that they name: `expert_ids`: each row names two different experts. On every device the first 25 rows all name one expert first, the same expert on every device. `slot_ids`: within the rows of one device, first choices are placed before second choices, each in row order; a pair's slot is the number of that device's earlier pairs naming the same expert, stored as 24 when it is 24 or more, which marks a dropped pair. Kept pairs of one device never share an expert and a slot; on every device one expert has all 24 slots filled and a pair dropped.
All inputs are finite; a program needn't handle non-finite values.
Results may differ from the reference program's by a relative error of at most 0.022.
Values may be sent and summed in bfloat16 or wider, within the bound.
A program may use at most 128 MiB of HBM per device.

```python
import jax
import jax.numpy as jnp
from jax import lax

D = 768
HEADS = 12
HDIM = 64
FF = 3072
SEQ = 197
EXPERTS = 16
TOK_DEV = 197
IMAGES = 32
TOKENS = 6304
CAP = 24
N_REPLICA = 2
N_SHARD = 16


def route_pairs(key):
    base = jax.random.fold_in(key, 101)
    subkeys = jax.random.split(base, 5)
    row_index = jnp.arange(TOKENS, dtype=jnp.int32) % TOK_DEV
    smallest = jnp.minimum(jnp.minimum(jax.random.randint(subkeys[0], (TOKENS,), 0, EXPERTS), jax.random.randint(subkeys[1], (TOKENS,), 0, EXPERTS)), jax.random.randint(subkeys[2], (TOKENS,), 0, EXPERTS))
    ranked = jnp.where(row_index < CAP + 1, 0, smallest).astype(jnp.int32)
    shuffle = jax.random.permutation(subkeys[3], EXPERTS).astype(jnp.int32)
    offset = jax.random.randint(subkeys[4], (TOKENS,), 1, EXPERTS).astype(jnp.int32)
    first_pick = shuffle[ranked]
    second_pick = shuffle[(ranked + offset) % EXPERTS]
    blocks = TOKENS // TOK_DEV
    queued = jnp.concatenate([first_pick.reshape(blocks, TOK_DEV), second_pick.reshape(blocks, TOK_DEV)], axis=1)
    onehot = (queued[:, :, None] == jnp.arange(EXPERTS, dtype=jnp.int32)[None, None, :]).astype(jnp.int32)
    before = jnp.cumsum(onehot, axis=1) - onehot
    placed = jnp.minimum(jnp.sum(before * onehot, axis=2), CAP).astype(jnp.int32)
    slot_first = placed[:, :TOK_DEV].reshape(TOKENS)
    slot_second = placed[:, TOK_DEV:].reshape(TOKENS)
    return (jnp.stack([first_pick, second_pick], axis=1), jnp.stack([slot_first, slot_second], axis=1))


def draw_expert_ids(key, part):
    return route_pairs(key)[0]


def draw_slot_ids(key, part):
    return route_pairs(key)[1]


def level_of(key, extent, shards, low, largest):
    def one(axis_at, parts):
        steps = jax.random.uniform(jax.random.fold_in(jax.random.fold_in(key, 6), axis_at), (parts,), jnp.float32, low / len(shards), largest / len(shards))
        return jnp.repeat(jnp.exp(steps), extent[axis_at] // parts).reshape((-1,) + (1,) * (len(extent) - axis_at - 1))

    level = one(*shards[0])
    for cut in shards[1:]:
        level = level * one(*cut)
    return level


def gaussian(key, extent, scale, limit, cuts=(), kind=jnp.bfloat16):
    entries = scale * jax.random.normal(key, extent, jnp.float32)
    if cuts:
        entries = entries * level_of(key, extent, cuts, -0.22, 0.18)
    return jnp.clip(entries, -limit, limit).astype(kind)


def setup_inputs(seed: int = 0) -> dict:
    seeds = jax.random.split(jax.random.key(seed), 19)
    return {
        "tokens": gaussian(seeds[0], (IMAGES, SEQ, D), 1.0, 6.0, ((0, 32),)),
        "cotangent": gaussian(seeds[1], (IMAGES, SEQ, D), 1.0, 6.0, ((0, 32),)),
        "norm1_gain": jnp.clip(1.0 + 0.1 * jax.random.normal(seeds[2], (D,), jnp.float32), 0.5, 1.5).astype(jnp.bfloat16),
        "norm1_bias": gaussian(seeds[3], (D,), 0.5, 3.0, ((0, 16),)),
        "proj_in": gaussian(seeds[4], (D, 3 * D), D ** -0.5, 0.21875, ((0, 16),)),
        "query_bias": gaussian(seeds[5], (D,), 1.0, 6.0, ((0, 16),)),
        "value_bias": gaussian(seeds[6], (D,), 0.5, 3.0, ((0, 16),)),
        "proj_out": gaussian(seeds[7], (D, D), (D // 8) ** -0.5, 0.625, ((0, 16),)),
        "out_bias": gaussian(seeds[8], (D,), 0.5, 3.0, ((0, 16),)),
        "norm2_gain": jnp.clip(1.0 + 0.1 * jax.random.normal(seeds[9], (D,), jnp.float32), 0.5, 1.5).astype(jnp.bfloat16),
        "norm2_bias": gaussian(seeds[10], (D,), 0.5, 3.0, ((0, 16),)),
        "router": gaussian(seeds[11], (D, EXPERTS), D ** -0.5, 0.21875, ((0, 16),)),
        "up_weight": gaussian(seeds[12], (EXPERTS, D, FF), D ** -0.5, 0.21875, ((0, 16),)),
        "up_bias": gaussian(seeds[13], (EXPERTS, FF), 0.5, 3.0, ((0, 16),)),
        "down_weight": gaussian(seeds[14], (EXPERTS, FF, D), (max(FF // 256, 1)) ** -0.5, 1.75, ((0, 16),)),
        "down_bias": gaussian(seeds[15], (EXPERTS, D), 4.0, 24.0, ((0, 16),)),
        "expert_ids": draw_expert_ids(jax.random.fold_in(seeds[18], 71), 0),
        "slot_ids": draw_slot_ids(jax.random.fold_in(seeds[18], 71), 0),
    }


EPS = 1e-06
SQRT_HALF = 0.7071067811865476
INV_ROOT_TWO_PI = 0.3989422804014327

def layer_norm(rows_in, norm_gain, norm_shift):
    average = lax.optimization_barrier(jnp.mean(rows_in, axis=-1, keepdims=True))
    centred = rows_in - average
    inv_std = lax.rsqrt(lax.optimization_barrier(jnp.mean(centred * centred, axis=-1, keepdims=True)) + EPS)
    normed = centred * inv_std
    return (normed, inv_std, normed * norm_gain + norm_shift)

def norm_back(grad_rows, normed, inv_std, norm_gain):
    scaled = grad_rows * norm_gain
    inner = scaled - lax.optimization_barrier(jnp.mean(scaled, axis=-1, keepdims=True)) - normed * lax.optimization_barrier(jnp.mean(scaled * normed, axis=-1, keepdims=True))
    return (inner * inv_std, lax.optimization_barrier(jnp.sum(grad_rows * normed, axis=0)), lax.optimization_barrier(jnp.sum(grad_rows, axis=0)))

def gelu_parts(pre_act):
    cumul = 0.5 * (1.0 + lax.erf(pre_act * SQRT_HALF))
    return (pre_act * cumul, cumul + pre_act * jnp.exp(-0.5 * pre_act * pre_act) * INV_ROOT_TWO_PI)

def split_heads(flat_rows):
    return flat_rows.reshape(-1, SEQ, HEADS, HDIM).astype(jnp.float32)

def route_table(id_block, slot_block):
    positions = jnp.arange(EXPERTS * CAP, dtype=jnp.int32)
    tables = []
    for choose in range(2):
        kept = slot_block[:, choose] < CAP
        target = jnp.where(kept, id_block[:, choose] * CAP + slot_block[:, choose], -1).astype(jnp.int32)
        tables.append((target[:, None] == positions[None, :]).astype(jnp.bfloat16))
    return tables

def pick_table(id_block):
    labels = jnp.arange(EXPERTS, dtype=jnp.int32)
    return [(id_block[:, choose][:, None] == labels[None, :]).astype(jnp.float32) for choose in range(2)]

def block_pass(dense, expert_set, tok_block, cot_block, id_block, slot_block):
    gain_one, shift_one, proj_full, query_shift, value_shift, outproj_full, out_shift, gain_two, shift_two, router_full = dense
    up_full, up_shift, down_full, down_shift = expert_set
    tok_rows = tok_block.astype(jnp.float32)
    normed_one, inv_one, pre_one = layer_norm(tok_rows, gain_one.astype(jnp.float32), shift_one.astype(jnp.float32))
    act_one = pre_one.astype(jnp.bfloat16)
    mixed = jnp.dot(act_one, proj_full, preferred_element_type=jnp.float32)
    query_part = (mixed[:, :D] + query_shift.astype(jnp.float32)).astype(jnp.bfloat16)
    key_part = mixed[:, D:2 * D].astype(jnp.bfloat16)
    value_part = (mixed[:, 2 * D:] + value_shift.astype(jnp.float32)).astype(jnp.bfloat16)
    query_heads = split_heads(query_part)
    key_heads = split_heads(key_part)
    value_heads = split_heads(value_part)
    scores = jnp.einsum('ishd,ithd->ihst', query_heads, key_heads) * HDIM ** (-0.5)
    log_total = jnp.log(lax.optimization_barrier(jnp.sum(jnp.exp(scores), axis=-1)))
    attn_probs = jnp.exp(scores - log_total[..., None]).astype(jnp.bfloat16)
    context = jnp.einsum('ihst,ithd->ishd', attn_probs.astype(jnp.float32), value_heads).reshape(-1, D).astype(jnp.bfloat16)
    resid = tok_rows + jnp.dot(context, outproj_full, preferred_element_type=jnp.float32) + out_shift.astype(jnp.float32)
    normed_two, inv_two, pre_two = layer_norm(resid, gain_two.astype(jnp.float32), shift_two.astype(jnp.float32))
    hidden = pre_two.astype(jnp.bfloat16)
    logits = jnp.dot(hidden, router_full, preferred_element_type=jnp.float32)
    exp_logits = jnp.exp(logits)
    gate_probs = exp_logits / lax.optimization_barrier(jnp.sum(exp_logits, axis=-1, keepdims=True))
    routes = route_table(id_block, slot_block)
    picks = pick_table(id_block)
    buffer = (jnp.dot(routes[0].T, hidden, preferred_element_type=jnp.float32) + jnp.dot(routes[1].T, hidden, preferred_element_type=jnp.float32)).astype(jnp.bfloat16).reshape(EXPERTS, CAP, D)
    buffer_wide = buffer.astype(jnp.float32)
    expert_pre = jnp.einsum('ecd,edf->ecf', buffer_wide, up_full) + up_shift[:, None, :]
    act_val, slope = gelu_parts(expert_pre)
    active = act_val.astype(jnp.bfloat16)
    active_wide = active.astype(jnp.float32)
    expert_out = (jnp.einsum('ecf,efd->ecd', active_wide, down_full) + down_shift[:, None, :]).astype(jnp.bfloat16).reshape(EXPERTS * CAP, D)
    gathered_pair = [jnp.dot(table, expert_out, preferred_element_type=jnp.float32) for table in routes]
    gate_pair = [lax.optimization_barrier(jnp.sum(gate_probs * pick, axis=-1)) for pick in picks]
    moe_sum = gate_pair[0][:, None] * gathered_pair[0] + gate_pair[1][:, None] * gathered_pair[1]
    out_rows = (resid + moe_sum).astype(jnp.bfloat16)
    grad_out = cot_block.astype(jnp.float32)
    grad_gate = [lax.optimization_barrier(jnp.sum(grad_out * part, axis=-1)) for part in gathered_pair]
    sent = [(gate[:, None] * grad_out).astype(jnp.bfloat16) for gate in gate_pair]
    grad_buffer = (jnp.dot(routes[0].T, sent[0], preferred_element_type=jnp.float32) + jnp.dot(routes[1].T, sent[1], preferred_element_type=jnp.float32)).astype(jnp.bfloat16).reshape(EXPERTS, CAP, D)
    grad_buffer_wide = grad_buffer.astype(jnp.float32)
    grad_active = jnp.einsum('ecd,efd->ecf', grad_buffer_wide, down_full)
    grad_pre = (grad_active * slope).astype(jnp.bfloat16)
    grad_pre_wide = grad_pre.astype(jnp.float32)
    expert_terms = (jnp.einsum('ecd,ecf->edf', buffer_wide, grad_pre_wide), lax.optimization_barrier(jnp.sum(grad_pre_wide, axis=1)), jnp.einsum('ecf,ecd->efd', active_wide, grad_buffer_wide), lax.optimization_barrier(jnp.sum(grad_buffer_wide, axis=1)))
    grad_in = jnp.einsum('ecf,edf->ecd', grad_pre_wide, up_full).astype(jnp.bfloat16).reshape(EXPERTS * CAP, D)
    grad_moe = jnp.dot(routes[0], grad_in, preferred_element_type=jnp.float32) + jnp.dot(routes[1], grad_in, preferred_element_type=jnp.float32)
    grad_gates = picks[0] * grad_gate[0][:, None] + picks[1] * grad_gate[1][:, None]
    grad_logits = (gate_probs * (grad_gates - lax.optimization_barrier(jnp.sum(gate_probs * grad_gates, axis=-1, keepdims=True)))).astype(jnp.bfloat16)
    router_term = jnp.dot(hidden.T, grad_logits, preferred_element_type=jnp.float32)
    grad_norm_two = grad_moe + jnp.dot(grad_logits, router_full.T, preferred_element_type=jnp.float32)
    grad_resid_two, gain_two_term, shift_two_term = norm_back(grad_norm_two, normed_two, inv_two, gain_two.astype(jnp.float32))
    grad_resid = grad_out + grad_resid_two
    resid_bf = grad_resid.astype(jnp.bfloat16)
    out_shift_term = lax.optimization_barrier(jnp.sum(grad_resid, axis=0))
    outproj_term = jnp.dot(context.T, resid_bf, preferred_element_type=jnp.float32)
    grad_context = jnp.dot(resid_bf, outproj_full.T, preferred_element_type=jnp.float32).astype(jnp.bfloat16)
    context_heads = split_heads(grad_context)
    scores_again = jnp.einsum('ishd,ithd->ihst', query_heads, key_heads) * HDIM ** (-0.5)
    probs_full = jnp.exp(scores_again - log_total[..., None])
    grad_probs = jnp.einsum('ishd,ithd->ihst', context_heads, value_heads)
    grad_scores = (probs_full * (grad_probs - lax.optimization_barrier(jnp.sum(probs_full * grad_probs, axis=-1, keepdims=True))) * HDIM ** (-0.5)).astype(jnp.bfloat16).astype(jnp.float32)
    probs_bf = probs_full.astype(jnp.bfloat16).astype(jnp.float32)
    grad_value = jnp.einsum('ihst,ishd->ithd', probs_bf, context_heads).reshape(-1, D)
    grad_query = jnp.einsum('ihst,ithd->ishd', grad_scores, key_heads).reshape(-1, D)
    grad_key = jnp.einsum('ihst,ishd->ithd', grad_scores, query_heads).reshape(-1, D)
    grad_mixed = jnp.concatenate([grad_query, grad_key, grad_value], axis=1).astype(jnp.bfloat16)
    proj_term = jnp.dot(act_one.T, grad_mixed, preferred_element_type=jnp.float32)
    grad_act = jnp.dot(grad_mixed, proj_full.T, preferred_element_type=jnp.float32)
    grad_tok_norm, gain_one_term, shift_one_term = norm_back(grad_act, normed_one, inv_one, gain_one.astype(jnp.float32))
    grad_rows = (grad_resid + grad_tok_norm).astype(jnp.bfloat16)
    dense_terms = (gain_one_term, shift_one_term, proj_term, lax.optimization_barrier(jnp.sum(grad_query, axis=0)), lax.optimization_barrier(jnp.sum(grad_value, axis=0)), outproj_term, out_shift_term, gain_two_term, shift_two_term, router_term)
    return (out_rows, grad_rows, dense_terms, expert_terms)

def add_pairs(first_set, second_set):
    return tuple((left + right for left, right in zip(first_set, second_set)))

def reference(tokens, cotangent, norm1_gain, norm1_bias, proj_in, query_bias, value_bias, proj_out, out_bias, norm2_gain, norm2_bias, router, up_weight, up_bias, down_weight, down_bias, expert_ids, slot_ids):
    dense = (norm1_gain, norm1_bias, proj_in, query_bias, value_bias, proj_out, out_bias, norm2_gain, norm2_bias, router)
    expert_set = (up_weight.astype(jnp.float32), up_bias.astype(jnp.float32), down_weight.astype(jnp.float32), down_bias.astype(jnp.float32))
    grouped = (tokens.reshape(N_REPLICA, N_SHARD, TOK_DEV, D), cotangent.reshape(N_REPLICA, N_SHARD, TOK_DEV, D), expert_ids.reshape(N_REPLICA, N_SHARD, TOK_DEV, 2), slot_ids.reshape(N_REPLICA, N_SHARD, TOK_DEV, 2))
    dense_zero = tuple((jnp.zeros(param.shape, jnp.float32) for param in dense))
    expert_zero = tuple((jnp.zeros(param.shape, jnp.float32) for param in expert_set))

    def shard_step(carry, block):
        dense_acc, expert_acc = carry
        out_rows, grad_rows, dense_terms, expert_terms = block_pass(dense, expert_set, block[0], block[1], block[2], block[3])
        return ((add_pairs(dense_acc, dense_terms), add_pairs(expert_acc, expert_terms)), (out_rows, grad_rows))

    def replica_step(carry, group):
        dense_acc, expert_acc = carry
        (dense_acc, expert_group), out_pair = lax.scan(shard_step, (dense_acc, expert_zero), group)
        rounded = tuple((lax.optimization_barrier(term.astype(jnp.bfloat16)).astype(jnp.float32) for term in expert_group))
        return ((dense_acc, add_pairs(expert_acc, rounded)), out_pair)
    (dense_grads, expert_grads), out_pair = lax.scan(replica_step, (dense_zero, expert_zero), grouped)
    block_out = out_pair[0].reshape(IMAGES, SEQ, D)
    tokens_grad = out_pair[1].reshape(IMAGES, SEQ, D)
    return (block_out, tokens_grad, dense_grads[0], dense_grads[1], dense_grads[2], dense_grads[3], dense_grads[4], dense_grads[5], dense_grads[6], dense_grads[7], dense_grads[8], dense_grads[9], expert_grads[0], expert_grads[1], expert_grads[2], expert_grads[3])
```

```python
import functools
from types import SimpleNamespace

import jax
import jax.numpy as jnp
from jax import lax
from jax.experimental import pallas as pl
from jax.experimental.pallas import tpu as pltpu
from jax.sharding import PartitionSpec as P

D = 768
HEADS = 12
HDIM = 64
SEQ = 197


EPS = 1e-06
SQRT_HALF = 0.7071067811865476
INV_ROOT_TWO_PI = 0.3989422804014327


def layer_norm(rows_in, norm_gain, norm_shift):
    average = jnp.mean(rows_in, axis=-1, keepdims=True)
    centred = rows_in - average
    inv_std = lax.rsqrt(jnp.mean(centred * centred, axis=-1, keepdims=True) + EPS)
    normed = centred * inv_std
    return (normed, inv_std, normed * norm_gain + norm_shift)


def norm_back(grad_rows, normed, inv_std, norm_gain):
    scaled = grad_rows * norm_gain
    inner = (
        scaled
        - jnp.mean(scaled, axis=-1, keepdims=True)
        - normed * jnp.mean(scaled * normed, axis=-1, keepdims=True)
    )
    return (inner * inv_std, jnp.sum(grad_rows * normed, axis=0), jnp.sum(grad_rows, axis=0))


def gelu_parts(pre_act):
    cumul = 0.5 * (1.0 + lax.erf(pre_act * SQRT_HALF))
    return (pre_act * cumul, cumul + pre_act * jnp.exp(-0.5 * pre_act * pre_act) * INV_ROOT_TWO_PI)


def route_table(expert_ids, slot_ids, experts, capacity):
    positions = jnp.arange(experts * capacity, dtype=jnp.int32)
    tables = []
    for choose in range(2):
        kept = slot_ids[:, choose] < capacity
        target = jnp.where(kept, expert_ids[:, choose] * capacity + slot_ids[:, choose], -1)
        tables.append((target[:, None] == positions[None, :]).astype(jnp.bfloat16))
    return tables


def pick_table(expert_ids, experts):
    labels = jnp.arange(experts, dtype=jnp.int32)
    return [
        (expert_ids[:, choose][:, None] == labels[None, :]).astype(jnp.float32)
        for choose in range(2)
    ]


def lane_pad(blocks):
    rows = blocks[0].shape[0]
    spare = -sum(block.shape[1] for block in blocks) % 128
    return jnp.concatenate(blocks + [jnp.zeros((rows, spare), blocks[0].dtype)], axis=1)


def other_replicas(value):
    size = lax.axis_size("replica")
    return [
        lax.ppermute(value, "replica", [(at, (at + step) % size) for at in range(size)])
        for step in range(1, size)
    ]


def to_expert(value, local_experts, capacity):
    shards, width = value.shape[0], value.shape[-1]
    return (
        value.reshape(shards, local_experts, capacity, width)
        .swapaxes(0, 1)
        .reshape(local_experts, shards * capacity, width)
    )


def from_expert(value, shards, capacity):
    local_experts, width = value.shape[0], value.shape[-1]
    return (
        value.reshape(local_experts, shards, capacity, width)
        .swapaxes(0, 1)
        .reshape(shards, local_experts * capacity, width)
    )


def expert_middle(rows, grad_rows, up_weight, up_bias, down_weight):
    expert_pre = (
        jnp.einsum("ecd,edf->ecf", rows, up_weight, preferred_element_type=jnp.float32)
        + up_bias.astype(jnp.float32)[:, None, :]
    )
    act_val, slope = gelu_parts(expert_pre)
    grad_active = jnp.einsum(
        "ecd,efd->ecf", grad_rows, down_weight, preferred_element_type=jnp.float32
    )
    return (act_val.astype(jnp.bfloat16), (grad_active * slope).astype(jnp.bfloat16))


def plain_body(
    tokens,
    cotangent,
    norm1_gain,
    norm1_bias,
    proj_in,
    query_bias,
    value_bias,
    proj_out,
    out_bias,
    norm2_gain,
    norm2_bias,
    router,
    up_weight,
    up_bias,
    down_weight,
    down_bias,
    expert_ids,
    slot_ids,
):
    images = tokens.shape[0]
    small = jnp.stack(
        [norm1_gain, norm1_bias, query_bias, value_bias, out_bias, norm2_gain, norm2_bias],
        axis=1,
    )
    width_in, width_small = proj_in.shape[1], small.shape[1] + router.shape[1]
    first = lax.all_gather(
        lane_pad([proj_in, proj_out, small, router]), "shard", axis=0, tiled=True
    )
    width_both = width_in + proj_out.shape[1]
    proj_full = first[:, :width_in]
    outproj_full = first[:, width_in:width_both]
    small_full = first[:, width_both : width_both + small.shape[1]]
    router_full = first[:, width_both + small.shape[1] : width_both + width_small]
    (
        gain_one,
        shift_one,
        query_shift,
        value_shift,
        out_shift,
        gain_two,
        shift_two,
    ) = [row for row in small_full.T]
    tok_rows = tokens.reshape(-1, D).astype(jnp.float32)
    normed_one, inv_one, pre_one = layer_norm(
        tok_rows, gain_one.astype(jnp.float32), shift_one.astype(jnp.float32)
    )
    act_one = pre_one.astype(jnp.bfloat16)
    mixed = jnp.dot(act_one, proj_full, preferred_element_type=jnp.float32)
    query_part = (mixed[:, :D] + query_shift.astype(jnp.float32)).astype(jnp.bfloat16)
    key_part = mixed[:, D : 2 * D].astype(jnp.bfloat16)
    value_part = (mixed[:, 2 * D :] + value_shift.astype(jnp.float32)).astype(jnp.bfloat16)
    query_heads = query_part.reshape(images, SEQ, HEADS, HDIM)
    key_heads = key_part.reshape(images, SEQ, HEADS, HDIM)
    value_heads = value_part.reshape(images, SEQ, HEADS, HDIM)
    scores = jnp.einsum(
        "ishd,ithd->ihst", query_heads, key_heads, preferred_element_type=jnp.float32
    ) * HDIM ** (-0.5)
    log_total = jnp.log(jnp.sum(jnp.exp(scores), axis=-1))
    attn_probs = jnp.exp(scores - log_total[..., None]).astype(jnp.bfloat16)
    context = (
        jnp.einsum("ihst,ithd->ishd", attn_probs, value_heads, preferred_element_type=jnp.float32)
        .reshape(-1, D)
        .astype(jnp.bfloat16)
    )
    resid = (
        tok_rows
        + jnp.dot(context, outproj_full, preferred_element_type=jnp.float32)
        + out_shift.astype(jnp.float32)
    )
    normed_two, inv_two, pre_two = layer_norm(
        resid, gain_two.astype(jnp.float32), shift_two.astype(jnp.float32)
    )
    hidden = pre_two.astype(jnp.bfloat16)
    logits = jnp.dot(hidden, router_full, preferred_element_type=jnp.float32)
    exp_logits = jnp.exp(logits)
    gate_probs = exp_logits / jnp.sum(exp_logits, axis=-1, keepdims=True)
    local_experts = up_weight.shape[0]
    experts = local_experts * lax.axis_size("shard")
    capacity = 2 * tok_rows.shape[0] // experts
    routes = route_table(expert_ids, slot_ids, experts, capacity)
    picks = pick_table(expert_ids, experts)
    both = jnp.concatenate(routes, axis=0)
    either = routes[0] + routes[1]
    gate_pair = [jnp.sum(gate_probs * pick, axis=-1) for pick in picks]
    grad_out = cotangent.reshape(-1, D).astype(jnp.float32)
    sent = jnp.concatenate(
        [(gate[:, None] * grad_out).astype(jnp.bfloat16) for gate in gate_pair], axis=0
    )
    buffer = jnp.dot(either.T, hidden, preferred_element_type=jnp.float32)
    grad_buffer = jnp.dot(both.T, sent, preferred_element_type=jnp.float32)
    shards = lax.axis_size("shard")
    outgoing = (
        jnp.concatenate([buffer, grad_buffer], axis=1)
        .astype(jnp.bfloat16)
        .reshape(shards, local_experts * capacity, 2 * D)
    )
    landed = to_expert(
        lax.all_to_all(outgoing, "shard", split_axis=0, concat_axis=0, tiled=True),
        local_experts,
        capacity,
    )
    arrived, grad_arrived = landed[..., :D], landed[..., D:]
    others = other_replicas(landed)
    active, grad_pre = expert_middle(arrived, grad_arrived, up_weight, up_bias, down_weight)
    expert_out = (
        jnp.einsum("ecf,efd->ecd", active, down_weight, preferred_element_type=jnp.float32)
        + down_bias.astype(jnp.float32)[:, None, :]
    ).astype(jnp.bfloat16)
    grad_in = jnp.einsum(
        "ecf,edf->ecd", grad_pre, up_weight, preferred_element_type=jnp.float32
    ).astype(jnp.bfloat16)
    answer = from_expert(jnp.concatenate([expert_out, grad_in], axis=2), shards, capacity)
    back = lax.all_to_all(answer, "shard", split_axis=0, concat_axis=0, tiled=True).reshape(
        experts * capacity, 2 * D
    )
    returned, grad_back = back[:, :D], back[:, D:]

    replicas = lax.axis_size("replica")
    ours = lax.axis_index("replica")
    part = up_weight.shape[2] // replicas
    up_part = lax.dynamic_slice_in_dim(up_weight, ours * part, part, axis=2)
    up_bias_part = lax.dynamic_slice_in_dim(up_bias, ours * part, part, axis=1)
    down_part = lax.dynamic_slice_in_dim(down_weight, ours * part, part, axis=1)
    active_parts = [lax.dynamic_slice_in_dim(active, ours * part, part, axis=2)]
    grad_pre_parts = [lax.dynamic_slice_in_dim(grad_pre, ours * part, part, axis=2)]
    for other in others:
        other_active, other_pre = expert_middle(
            other[..., :D], other[..., D:], up_part, up_bias_part, down_part
        )
        active_parts.append(other_active)
        grad_pre_parts.append(other_pre)
    all_rows = jnp.concatenate([landed] + others, axis=1)
    all_active = jnp.concatenate(active_parts, axis=1)
    all_pre = jnp.concatenate(grad_pre_parts, axis=1)
    width_part = D // replicas
    expert_grads = (
        jnp.einsum("ecd,ecf->edf", all_rows[..., :D], all_pre, preferred_element_type=jnp.float32),
        jnp.sum(all_pre, axis=1, dtype=jnp.float32),
        jnp.einsum(
            "ecf,ecd->efd", all_active, all_rows[..., D:], preferred_element_type=jnp.float32
        ),
        lax.dynamic_slice_in_dim(
            jnp.sum(all_rows[..., D:], axis=1, dtype=jnp.float32),
            ours * width_part,
            width_part,
            axis=1,
        ),
    )

    rows_here = tok_rows.shape[0]
    gathered_both = jnp.dot(both, returned, preferred_element_type=jnp.float32)
    gathered_pair = [gathered_both[:rows_here], gathered_both[rows_here:]]
    moe_sum = gate_pair[0][:, None] * gathered_pair[0] + gate_pair[1][:, None] * gathered_pair[1]
    block_out = (resid + moe_sum).astype(jnp.bfloat16).reshape(tokens.shape)
    grad_gate = [jnp.sum(grad_out * part_k, axis=-1) for part_k in gathered_pair]
    back_gain_one, back_proj, back_outproj, back_gain_two, back_router = (
        gain_one,
        proj_full,
        outproj_full,
        gain_two,
        router_full,
    )
    grad_moe = jnp.dot(either, grad_back, preferred_element_type=jnp.float32)
    grad_gates = picks[0] * grad_gate[0][:, None] + picks[1] * grad_gate[1][:, None]
    grad_logits = (
        gate_probs * (grad_gates - jnp.sum(gate_probs * grad_gates, axis=-1, keepdims=True))
    ).astype(jnp.bfloat16)
    router_term = jnp.dot(hidden.T, grad_logits, preferred_element_type=jnp.float32)
    grad_norm_two = grad_moe + jnp.dot(
        grad_logits, back_router.T, preferred_element_type=jnp.float32
    )
    grad_resid_two, gain_two_term, shift_two_term = norm_back(
        grad_norm_two, normed_two, inv_two, back_gain_two.astype(jnp.float32)
    )
    grad_resid = grad_out + grad_resid_two
    resid_bf = grad_resid.astype(jnp.bfloat16)
    out_shift_term = jnp.sum(grad_resid, axis=0)
    outproj_term = jnp.dot(context.T, resid_bf, preferred_element_type=jnp.float32)
    grad_context = (
        jnp.dot(resid_bf, back_outproj.T, preferred_element_type=jnp.float32)
        .astype(jnp.bfloat16)
        .reshape(images, SEQ, HEADS, HDIM)
    )
    scores_again = jnp.einsum(
        "ishd,ithd->ihst", query_heads, key_heads, preferred_element_type=jnp.float32
    ) * HDIM ** (-0.5)
    probs_full = jnp.exp(scores_again - log_total[..., None])
    grad_probs = jnp.einsum(
        "ishd,ithd->ihst", grad_context, value_heads, preferred_element_type=jnp.float32
    )
    grad_scores = (
        probs_full
        * (grad_probs - jnp.sum(probs_full * grad_probs, axis=-1, keepdims=True))
        * HDIM ** (-0.5)
    ).astype(jnp.bfloat16)
    probs_bf = probs_full.astype(jnp.bfloat16)
    grad_value = jnp.einsum(
        "ihst,ishd->ithd", probs_bf, grad_context, preferred_element_type=jnp.float32
    ).reshape(-1, D)
    grad_query = jnp.einsum(
        "ihst,ithd->ishd", grad_scores, key_heads, preferred_element_type=jnp.float32
    ).reshape(-1, D)
    grad_key = jnp.einsum(
        "ihst,ishd->ithd", grad_scores, query_heads, preferred_element_type=jnp.float32
    ).reshape(-1, D)
    grad_mixed = jnp.concatenate([grad_query, grad_key, grad_value], axis=1).astype(jnp.bfloat16)
    proj_term = jnp.dot(act_one.T, grad_mixed, preferred_element_type=jnp.float32)
    grad_act = jnp.dot(grad_mixed, back_proj.T, preferred_element_type=jnp.float32)
    grad_tok_norm, gain_one_term, shift_one_term = norm_back(
        grad_act, normed_one, inv_one, back_gain_one.astype(jnp.float32)
    )
    tokens_grad = (grad_resid + grad_tok_norm).astype(jnp.bfloat16).reshape(tokens.shape)
    query_shift_term = jnp.sum(grad_query, axis=0)
    value_shift_term = jnp.sum(grad_value, axis=0)
    column_sums = [
        gain_one_term,
        shift_one_term,
        query_shift_term,
        value_shift_term,
        out_shift_term,
        gain_two_term,
        shift_two_term,
    ]
    summed = lax.psum_scatter(
        lane_pad(
            [
                proj_term.astype(jnp.bfloat16),
                outproj_term.astype(jnp.bfloat16),
                lax.optimization_barrier(
                    lane_pad(
                        [
                            jnp.stack(column_sums, axis=0).astype(jnp.bfloat16).T,
                            router_term.astype(jnp.bfloat16),
                        ]
                    )
                ),
            ]
        ),
        "shard",
        scatter_dimension=0,
        tiled=True,
    )
    total = summed.astype(jnp.float32)
    for other in other_replicas(summed):
        total = total + other.astype(jnp.float32)
    small_total = total[:, width_both:]
    columns = len(column_sums)
    dense_grads = (
        small_total[:, 0],
        small_total[:, 1],
        total[:, :width_in],
        small_total[:, 2],
        small_total[:, 3],
        total[:, width_in:width_both],
        small_total[:, 4],
        small_total[:, 5],
        small_total[:, 6],
        small_total[:, columns : columns + experts],
    )
    return (
        block_out,
        tokens_grad,
        dense_grads[0],
        dense_grads[1],
        dense_grads[2],
        dense_grads[3],
        dense_grads[4],
        dense_grads[5],
        dense_grads[6],
        dense_grads[7],
        dense_grads[8],
        dense_grads[9],
        expert_grads[0],
        expert_grads[1],
        expert_grads[2],
        expert_grads[3],
    )


F32 = jnp.float32
BF16 = jnp.bfloat16
LANES = 128
VECTORS = 7


def dot(left, right):
    return jnp.dot(left, right, preferred_element_type=F32)


def dot_nt(left, right):
    return lax.dot_general(left, right, (((1,), (1,)), ((), ())), preferred_element_type=F32)


def dot_tn(left, right):
    return lax.dot_general(left, right, (((0,), (0,)), ((), ())), preferred_element_type=F32)


def iota(shape, axis):
    return lax.broadcasted_iota(jnp.int32, shape, axis)


class Plan:
    def __init__(self, shards, replicas, rows, hidden_units, local_experts):
        self.S, self.R, self.T, self.FF = shards, replicas, rows, hidden_units
        self.E = local_experts * shards
        self.C = 2 * rows // self.E
        self.TP = -(-rows // 16) * 16
        self.K = D // shards
        self.q = 2 if self.C % 16 and (2 * self.C) % 16 == 0 else 1
        self.CR = self.C if self.q == 2 else -(-self.C // 16) * 16
        self.BR = self.CR * self.q
        self.LW = D // self.q
        self.SB = shards * self.BR
        self.N = shards * self.CR
        self.part = hidden_units // replicas
        self.core = 2
        chips = shards // 2
        self.Z = 4 if chips % 4 == 0 else chips
        self.Y = chips // self.Z


def block_kernel(
    plan, out_names, tok, cot, w_in, w_out, router, ids, slots, upb, downb, *refs, **scratch
):
    vectors, (up_h, down_h), refs = refs[:VECTORS], refs[VECTORS : VECTORS + 2], refs[VECTORS + 2 :]
    r_ = SimpleNamespace(
        tok=tok, cot=cot, w_in=w_in, w_out=w_out, ids=ids, slots=slots, upb=upb,
        downb=downb, up_h=up_h, down_h=down_h, **dict(zip(out_names, refs)), **scratch,
    )
    r_.rbuf, r_.obuf = r_.hbuf, r_.cbuf
    S, R, T, TP, FF, E, C = plan.S, plan.R, plan.T, plan.TP, plan.FF, plan.E, plan.C
    K, q, CR, BR, LW, SB, N, Z, Y = (
        plan.K, plan.q, plan.CR, plan.BR, plan.LW, plan.SB, plan.N, plan.Z, plan.Y,
    )
    part = plan.part
    me = lax.axis_index("shard")
    mine = lax.axis_index("replica")
    core = lax.rem(me, 2)
    at_y = lax.rem(lax.div(me, 2), Y)
    at_z = lax.div(me, 2 * Y)
    other_core = 1 - core

    def shard_of(z, y, c):
        return (z * Y + y) * 2 + c

    def turn(base, step, size):
        return lax.rem(base + step, size)

    def copy_to(src, dst, send, recv, **device):
        return pltpu.make_async_remote_copy(
            src_ref=src, dst_ref=dst, send_sem=send, recv_sem=recv,
            device_id=device, device_id_type=pl.DeviceIdType.MESH,
        )

    load_up = pltpu.make_async_copy(r_.up_h, r_.up, r_.load_sem.at[0])
    load_down = pltpu.make_async_copy(r_.down_h, r_.down, r_.load_sem.at[1])
    load_up.start()
    load_down.start()

    turned = r_.turned
    turned[...] = jnp.zeros((LANES, LANES), F32)
    turned[0:E, 0:K] = router[...].astype(F32)
    for i, vector_ref in enumerate(vectors):
        turned[E + i : E + i + 1, 0:K] = vector_ref[...].astype(F32).reshape(1, K)
    r_.small[...] = turned[...].T[0:K, :].astype(BF16)

    barrier = pltpu.get_barrier_semaphore()
    for step in range(1, S):
        pl.semaphore_signal(
            barrier, inc=1, device_id={"shard": turn(me, step, S)}, device_id_type=pl.DeviceIdType.MESH
        )
    for step in range(1, R):
        pl.semaphore_signal(
            barrier, inc=1, device_id={"replica": turn(mine, step, R)}, device_id_type=pl.DeviceIdType.MESH
        )
    pl.semaphore_wait(barrier, S - 1 + R - 1)

    gathers = [(r_.small, r_.smf), (r_.w_in, r_.wf_in), (r_.w_out, r_.wf_out)]
    sent = [[], [], []]

    def block_of(ref, s):
        return ref.at[pl.ds(pl.multiple_of(s * K, 16), K), :]

    def send_block(a, s, src, peer):
        copy = copy_to(
            src, block_of(gathers[a][1], s), r_.ag_send.at[a, len(sent[a])], r_.ag_recv.at[a, s],
            shard=peer,
        )
        copy.start()
        sent[a].append(copy)

    def wait_block(a, s):
        copy_to(
            gathers[a][0], block_of(gathers[a][1], s), r_.ag_send.at[a, 0], r_.ag_recv.at[a, s],
            shard=s,
        ).wait_recv()

    def gather_start(a):
        src = gathers[a][0]
        for dz in range(1, Z):
            send_block(a, me, src, shard_of(turn(at_z, dz, Z), at_y, core))
        for dy in range(1, Y):
            send_block(a, me, src, shard_of(at_z, turn(at_y, dy, Y), core))
        send_block(a, me, src, shard_of(at_z, at_y, other_core))
        gathers[a][1][pl.ds(pl.multiple_of(me * K, 16), K), :] = src[...]

    def gather_z(a):
        for dz in [d for d in (1, 3, 2) if d < Z] + list(range(4, Z)):
            s = shard_of(turn(at_z, dz, Z), at_y, core)
            wait_block(a, s)
            src = block_of(gathers[a][1], s)
            for dy in range(1, Y):
                send_block(a, s, src, shard_of(at_z, turn(at_y, dy, Y), core))
            send_block(a, s, src, shard_of(at_z, at_y, other_core))

    def gather_y(a):
        for dz in range(Z):
            for dy in range(1, Y):
                s = shard_of(turn(at_z, dz, Z), turn(at_y, dy, Y), core)
                wait_block(a, s)
                send_block(a, s, block_of(gathers[a][1], s), shard_of(at_z, at_y, other_core))

    def gather_end(a):
        for dz in range(Z):
            for dy in range(Y):
                wait_block(a, shard_of(turn(at_z, dz, Z), turn(at_y, dy, Y), other_core))

    for a in range(3):
        gather_start(a)

    def rows_start(buf, land, sems):
        land[me] = buf[me]

        def go(step, carry):
            peer = turn(me, step, S)
            copy_to(
                buf.at[peer], land.at[me], sems.at[0, step], sems.at[1, me], shard=peer
            ).start()
            return carry

        lax.fori_loop(1, S, go, 0)

    def rows_wait(buf, land, sems):
        def go(step, carry):
            src = turn(me, step, S)
            copy_to(
                buf.at[src], land.at[src], sems.at[0, step], sems.at[1, src], shard=src
            ).wait_recv()
            return carry

        lax.fori_loop(1, S, go, 0)

    def rows_drain(buf, land, sems):
        def go(step, carry):
            peer = turn(me, step, S)
            copy_to(
                buf.at[peer], land.at[me], sems.at[0, step], sems.at[1, me], shard=peer
            ).wait_send()
            return carry

        lax.fori_loop(1, S, go, 0)

    def replicas_copies(land, others, sems):
        return [
            copy_to(
                land, others.at[step - 1], sems.at[0, step], sems.at[1, step],
                replica=turn(mine, step, R),
            )
            for step in range(1, R)
        ]

    pairs_at = r_.pairs_at
    pairs_at[...] = jnp.full(pairs_at.shape, C, F32)
    pairs_at[0:2, 0:T] = r_.ids[...].astype(F32)
    pairs_at[2:4, 0:T] = r_.slots[...].astype(F32)
    pair_columns = pairs_at[...].T[0:TP, :].astype(jnp.int32)
    ids_v, slots_v = pair_columns[:, 0:2], pair_columns[:, 2:4]
    columns = iota((TP, SB), 1)
    for k in range(2):
        base = jnp.where(
            slots_v[:, k : k + 1] < C, ids_v[:, k : k + 1] * BR + slots_v[:, k : k + 1], -4 * SB
        )
        for i in range(q):
            r_.place[k, i] = jnp.where(columns == base + i * CR, 1.0, 0.0).astype(BF16)

    slot_row = iota((N, SB), 0)
    slot_peer = lax.shift_right_logical(slot_row * (65536 // CR + 1), 16)
    slot_col = slot_peer * BR + (slot_row - slot_peer * CR)
    for i in range(q):
        r_.unroll[i] = jnp.where(iota((N, SB), 1) == slot_col + i * CR, 1.0, 0.0).astype(BF16)

    def pack_tokens(src, dst):
        acc = None
        for i in range(q):
            table = r_.place[0, i] + r_.place[1, i]
            term = dot_tn(table, src[:, i * LW : (i + 1) * LW])
            acc = term if acc is None else acc + term
        dst[...] = acc.astype(BF16).reshape(S, BR, LW)

    def unpack(land, dst):
        flat = land.reshape(SB, LW)
        for i in range(q):
            dst[:, i * LW : (i + 1) * LW] = dot(r_.unroll[i], flat).astype(BF16)

    def pack_slots(value, dst):
        acc = None
        for i in range(q):
            term = dot_tn(r_.unroll[i], value[:, i * LW : (i + 1) * LW])
            acc = term if acc is None else acc + term
        dst[...] = acc.astype(BF16).reshape(S, BR, LW)

    tokf, cotf, n1, n2, resid, gres = r_.tokf, r_.cotf, r_.n1, r_.n2, r_.resid, r_.gres
    tokf[T - T % 8 :, :] = jnp.zeros((TP - (T - T % 8), D), F32)
    cotf[T - T % 8 :, :] = jnp.zeros((TP - (T - T % 8), D), F32)
    tokf[0:T, :] = r_.tok[...].astype(F32)
    cotf[0:T, :] = r_.cot[...].astype(F32)
    r_.tmpb[...] = cotf[...].astype(BF16)
    pack_tokens(r_.tmpb, r_.cbuf)

    def normalise(rows):
        average = jnp.mean(rows, axis=-1, keepdims=True)
        centred = rows - average
        inv = lax.rsqrt(jnp.mean(centred * centred, axis=-1, keepdims=True) + EPS)
        return centred * inv, inv

    normed_one, inv_one = normalise(tokf[...])
    n1[...] = normed_one

    gather_z(0)
    gather_z(1)
    gather_y(0)
    gather_end(0)
    r_.smt[...] = r_.smf[...].astype(F32).T
    smt = r_.smt

    def vector(i):
        return smt[E + i : E + i + 1, :]

    r_.act1[...] = (n1[...] * vector(0) + vector(1)).astype(BF16)
    bias = r_.bias
    bias[:, 0:D] = jnp.broadcast_to(vector(2), (8, D))
    bias[:, D : 2 * D] = jnp.zeros((8, D), F32)
    bias[:, 2 * D : 3 * D] = jnp.broadcast_to(vector(3), (8, D))
    gather_y(1)
    gather_end(1)
    rows_start(r_.cbuf, r_.cland, r_.c_sem)

    WT = 256

    def qkv_step(j, carry):
        cut = pl.ds(pl.multiple_of(j * WT, WT), WT)
        value = dot(r_.act1[...], r_.wf_in[:, cut]) + bias[0:1, cut]
        r_.qkv[:, cut] = value.astype(BF16)
        return carry

    lax.fori_loop(0, 3 * D // WT, qkv_step, 0)
    gather_z(2)

    low = iota((TP, LANES), 1) < HDIM
    key_ok = iota((TP, TP), 1) < T
    scale = HDIM ** (-0.5)

    def halves(value):
        zero = jnp.zeros_like(value)
        return jnp.where(low, value, zero), jnp.where(low, zero, value)

    def pair_cuts(i):
        return [pl.ds(pl.multiple_of(i * LANES + off, LANES), LANES) for off in (0, D, 2 * D)]

    def attend(i, carry):
        cut_q, cut_k, cut_v = pair_cuts(i)
        keys, values = r_.qkv[:, cut_k], r_.qkv[:, cut_v]
        found = []
        for a, query in enumerate(halves(r_.qkv[:, cut_q])):
            scores = dot_nt(query, keys) * scale
            weight = jnp.where(key_ok, jnp.exp(scores), 0.0)
            probs = weight * (1.0 / jnp.sum(weight, axis=-1, keepdims=True))
            r_.probs[2 * i + a] = probs
            found.append(dot(probs.astype(BF16), values))
        r_.ctx[:, cut_q] = jnp.where(low, found[0], found[1]).astype(BF16)
        return carry

    pairs = HEADS // 2
    lax.fori_loop(0, pairs // 2, attend, 0)
    gather_y(2)
    lax.fori_loop(pairs // 2, pairs, attend, 0)
    gather_end(2)
    for j in range(D // WT):
        cut = slice(j * WT, (j + 1) * WT)
        resid[:, cut] = tokf[:, cut] + dot(r_.ctx[...], r_.wf_out[:, cut]) + vector(4)[:, cut]
    normed_two, inv_two = normalise(resid[...])
    n2[...] = normed_two
    r_.hid[...] = (normed_two * vector(5) + vector(6)).astype(BF16)
    pack_tokens(r_.hid, r_.hbuf)
    rows_wait(r_.cbuf, r_.cland, r_.c_sem)
    rows_start(r_.hbuf, r_.hland, r_.h_sem)
    cot_copies = replicas_copies(r_.cland, r_.coth, r_.cx_sem)
    for copy in cot_copies:
        copy.start()

    def gates_of(rows):
        logits = dot(rows, r_.smf[...])
        weight = jnp.where(iota(logits.shape, 1) < E, jnp.exp(logits), 0.0)
        return weight / jnp.sum(weight, axis=-1, keepdims=True)

    gates = gates_of(r_.hid[...])
    lanes = iota((TP, LANES), 1)
    pair_gate = [
        jnp.sum(jnp.where(lanes == ids_v[:, k : k + 1], gates, 0.0), axis=-1, keepdims=True)
        for k in range(2)
    ]

    FT = 256
    load_up.wait()
    load_down.wait()
    up, down = r_.up, r_.down
    unpack(r_.cland[...], r_.yrow)

    def early(j, carry):
        cut = pl.ds(pl.multiple_of(j * FT, FT), FT)
        r_.ga[:, cut] = dot_nt(r_.yrow[...], down[cut, :]).astype(BF16)
        return carry

    lax.fori_loop(0, FF // FT, early, 0)

    rows_wait(r_.hbuf, r_.hland, r_.h_sem)
    hid_copies = replicas_copies(r_.hland, r_.hoth, r_.hx_sem)
    for copy in hid_copies:
        copy.start()
    unpack(r_.hland[...], r_.xrow)
    slot_lane = iota((N, LANES), 1)
    own_gates = gates_of(r_.xrow[...])
    own_gate = jnp.sum(jnp.where(slot_lane == me, own_gates, 0.0), axis=-1, keepdims=True)
    r_.gbrow[...] = (own_gate * r_.yrow[...].astype(F32)).astype(BF16)

    def gelu_kernel(pre):
        cumul = 0.5 * (1.0 + lax.erf(pre * SQRT_HALF))
        return pre * cumul, cumul + pre * jnp.exp(-0.5 * pre * pre) * INV_ROOT_TWO_PI

    r_.gacc[...] = jnp.zeros((N, D), F32)
    r_.ggate[...] = jnp.zeros((N, LANES), F32)
    r_.gatec[...] = jnp.broadcast_to(own_gate, (N, LANES))

    def middle(j, carry):
        cut = pl.ds(pl.multiple_of(j * FT, FT), FT)
        pre = dot(r_.xrow[...], up[:, cut]) + r_.upb[:, cut].astype(F32)
        act_val, slope = gelu_kernel(pre)
        grad_act = r_.ga[:, cut].astype(F32)
        r_.act[:, cut] = act_val.astype(BF16)
        grad_pre = (r_.gatec[:, 0:1] * grad_act * slope).astype(BF16)
        r_.gp[:, cut] = grad_pre
        r_.gacc[...] += dot_nt(grad_pre, up[:, cut])
        both = act_val * grad_act
        r_.ggate[...] += sum(both[:, f : f + LANES] for f in range(0, FT, LANES))
        return carry

    lax.fori_loop(0, FF // FT, middle, 0)
    gate_grad = jnp.sum(r_.ggate[...], axis=-1, keepdims=True) + jnp.sum(
        r_.yrow[...].astype(F32) * r_.downb[...].astype(F32), axis=-1, keepdims=True
    )
    picked = jnp.where(slot_lane == me, 1.0, 0.0)
    contrib = (own_gates * (picked - own_gate) * gate_grad).astype(BF16)
    r_.gacc[...] += dot_nt(contrib, r_.smf[...])
    rows_drain(r_.hbuf, r_.hland, r_.h_sem)
    pack_slots(r_.gacc[...].astype(BF16), r_.rbuf)
    rows_start(r_.rbuf, r_.rland, r_.r_sem)
    r_.rterm[...] = dot_tn(r_.xrow[...], contrib)

    for j in range(D // WT):
        cut = slice(j * WT, (j + 1) * WT)
        r_.gacc[:, cut] = dot(r_.act[...], down[:, cut]) + r_.downb[:, cut].astype(F32)
    rows_drain(r_.cbuf, r_.cland, r_.c_sem)
    pack_slots(r_.gacc[...].astype(BF16), r_.obuf)
    rows_start(r_.obuf, r_.oland, r_.o_sem)

    my_part = pl.ds(pl.multiple_of(mine * part, LANES), part)
    outs = []

    def keep(src, dst):
        copy = pltpu.make_async_copy(src, dst, r_.keep_sem.at[len(outs)])
        copy.start()
        outs.append(copy)

    keep(r_.xrow, r_.x_all.at[0:N])
    keep(r_.gbrow, r_.gb_all.at[0:N])
    keep(r_.act.at[:, my_part], r_.act_all.at[0:N])
    keep(r_.gp.at[:, my_part], r_.gp_all.at[0:N])

    for copy in cot_copies + hid_copies:
        copy.wait_recv()
    for step in range(R - 1):
        unpack(r_.coth[step], r_.yo.at[step])
        unpack(r_.hoth[step], r_.xo.at[step])
        yo, xo = r_.yo.at[step], r_.xo.at[step]
        far_gates = gates_of(xo[...])
        far_gate = jnp.sum(jnp.where(slot_lane == me, far_gates, 0.0), axis=-1, keepdims=True)
        yo[...] = (far_gate * yo[...].astype(F32)).astype(BF16)

        def far(j, carry):
            cut = pl.ds(pl.multiple_of(j * FT, FT), FT)
            whole = pl.ds(pl.multiple_of(mine * part + j * FT, LANES), FT)
            rows_cut = pl.ds(pl.multiple_of(mine * part + j * FT, LANES), FT)
            pre = dot(xo[...], up[:, whole]) + r_.upb[:, whole].astype(F32)
            act_val, slope = gelu_kernel(pre)
            r_.act_o[step, :, cut] = act_val.astype(BF16)
            grad_act = dot_nt(yo[...], down[rows_cut, :])
            r_.gp_o[step, :, cut] = (grad_act * slope).astype(BF16)
            return carry

        lax.fori_loop(0, part // FT, far, 0)
        lo, hi = (step + 1) * N, (step + 2) * N
        keep(r_.xo.at[step], r_.x_all.at[lo:hi])
        keep(r_.yo.at[step], r_.gb_all.at[lo:hi])
        keep(r_.act_o.at[step], r_.act_all.at[lo:hi])
        keep(r_.gp_o.at[step], r_.gp_all.at[lo:hi])

    pending = []

    def launch(copies):
        for copy in copies:
            copy.start()
        pending.extend(copies)
        return copies

    def core_start(tag):
        own, from_core, _, _, _, sems = tag
        return launch(
            [
                copy_to(
                    own.at[other_core], from_core, sems.at[0], sems.at[1],
                    shard=shard_of(at_z, at_y, other_core),
                )
            ]
        )

    def y_start(tag, before):
        own, from_core, from_y, _, _, sems = tag
        for copy in before:
            copy.wait_recv()
        for y in range(Y):
            own[core, y] = (own[core, y].astype(F32) + from_core[y].astype(F32)).astype(BF16)
        return launch(
            [
                copy_to(
                    own.at[core, turn(at_y, dy, Y)], from_y.at[dy - 1], sems.at[2 * dy],
                    sems.at[2 * dy + 1], shard=shard_of(at_z, turn(at_y, dy, Y), core),
                )
                for dy in range(1, Y)
            ]
        )

    def z_start(tag, before):
        own, _, from_y, from_z, _, sems = tag
        for copy in before:
            copy.wait_recv()
        total = own[core, at_y].astype(F32)
        for dy in range(1, Y):
            total = total + from_y[dy - 1].astype(F32)
        own[core, at_y] = total.astype(BF16)
        base = 2 * Y
        return launch(
            [
                copy_to(
                    own.at[core, at_y, turn(at_z, dz, Z)], from_z.at[dz - 1], sems.at[base + 2 * dz - 2],
                    sems.at[base + 2 * dz - 1], shard=shard_of(turn(at_z, dz, Z), at_y, core),
                )
                for dz in range(1, Z)
            ]
        )

    def x_start(tag, before):
        own, _, _, from_z, from_x, sems = tag
        for copy in before:
            copy.wait_recv()
        total = own[core, at_y, at_z].astype(F32)
        for dz in range(1, Z):
            total = total + from_z[dz - 1].astype(F32)
        own[core, at_y, at_z] = total.astype(BF16)
        base = 2 * Y + 2 * Z - 2
        return launch(
            [
                copy_to(
                    own.at[core, at_y, at_z], from_x.at[dx - 1], sems.at[base + 2 * dx - 2],
                    sems.at[base + 2 * dx - 1], replica=turn(mine, dx, R),
                )
                for dx in range(1, R)
            ]
        )

    def finish(tag, before, out):
        own, _, _, _, from_x, _ = tag
        for copy in before:
            copy.wait_recv()
        total = own[core, at_y, at_z].astype(F32)
        for dx in range(1, R):
            total = total + from_x[dx - 1].astype(F32)
        out[...] = total

    def put_part(tag, lane_at, value):
        own = tag[0]
        wide = value.shape[1]
        low_value = value.astype(BF16)
        for z in range(Z):
            for y in range(Y):
                for c in range(2):
                    s = (z * Y + y) * 2 + c
                    own[c, y, z, :, lane_at : lane_at + wide] = low_value[s * K : (s + 1) * K, :]

    vecs = r_.vecs
    vecs[...] = jnp.zeros((LANES, D), F32)

    def put_vector(i, value):
        vecs[E + i : E + i + 1, :] = value

    rows_wait(r_.rbuf, r_.rland, r_.r_sem)
    flat_back = r_.rland[...].reshape(SB, LW)
    for i in range(q):
        r_.gn[:, i * LW : (i + 1) * LW] = dot(r_.place[0, i] + r_.place[1, i], flat_back)

    def norm_grad(grad_rows, normed, inv, gain, at_gain, at_bias):
        scaled = grad_rows * gain
        inner = (
            scaled
            - jnp.mean(scaled, axis=-1, keepdims=True)
            - normed * jnp.mean(scaled * normed, axis=-1, keepdims=True)
        )
        put_vector(at_gain, jnp.sum(grad_rows * normed, axis=0, keepdims=True))
        put_vector(at_bias, jnp.sum(grad_rows, axis=0, keepdims=True))
        return inner * inv

    gres[...] = cotf[...] + norm_grad(r_.gn[...], n2[...], inv_two, vector(5), 5, 6)
    put_vector(4, jnp.sum(gres[...], axis=0, keepdims=True))
    r_.tmpb[...] = gres[...].astype(BF16)
    for j in range(D // WT):
        cut = slice(j * WT, (j + 1) * WT)
        put_part(r_.rs_o, j * WT, dot_tn(r_.ctx[...], r_.tmpb[:, cut]))
    stage_o = core_start(r_.rs_o)
    for j in range(D // WT):
        cut = slice(j * WT, (j + 1) * WT)
        r_.gctx[:, cut] = dot_nt(r_.tmpb[...], r_.wf_out[cut, :]).astype(BF16)

    def attend_back(i, carry):
        cut_q, cut_k, cut_v = pair_cuts(i)
        query, keys, values = r_.qkv[:, cut_q], r_.qkv[:, cut_k], r_.qkv[:, cut_v]
        query_half, key_half, grad_half = halves(query), halves(keys), halves(r_.gctx[:, cut_q])
        grad_q = grad_k = grad_v = None
        for a in range(2):
            probs = r_.probs[2 * i + a]
            grad_probs = dot_nt(grad_half[a], values)
            inner = jnp.sum(probs * grad_probs, axis=-1, keepdims=True)
            grad_scores = (probs * (grad_probs - inner) * scale).astype(BF16)
            terms = (
                dot(grad_scores, key_half[a]),
                dot_tn(grad_scores, query_half[a]),
                dot_tn(probs.astype(BF16), grad_half[a]),
            )
            if a == 0:
                grad_q, grad_k, grad_v = terms
            else:
                grad_q, grad_k, grad_v = grad_q + terms[0], grad_k + terms[1], grad_v + terms[2]
        r_.gm[:, cut_q] = grad_q.astype(BF16)
        r_.gm[:, cut_k] = grad_k.astype(BF16)
        r_.gm[:, cut_v] = grad_v.astype(BF16)
        vecs[E + 2 : E + 3, cut_q] = jnp.sum(grad_q, axis=0, keepdims=True)
        vecs[E + 3 : E + 4, cut_q] = jnp.sum(grad_v, axis=0, keepdims=True)
        return carry

    lax.fori_loop(0, pairs, attend_back, 0)
    stage_o = y_start(r_.rs_o, stage_o)
    stages = {}
    for tag, at in ((r_.rs_v, 2 * D), (r_.rs_k, D), (r_.rs_q, 0)):
        for j in range(D // WT):
            put_part(
                tag, j * WT, dot_tn(r_.act1[...], r_.gm[:, at + j * WT : at + (j + 1) * WT])
            )
        stages[at] = tag, core_start(tag)

    for j in range(D // WT):
        cut = slice(j * WT, (j + 1) * WT)
        r_.gn[:, cut] = dot_nt(r_.gm[...], r_.wf_in[cut, :])
    grad_tok = gres[...] + norm_grad(r_.gn[...], n1[...], inv_one, vector(0), 0, 1)
    r_.o_grad[...] = grad_tok[0:T].astype(BF16)
    put_part(r_.rs_s, 0, vecs[...].T + r_.rterm[...])
    stages[-1] = r_.rs_s, core_start(r_.rs_s)
    stage_o = z_start(r_.rs_o, stage_o)
    for at in (2 * D, D, 0, -1):
        stages[at] = stages[at][0], y_start(*stages[at])

    rows_wait(r_.obuf, r_.oland, r_.o_sem)
    flat_out = r_.oland[...].reshape(SB, LW)
    for i in range(q):
        cut = slice(i * LW, (i + 1) * LW)
        total = resid[:, cut]
        for k in range(2):
            total = total + pair_gate[k] * dot(r_.place[k, i], flat_out)
        r_.o_rows[:, cut] = total[0:T].astype(BF16)

    stage_o = x_start(r_.rs_o, stage_o)
    for at in (2 * D, D, 0, -1):
        stages[at] = stages[at][0], z_start(*stages[at])
    finish(r_.rs_o, stage_o, r_.o_out)
    for at in (2 * D, D, 0, -1):
        stages[at] = stages[at][0], x_start(*stages[at])
    for tag, at in ((r_.rs_v, 2 * D), (r_.rs_k, D), (r_.rs_q, 0)):
        finish(*stages[at], r_.o_proj.at[:, at : at + D])
    finish(*stages[-1], turned.at[0:K])
    r_.o_small[...] = turned[...].T[0 : r_.o_small.shape[0], 0:K]

    for a in range(3):
        for copy in sent[a]:
            copy.wait_send()
    rows_drain(r_.rbuf, r_.rland, r_.r_sem)
    rows_drain(r_.obuf, r_.oland, r_.o_sem)
    for copy in cot_copies + hid_copies + pending:
        copy.wait_send()
    for copy in outs:
        copy.wait()


def call_block(plan, *arrays):
    S, R, TP, FF, E = plan.S, plan.R, plan.TP, plan.FF, plan.E
    K, q, BR, LW, SB, N, Z, Y, part = (
        plan.K, plan.q, plan.BR, plan.LW, plan.SB, plan.N, plan.Z, plan.Y, plan.part,
    )
    vmem = pl.BlockSpec(memory_space=pltpu.VMEM)
    anyw = pl.BlockSpec(memory_space=pl.ANY)
    outs = dict(
        o_rows=((plan.T, D), BF16, vmem),
        o_grad=((plan.T, D), BF16, vmem),
        o_proj=((K, 3 * D), F32, vmem),
        o_out=((K, D), F32, vmem),
        o_small=((-(-(E + VECTORS) // 8) * 8, K), F32, vmem),
        x_all=((R * N, D), BF16, anyw),
        gb_all=((R * N, D), BF16, anyw),
        act_all=((R * N, part), BF16, anyw),
        gp_all=((R * N, part), BF16, anyw),
    )

    def landing(wide):
        return (
            pltpu.VMEM((2, Y, Z, K, wide), BF16),
            pltpu.VMEM((Y, Z, K, wide), BF16),
            pltpu.VMEM((max(Y - 1, 1), Z, K, wide), BF16),
            pltpu.VMEM((max(Z - 1, 1), K, wide), BF16),
            pltpu.VMEM((max(R - 1, 1), K, wide), BF16),
            pltpu.SemaphoreType.DMA((2 * (Y + Z + R),)),
        )

    def pairs_of(*extent):
        return pltpu.SemaphoreType.DMA(extent)

    rows = pltpu.VMEM((S, BR, LW), BF16)
    far_rows = pltpu.VMEM((R - 1, S, BR, LW), BF16)
    wide_rows = pltpu.VMEM((TP, D), F32)
    half_rows = pltpu.VMEM((TP, D), BF16)
    slot_rows = pltpu.VMEM((N, D), BF16)
    scratch = dict(
        up=pltpu.VMEM((D, FF), BF16),
        down=pltpu.VMEM((FF, D), BF16),
        wf_in=pltpu.VMEM((D, 3 * D), BF16),
        wf_out=pltpu.VMEM((D, D), BF16),
        smf=pltpu.VMEM((D, LANES), BF16),
        smt=pltpu.VMEM((LANES, D), F32),
        turned=pltpu.VMEM((LANES, LANES), F32),
        small=pltpu.VMEM((K, LANES), BF16),
        pairs_at=pltpu.VMEM((LANES, -(-TP // LANES) * LANES), F32),
        place=pltpu.VMEM((2, q, TP, SB), BF16),
        unroll=pltpu.VMEM((q, N, SB), BF16),
        tokf=wide_rows, cotf=wide_rows, n1=wide_rows, n2=wide_rows, resid=wide_rows, gres=wide_rows,
        gn=wide_rows,
        tmpb=half_rows, act1=half_rows, hid=half_rows, ctx=half_rows, gctx=half_rows,
        bias=pltpu.VMEM((8, 3 * D), F32),
        qkv=pltpu.VMEM((TP, 3 * D), BF16),
        gm=pltpu.VMEM((TP, 3 * D), BF16),
        probs=pltpu.VMEM((HEADS, TP, TP), F32),
        cbuf=rows, cland=rows, hbuf=rows, hland=rows, rland=rows, oland=rows,
        coth=far_rows, hoth=far_rows,
        yrow=slot_rows, xrow=slot_rows, gbrow=slot_rows,
        yo=pltpu.VMEM((R - 1, N, D), BF16),
        xo=pltpu.VMEM((R - 1, N, D), BF16),
        ga=pltpu.VMEM((N, FF), BF16),
        act=pltpu.VMEM((N, FF), BF16),
        gp=pltpu.VMEM((N, FF), BF16),
        act_o=pltpu.VMEM((R - 1, N, part), BF16),
        gp_o=pltpu.VMEM((R - 1, N, part), BF16),
        gacc=pltpu.VMEM((N, D), F32),
        ggate=pltpu.VMEM((N, LANES), F32),
        gatec=pltpu.VMEM((N, LANES), F32),
        rterm=pltpu.VMEM((D, LANES), F32),
        vecs=pltpu.VMEM((LANES, D), F32),
        rs_o=landing(D), rs_v=landing(D), rs_k=landing(D), rs_q=landing(D), rs_s=landing(LANES),
        load_sem=pairs_of(2),
        ag_send=pairs_of(3, 2 * S),
        ag_recv=pairs_of(3, S),
        c_sem=pairs_of(2, S),
        h_sem=pairs_of(2, S),
        r_sem=pairs_of(2, S),
        o_sem=pairs_of(2, S),
        cx_sem=pairs_of(2, R),
        hx_sem=pairs_of(2, R),
        keep_sem=pairs_of(4 * R),
    )
    return pl.pallas_call(
        functools.partial(block_kernel, plan, list(outs)),
        out_shape=[jax.ShapeDtypeStruct(o[0], o[1]) for o in outs.values()],
        in_specs=[vmem] * (9 + VECTORS) + [anyw] * 2,
        out_specs=[o[2] for o in outs.values()],
        scratch_shapes=scratch,
        compiler_params=pltpu.CompilerParams(
            collective_id=0, has_side_effects=True, vmem_limit_bytes=60 * 1024 * 1024
        ),
        cost_estimate=pl.CostEstimate(
            flops=12 * N * D * FF, bytes_accessed=4 * D * FF, transcendentals=2 * N * FF
        ),
    )(*arrays)


def body(
    tokens, cotangent, norm1_gain, norm1_bias, proj_in, query_bias, value_bias, proj_out, out_bias,
    norm2_gain, norm2_bias, router, up_weight, up_bias, down_weight, down_bias, expert_ids, slot_ids,
):
    shards, replicas = lax.axis_size("shard"), lax.axis_size("replica")
    rows = tokens.shape[0] * tokens.shape[1]
    plan = Plan(shards, replicas, rows, up_weight.shape[2], up_weight.shape[0])
    (o_rows, o_grad, o_proj, o_out, o_small, x_all, gb_all, act_all, gp_all) = call_block(
        plan, tokens.reshape(rows, D), cotangent.reshape(rows, D), proj_in, proj_out, router.T,
        expert_ids.T, slot_ids.T, up_bias, down_bias, norm1_gain, norm1_bias, query_bias, value_bias,
        out_bias, norm2_gain, norm2_bias, up_weight[0], down_weight[0],
    )
    ours = lax.axis_index("replica")
    width = D // replicas
    up_grad = dot_tn(x_all, gp_all)[None]
    down_grad = dot_tn(act_all, gb_all)[None]
    up_bias_grad = jnp.sum(gp_all, axis=0, dtype=F32)[None]
    down_bias_grad = lax.dynamic_slice_in_dim(
        jnp.sum(gb_all, axis=0, dtype=F32), ours * width, width, axis=0
    )[None]
    e = plan.E
    vec = [o_small[e + i] for i in range(VECTORS)]
    return (
        o_rows.reshape(tokens.shape),
        o_grad.reshape(tokens.shape),
        vec[0], vec[1], o_proj, vec[2], vec[3], o_out, vec[4], vec[5], vec[6], o_small[:e].T,
        up_grad, up_bias_grad, down_grad, down_bias_grad,
    )


def fits_kernel(mesh):
    shards, replicas = mesh.shape["shard"], mesh.shape["replica"]
    return shards % 2 == 0 and (D // shards) % 16 == 0 and replicas == 2


def solution(mesh):
    in_specs = (
        P(("replica", "shard"), None, None),
        P(("replica", "shard"), None, None),
        P("shard"),
        P("shard"),
        P("shard", None),
        P("shard"),
        P("shard"),
        P("shard", None),
        P("shard"),
        P("shard"),
        P("shard"),
        P("shard", None),
        P("shard", None, None),
        P("shard", None),
        P("shard", None, None),
        P("shard", None),
        P(("replica", "shard"), None),
        P(("replica", "shard"), None),
    )
    out_specs = (
        P(("replica", "shard"), None, None),
        P(("replica", "shard"), None, None),
        P("shard"),
        P("shard"),
        P("shard", None),
        P("shard"),
        P("shard"),
        P("shard", None),
        P("shard"),
        P("shard"),
        P("shard"),
        P("shard", None),
        P("shard", None, "replica"),
        P("shard", "replica"),
        P("shard", "replica", None),
        P("shard", "replica"),
    )
    chosen = body if fits_kernel(mesh) else plain_body
    return jax.shard_map(chosen, mesh=mesh, in_specs=in_specs, out_specs=out_specs, check_vma=False)
```

```python
import functools
from types import SimpleNamespace

import jax
import jax.numpy as jnp
from jax import lax
from jax.experimental import pallas as pl
from jax.experimental.pallas import tpu as pltpu
from jax.sharding import PartitionSpec as P

D = 768
HEADS = 12
HDIM = 64
SEQ = 197


EPS = 1e-06
SQRT_HALF = 0.7071067811865476
INV_ROOT_TWO_PI = 0.3989422804014327


def layer_norm(rows_in, norm_gain, norm_shift):
    average = jnp.mean(rows_in, axis=-1, keepdims=True)
    centred = rows_in - average
    inv_std = lax.rsqrt(jnp.mean(centred * centred, axis=-1, keepdims=True) + EPS)
    normed = centred * inv_std
    return (normed, inv_std, normed * norm_gain + norm_shift)


def norm_back(grad_rows, normed, inv_std, norm_gain):
    scaled = grad_rows * norm_gain
    inner = (
        scaled
        - jnp.mean(scaled, axis=-1, keepdims=True)
        - normed * jnp.mean(scaled * normed, axis=-1, keepdims=True)
    )
    return (inner * inv_std, jnp.sum(grad_rows * normed, axis=0), jnp.sum(grad_rows, axis=0))


def gelu_parts(pre_act):
    cumul = 0.5 * (1.0 + lax.erf(pre_act * SQRT_HALF))
    return (pre_act * cumul, cumul + pre_act * jnp.exp(-0.5 * pre_act * pre_act) * INV_ROOT_TWO_PI)


def route_table(expert_ids, slot_ids, experts, capacity):
    positions = jnp.arange(experts * capacity, dtype=jnp.int32)
    tables = []
    for choose in range(2):
        kept = slot_ids[:, choose] < capacity
        target = jnp.where(kept, expert_ids[:, choose] * capacity + slot_ids[:, choose], -1)
        tables.append((target[:, None] == positions[None, :]).astype(jnp.bfloat16))
    return tables


def pick_table(expert_ids, experts):
    labels = jnp.arange(experts, dtype=jnp.int32)
    return [
        (expert_ids[:, choose][:, None] == labels[None, :]).astype(jnp.float32)
        for choose in range(2)
    ]


def lane_pad(blocks):
    rows = blocks[0].shape[0]
    spare = -sum(block.shape[1] for block in blocks) % 128
    return jnp.concatenate(blocks + [jnp.zeros((rows, spare), blocks[0].dtype)], axis=1)


def other_replicas(value):
    size = lax.axis_size("replica")
    return [
        lax.ppermute(value, "replica", [(at, (at + step) % size) for at in range(size)])
        for step in range(1, size)
    ]


def to_expert(value, local_experts, capacity):
    shards, width = value.shape[0], value.shape[-1]
    return (
        value.reshape(shards, local_experts, capacity, width)
        .swapaxes(0, 1)
        .reshape(local_experts, shards * capacity, width)
    )


def from_expert(value, shards, capacity):
    local_experts, width = value.shape[0], value.shape[-1]
    return (
        value.reshape(local_experts, shards, capacity, width)
        .swapaxes(0, 1)
        .reshape(shards, local_experts * capacity, width)
    )


def expert_middle(rows, grad_rows, up_weight, up_bias, down_weight):
    expert_pre = (
        jnp.einsum("ecd,edf->ecf", rows, up_weight, preferred_element_type=jnp.float32)
        + up_bias.astype(jnp.float32)[:, None, :]
    )
    act_val, slope = gelu_parts(expert_pre)
    grad_active = jnp.einsum(
        "ecd,efd->ecf", grad_rows, down_weight, preferred_element_type=jnp.float32
    )
    return (act_val.astype(jnp.bfloat16), (grad_active * slope).astype(jnp.bfloat16))


def plain_body(
    tokens,
    cotangent,
    norm1_gain,
    norm1_bias,
    proj_in,
    query_bias,
    value_bias,
    proj_out,
    out_bias,
    norm2_gain,
    norm2_bias,
    router,
    up_weight,
    up_bias,
    down_weight,
    down_bias,
    expert_ids,
    slot_ids,
):
    images = tokens.shape[0]
    small = jnp.stack(
        [norm1_gain, norm1_bias, query_bias, value_bias, out_bias, norm2_gain, norm2_bias],
        axis=1,
    )
    width_in, width_small = proj_in.shape[1], small.shape[1] + router.shape[1]
    first = lax.all_gather(
        lane_pad([proj_in, proj_out, small, router]), "shard", axis=0, tiled=True
    )
    width_both = width_in + proj_out.shape[1]
    proj_full = first[:, :width_in]
    outproj_full = first[:, width_in:width_both]
    small_full = first[:, width_both : width_both + small.shape[1]]
    router_full = first[:, width_both + small.shape[1] : width_both + width_small]
    (
        gain_one,
        shift_one,
        query_shift,
        value_shift,
        out_shift,
        gain_two,
        shift_two,
    ) = [row for row in small_full.T]
    tok_rows = tokens.reshape(-1, D).astype(jnp.float32)
    normed_one, inv_one, pre_one = layer_norm(
        tok_rows, gain_one.astype(jnp.float32), shift_one.astype(jnp.float32)
    )
    act_one = pre_one.astype(jnp.bfloat16)
    mixed = jnp.dot(act_one, proj_full, preferred_element_type=jnp.float32)
    query_part = (mixed[:, :D] + query_shift.astype(jnp.float32)).astype(jnp.bfloat16)
    key_part = mixed[:, D : 2 * D].astype(jnp.bfloat16)
    value_part = (mixed[:, 2 * D :] + value_shift.astype(jnp.float32)).astype(jnp.bfloat16)
    query_heads = query_part.reshape(images, SEQ, HEADS, HDIM)
    key_heads = key_part.reshape(images, SEQ, HEADS, HDIM)
    value_heads = value_part.reshape(images, SEQ, HEADS, HDIM)
    scores = jnp.einsum(
        "ishd,ithd->ihst", query_heads, key_heads, preferred_element_type=jnp.float32
    ) * HDIM ** (-0.5)
    log_total = jnp.log(jnp.sum(jnp.exp(scores), axis=-1))
    attn_probs = jnp.exp(scores - log_total[..., None]).astype(jnp.bfloat16)
    context = (
        jnp.einsum("ihst,ithd->ishd", attn_probs, value_heads, preferred_element_type=jnp.float32)
        .reshape(-1, D)
        .astype(jnp.bfloat16)
    )
    resid = (
        tok_rows
        + jnp.dot(context, outproj_full, preferred_element_type=jnp.float32)
        + out_shift.astype(jnp.float32)
    )
    normed_two, inv_two, pre_two = layer_norm(
        resid, gain_two.astype(jnp.float32), shift_two.astype(jnp.float32)
    )
    hidden = pre_two.astype(jnp.bfloat16)
    logits = jnp.dot(hidden, router_full, preferred_element_type=jnp.float32)
    exp_logits = jnp.exp(logits)
    gate_probs = exp_logits / jnp.sum(exp_logits, axis=-1, keepdims=True)
    local_experts = up_weight.shape[0]
    experts = local_experts * lax.axis_size("shard")
    capacity = 2 * tok_rows.shape[0] // experts
    routes = route_table(expert_ids, slot_ids, experts, capacity)
    picks = pick_table(expert_ids, experts)
    both = jnp.concatenate(routes, axis=0)
    either = routes[0] + routes[1]
    gate_pair = [jnp.sum(gate_probs * pick, axis=-1) for pick in picks]
    grad_out = cotangent.reshape(-1, D).astype(jnp.float32)
    sent = jnp.concatenate(
        [(gate[:, None] * grad_out).astype(jnp.bfloat16) for gate in gate_pair], axis=0
    )
    buffer = jnp.dot(either.T, hidden, preferred_element_type=jnp.float32)
    grad_buffer = jnp.dot(both.T, sent, preferred_element_type=jnp.float32)
    shards = lax.axis_size("shard")
    outgoing = (
        jnp.concatenate([buffer, grad_buffer], axis=1)
        .astype(jnp.bfloat16)
        .reshape(shards, local_experts * capacity, 2 * D)
    )
    landed = to_expert(
        lax.all_to_all(outgoing, "shard", split_axis=0, concat_axis=0, tiled=True),
        local_experts,
        capacity,
    )
    arrived, grad_arrived = landed[..., :D], landed[..., D:]
    others = other_replicas(landed)
    active, grad_pre = expert_middle(arrived, grad_arrived, up_weight, up_bias, down_weight)
    expert_out = (
        jnp.einsum("ecf,efd->ecd", active, down_weight, preferred_element_type=jnp.float32)
        + down_bias.astype(jnp.float32)[:, None, :]
    ).astype(jnp.bfloat16)
    grad_in = jnp.einsum(
        "ecf,edf->ecd", grad_pre, up_weight, preferred_element_type=jnp.float32
    ).astype(jnp.bfloat16)
    answer = from_expert(jnp.concatenate([expert_out, grad_in], axis=2), shards, capacity)
    back = lax.all_to_all(answer, "shard", split_axis=0, concat_axis=0, tiled=True).reshape(
        experts * capacity, 2 * D
    )
    returned, grad_back = back[:, :D], back[:, D:]

    replicas = lax.axis_size("replica")
    ours = lax.axis_index("replica")
    part = up_weight.shape[2] // replicas
    up_part = lax.dynamic_slice_in_dim(up_weight, ours * part, part, axis=2)
    up_bias_part = lax.dynamic_slice_in_dim(up_bias, ours * part, part, axis=1)
    down_part = lax.dynamic_slice_in_dim(down_weight, ours * part, part, axis=1)
    active_parts = [lax.dynamic_slice_in_dim(active, ours * part, part, axis=2)]
    grad_pre_parts = [lax.dynamic_slice_in_dim(grad_pre, ours * part, part, axis=2)]
    for other in others:
        other_active, other_pre = expert_middle(
            other[..., :D], other[..., D:], up_part, up_bias_part, down_part
        )
        active_parts.append(other_active)
        grad_pre_parts.append(other_pre)
    all_rows = jnp.concatenate([landed] + others, axis=1)
    all_active = jnp.concatenate(active_parts, axis=1)
    all_pre = jnp.concatenate(grad_pre_parts, axis=1)
    width_part = D // replicas
    expert_grads = (
        jnp.einsum("ecd,ecf->edf", all_rows[..., :D], all_pre, preferred_element_type=jnp.float32),
        jnp.sum(all_pre, axis=1, dtype=jnp.float32),
        jnp.einsum(
            "ecf,ecd->efd", all_active, all_rows[..., D:], preferred_element_type=jnp.float32
        ),
        lax.dynamic_slice_in_dim(
            jnp.sum(all_rows[..., D:], axis=1, dtype=jnp.float32),
            ours * width_part,
            width_part,
            axis=1,
        ),
    )

    rows_here = tok_rows.shape[0]
    gathered_both = jnp.dot(both, returned, preferred_element_type=jnp.float32)
    gathered_pair = [gathered_both[:rows_here], gathered_both[rows_here:]]
    moe_sum = gate_pair[0][:, None] * gathered_pair[0] + gate_pair[1][:, None] * gathered_pair[1]
    block_out = (resid + moe_sum).astype(jnp.bfloat16).reshape(tokens.shape)
    grad_gate = [jnp.sum(grad_out * part_k, axis=-1) for part_k in gathered_pair]
    back_gain_one, back_proj, back_outproj, back_gain_two, back_router = (
        gain_one,
        proj_full,
        outproj_full,
        gain_two,
        router_full,
    )
    grad_moe = jnp.dot(either, grad_back, preferred_element_type=jnp.float32)
    grad_gates = picks[0] * grad_gate[0][:, None] + picks[1] * grad_gate[1][:, None]
    grad_logits = (
        gate_probs * (grad_gates - jnp.sum(gate_probs * grad_gates, axis=-1, keepdims=True))
    ).astype(jnp.bfloat16)
    router_term = jnp.dot(hidden.T, grad_logits, preferred_element_type=jnp.float32)
    grad_norm_two = grad_moe + jnp.dot(
        grad_logits, back_router.T, preferred_element_type=jnp.float32
    )
    grad_resid_two, gain_two_term, shift_two_term = norm_back(
        grad_norm_two, normed_two, inv_two, back_gain_two.astype(jnp.float32)
    )
    grad_resid = grad_out + grad_resid_two
    resid_bf = grad_resid.astype(jnp.bfloat16)
    out_shift_term = jnp.sum(grad_resid, axis=0)
    outproj_term = jnp.dot(context.T, resid_bf, preferred_element_type=jnp.float32)
    grad_context = (
        jnp.dot(resid_bf, back_outproj.T, preferred_element_type=jnp.float32)
        .astype(jnp.bfloat16)
        .reshape(images, SEQ, HEADS, HDIM)
    )
    scores_again = jnp.einsum(
        "ishd,ithd->ihst", query_heads, key_heads, preferred_element_type=jnp.float32
    ) * HDIM ** (-0.5)
    probs_full = jnp.exp(scores_again - log_total[..., None])
    grad_probs = jnp.einsum(
        "ishd,ithd->ihst", grad_context, value_heads, preferred_element_type=jnp.float32
    )
    grad_scores = (
        probs_full
        * (grad_probs - jnp.sum(probs_full * grad_probs, axis=-1, keepdims=True))
        * HDIM ** (-0.5)
    ).astype(jnp.bfloat16)
    probs_bf = probs_full.astype(jnp.bfloat16)
    grad_value = jnp.einsum(
        "ihst,ishd->ithd", probs_bf, grad_context, preferred_element_type=jnp.float32
    ).reshape(-1, D)
    grad_query = jnp.einsum(
        "ihst,ithd->ishd", grad_scores, key_heads, preferred_element_type=jnp.float32
    ).reshape(-1, D)
    grad_key = jnp.einsum(
        "ihst,ishd->ithd", grad_scores, query_heads, preferred_element_type=jnp.float32
    ).reshape(-1, D)
    grad_mixed = jnp.concatenate([grad_query, grad_key, grad_value], axis=1).astype(jnp.bfloat16)
    proj_term = jnp.dot(act_one.T, grad_mixed, preferred_element_type=jnp.float32)
    grad_act = jnp.dot(grad_mixed, back_proj.T, preferred_element_type=jnp.float32)
    grad_tok_norm, gain_one_term, shift_one_term = norm_back(
        grad_act, normed_one, inv_one, back_gain_one.astype(jnp.float32)
    )
    tokens_grad = (grad_resid + grad_tok_norm).astype(jnp.bfloat16).reshape(tokens.shape)
    query_shift_term = jnp.sum(grad_query, axis=0)
    value_shift_term = jnp.sum(grad_value, axis=0)
    column_sums = [
        gain_one_term,
        shift_one_term,
        query_shift_term,
        value_shift_term,
        out_shift_term,
        gain_two_term,
        shift_two_term,
    ]
    summed = lax.psum_scatter(
        lane_pad(
            [
                proj_term.astype(jnp.bfloat16),
                outproj_term.astype(jnp.bfloat16),
                lax.optimization_barrier(
                    lane_pad(
                        [
                            jnp.stack(column_sums, axis=0).astype(jnp.bfloat16).T,
                            router_term.astype(jnp.bfloat16),
                        ]
                    )
                ),
            ]
        ),
        "shard",
        scatter_dimension=0,
        tiled=True,
    )
    total = summed.astype(jnp.float32)
    for other in other_replicas(summed):
        total = total + other.astype(jnp.float32)
    small_total = total[:, width_both:]
    columns = len(column_sums)
    dense_grads = (
        small_total[:, 0],
        small_total[:, 1],
        total[:, :width_in],
        small_total[:, 2],
        small_total[:, 3],
        total[:, width_in:width_both],
        small_total[:, 4],
        small_total[:, 5],
        small_total[:, 6],
        small_total[:, columns : columns + experts],
    )
    return (
        block_out,
        tokens_grad,
        dense_grads[0],
        dense_grads[1],
        dense_grads[2],
        dense_grads[3],
        dense_grads[4],
        dense_grads[5],
        dense_grads[6],
        dense_grads[7],
        dense_grads[8],
        dense_grads[9],
        expert_grads[0],
        expert_grads[1],
        expert_grads[2],
        expert_grads[3],
    )


F32 = jnp.float32
BF16 = jnp.bfloat16
LANES = 128
VECTORS = 7


def dot(left, right):
    return jnp.dot(left, right, preferred_element_type=F32)


def dot_nt(left, right):
    return lax.dot_general(left, right, (((1,), (1,)), ((), ())), preferred_element_type=F32)


def dot_tn(left, right):
    return lax.dot_general(left, right, (((0,), (0,)), ((), ())), preferred_element_type=F32)


def iota(shape, axis):
    return lax.broadcasted_iota(jnp.int32, shape, axis)


class Plan:
    def __init__(self, shards, replicas, rows, hidden_units, local_experts):
        self.S, self.R, self.T, self.FF = shards, replicas, rows, hidden_units
        self.E = local_experts * shards
        self.C = 2 * rows // self.E
        self.TP = -(-rows // 16) * 16
        self.K = D // shards
        self.q = 2 if self.C % 16 and (2 * self.C) % 16 == 0 else 1
        self.CR = self.C if self.q == 2 else -(-self.C // 16) * 16
        self.BR = self.CR * self.q
        self.LW = D // self.q
        self.SB = shards * self.BR
        self.N = shards * self.CR
        self.part = hidden_units // replicas
        self.core = 2
        chips = shards // 2
        self.Z = 4 if chips % 4 == 0 else chips
        self.Y = chips // self.Z


def block_kernel(
    plan, out_names, tok, cot, w_in, w_out, router, ids, slots, upb, downb, *refs, **scratch
):
    vectors, (up_h, down_h), refs = refs[:VECTORS], refs[VECTORS : VECTORS + 2], refs[VECTORS + 2 :]
    r_ = SimpleNamespace(
        tok=tok, cot=cot, w_in=w_in, w_out=w_out, ids=ids, slots=slots, upb=upb,
        downb=downb, up_h=up_h, down_h=down_h, **dict(zip(out_names, refs)), **scratch,
    )
    r_.rbuf, r_.obuf, r_.gctx, r_.yo, r_.gacc = r_.hbuf, r_.cbuf, r_.hid, r_.yrow, r_.stage.at[0]
    S, R, T, TP, FF, E, C = plan.S, plan.R, plan.T, plan.TP, plan.FF, plan.E, plan.C
    K, q, CR, BR, LW, SB, N, Z, Y = (
        plan.K, plan.q, plan.CR, plan.BR, plan.LW, plan.SB, plan.N, plan.Z, plan.Y,
    )
    part = plan.part
    me = lax.axis_index("shard")
    mine = lax.axis_index("replica")
    core = lax.rem(me, 2)
    at_y = lax.rem(lax.div(me, 2), Y)
    at_z = lax.div(me, 2 * Y)
    other_core = 1 - core

    def shard_of(z, y, c):
        return (z * Y + y) * 2 + c

    def turn(base, step, size):
        return lax.rem(base + step, size)

    def copy_to(src, dst, send, recv, **device):
        return pltpu.make_async_remote_copy(
            src_ref=src, dst_ref=dst, send_sem=send, recv_sem=recv,
            device_id=device, device_id_type=pl.DeviceIdType.MESH,
        )

    load_up = pltpu.make_async_copy(r_.up_h, r_.up, r_.load_sem.at[0])
    load_down = pltpu.make_async_copy(r_.down_h, r_.down, r_.load_sem.at[1])
    load_up.start()
    load_down.start()

    turned = r_.turned
    turned[...] = jnp.zeros((LANES, LANES), F32)
    turned[0:E, 0:K] = router[...].astype(F32)
    for i, vector_ref in enumerate(vectors):
        turned[E + i : E + i + 1, 0:K] = vector_ref[...].astype(F32).reshape(1, K)
    r_.small[...] = turned[...].T[0:K, :].astype(BF16)

    barrier = pltpu.get_barrier_semaphore()
    for step in range(1, S):
        pl.semaphore_signal(
            barrier, inc=1, device_id={"shard": turn(me, step, S)}, device_id_type=pl.DeviceIdType.MESH
        )
    for step in range(1, R):
        pl.semaphore_signal(
            barrier, inc=1, device_id={"replica": turn(mine, step, R)}, device_id_type=pl.DeviceIdType.MESH
        )
    pl.semaphore_wait(barrier, S - 1 + R - 1)

    both_lanes, own_lanes = pl.ds(2 * D, D), pl.ds(pl.multiple_of(mine * D, LANES), D)
    far_lanes = pl.ds(pl.multiple_of((1 - mine) * D, LANES), D)
    every = slice(None)
    SMALL, BOTH, OWN, FAR, OUT = range(5)
    gathers = [
        (r_.small, r_.smf, every),
        (r_.w_in, r_.wf_in, both_lanes),
        (r_.w_in, r_.wf_in, own_lanes),
        (r_.w_in, r_.wf_in, far_lanes),
        (r_.w_out, r_.wf_out, every),
    ]
    UP, DOWN, CORE, REPLICA, ACROSS = range(5)
    state = SimpleNamespace(drain=False)

    def rows_of(s):
        return pl.ds(pl.multiple_of(s * K, 16), K)

    def block_of(a, s):
        return gathers[a][1].at[rows_of(s), gathers[a][2]]

    def send_block(a, s, src, way, lands=None, **device):
        copy = copy_to(
            src, block_of(a, s), r_.ag_send.at[a, way, s],
            r_.ag_recv.at[a if lands is None else lands, s], **device,
        )
        if state.drain:
            copy.wait_send()
        else:
            copy.start()

    def wait_block(a, s):
        if not state.drain:
            copy_to(
                block_of(a, s), block_of(a, s), r_.ag_send.at[a, CORE, s], r_.ag_recv.at[a, s],
                shard=s,
            ).wait_recv()

    def to_core(a, s, src):
        send_block(a, s, src, CORE, shard=shard_of(at_z, at_y, other_core))

    def to_replica(a, s, src):
        if a == OWN:
            send_block(OWN, s, src, REPLICA, lands=FAR, replica=1 - mine)

    def along(a, s, src, up):
        @pl.when(at_z < Z - 1 if up else at_z > 0)
        def _():
            send_block(
                a, s, src, UP if up else DOWN,
                shard=shard_of(at_z + 1 if up else at_z - 1, at_y, core),
            )

    def across(a, s, src):
        for dy in range(1, Y):
            send_block(a, s, src, ACROSS + dy - 1, shard=shard_of(at_z, turn(at_y, dy, Y), core))

    def gather_start(a):
        src = gathers[a][0].at[:, gathers[a][2]]
        along(a, me, src, True)
        along(a, me, src, False)
        across(a, me, src)
        to_core(a, me, src)

    def at_distance(distance, go):
        if distance == 0:
            go(at_z, None)
            return

        @pl.when(at_z >= distance)
        def _():
            go(at_z - distance, True)

        @pl.when(at_z + distance < Z)
        def _():
            go(at_z + distance, False)

    def gather_z(distance, *which):
        def go(z, up):
            s = shard_of(z, at_y, core)
            for a in which:
                wait_block(a, s)
                src = block_of(a, s)
                along(a, s, src, up)
                across(a, s, src)
                to_replica(a, s, src)
                to_core(a, s, src)

        at_distance(distance, go)

    def gather_y(distance, *which):
        def go(z, up):
            for dy in range(1, Y):
                s = shard_of(z, turn(at_y, dy, Y), core)
                for a in which:
                    wait_block(a, s)
                    to_replica(a, s, block_of(a, s))
                    to_core(a, s, block_of(a, s))

        at_distance(distance, go)

    def gather_lines(*which):
        for distance in range(1, Z):
            gather_z(distance, *which)
            gather_y(distance - 1, *which)
        gather_y(Z - 1, *which)

    def gather_x():
        for distance in range(Z):

            def go(z, up):
                for dy in range(Y):
                    if distance or dy:
                        s = shard_of(z, turn(at_y, dy, Y), core)
                        wait_block(FAR, s)
                        to_core(FAR, s, block_of(FAR, s))

            at_distance(distance, go)

    def gather_end(*which):
        for dz in range(Z):
            for dy in range(Y):
                for a in which:
                    wait_block(a, shard_of(turn(at_z, dz, Z), turn(at_y, dy, Y), other_core))

    gather_start(SMALL)
    gather_start(BOTH)
    gather_start(OWN)
    to_core(FAR, me, r_.w_in.at[:, far_lanes])
    for src, dst in ((r_.small, r_.smf), (r_.w_in, r_.wf_in), (r_.w_out, r_.wf_out)):
        dst[rows_of(me), :] = src[...]

    def rows_start(buf, land, sems):
        land[me] = buf[me]

        def go(step, carry):
            peer = turn(me, step, S)
            copy_to(
                buf.at[peer], land.at[me], sems.at[0, step], sems.at[1, me], shard=peer
            ).start()
            return carry

        lax.fori_loop(1, S, go, 0)

    def rows_wait(buf, land, sems):
        def go(step, carry):
            src = turn(me, step, S)
            copy_to(
                buf.at[src], land.at[src], sems.at[0, step], sems.at[1, src], shard=src
            ).wait_recv()
            return carry

        lax.fori_loop(1, S, go, 0)

    def rows_drain(buf, land, sems):
        def go(step, carry):
            peer = turn(me, step, S)
            copy_to(
                buf.at[peer], land.at[me], sems.at[0, step], sems.at[1, me], shard=peer
            ).wait_send()
            return carry

        lax.fori_loop(1, S, go, 0)

    def replicas_copies(land, others, sems):
        return [
            copy_to(
                land, others.at[step - 1], sems.at[0, step], sems.at[1, step],
                replica=turn(mine, step, R),
            )
            for step in range(1, R)
        ]

    pairs_at = r_.pairs_at
    pairs_at[...] = jnp.full(pairs_at.shape, C, F32)
    pairs_at[0:2, 0:T] = r_.ids[...].astype(F32)
    pairs_at[2:4, 0:T] = r_.slots[...].astype(F32)
    pair_columns = pairs_at[...].T[0:TP, :].astype(jnp.int32)
    ids_v, slots_v = pair_columns[:, 0:2], pair_columns[:, 2:4]
    columns = iota((TP, SB), 1)
    for k in range(2):
        base = jnp.where(
            slots_v[:, k : k + 1] < C, ids_v[:, k : k + 1] * BR + slots_v[:, k : k + 1], -4 * SB
        )
        for i in range(q):
            r_.place[k, i] = jnp.where(columns == base + i * CR, 1.0, 0.0).astype(BF16)

    slot_row = iota((N, SB), 0)
    slot_peer = lax.shift_right_logical(slot_row * (65536 // CR + 1), 16)
    slot_col = slot_peer * BR + (slot_row - slot_peer * CR)
    for i in range(q):
        r_.unroll[i] = jnp.where(iota((N, SB), 1) == slot_col + i * CR, 1.0, 0.0).astype(BF16)

    def pack_tokens(src, dst):
        acc = None
        for i in range(q):
            table = r_.place[0, i] + r_.place[1, i]
            term = dot_tn(table, src[:, i * LW : (i + 1) * LW])
            acc = term if acc is None else acc + term
        dst[...] = acc.astype(BF16).reshape(S, BR, LW)

    def unpack(land, dst):
        flat = land.reshape(SB, LW)
        for i in range(q):
            dst[:, i * LW : (i + 1) * LW] = dot(r_.unroll[i], flat).astype(BF16)

    def pack_slots(value, dst):
        acc = None
        for i in range(q):
            term = dot_tn(r_.unroll[i], value[:, i * LW : (i + 1) * LW])
            acc = term if acc is None else acc + term
        dst[...] = acc.astype(BF16).reshape(S, BR, LW)

    cotf, n1, n2, resid, gres = r_.cotf, r_.n1, r_.n2, r_.resid, r_.gres
    resid[T - T % 8 :, :] = jnp.zeros((TP - (T - T % 8), D), F32)
    cotf[T - T % 8 :, :] = jnp.zeros((TP - (T - T % 8), D), F32)
    resid[0:T, :] = r_.tok[...].astype(F32)
    cotf[0:T, :] = r_.cot[...].astype(F32)
    r_.tmpb[...] = cotf[...].astype(BF16)
    pack_tokens(r_.tmpb, r_.cbuf)

    def normalise(rows):
        average = jnp.mean(rows, axis=-1, keepdims=True)
        centred = rows - average
        inv = lax.rsqrt(jnp.mean(centred * centred, axis=-1, keepdims=True) + EPS)
        return centred * inv, inv

    normed_one, inv_one = normalise(resid[...])
    n1[...] = normed_one

    gather_lines(SMALL)
    gather_end(SMALL)
    r_.smt[...] = r_.smf[...].astype(F32).T
    smt = r_.smt

    def vector(i):
        return smt[E + i : E + i + 1, :]

    r_.act1[...] = (n1[...] * vector(0) + vector(1)).astype(BF16)
    bias = r_.bias
    bias[:, 0:D] = jnp.broadcast_to(vector(2), (8, D))
    bias[:, D : 2 * D] = jnp.zeros((8, D), F32)
    bias[:, 2 * D : 3 * D] = jnp.broadcast_to(vector(3), (8, D))
    gather_lines(BOTH, OWN)
    gather_start(OUT)
    gather_x()
    gather_end(BOTH, OWN, FAR)
    rows_start(r_.cbuf, r_.cland, r_.c_sem)

    WT = 256

    def qkv_step(j, carry):
        cut = pl.ds(pl.multiple_of(j * WT, WT), WT)
        value = dot(r_.act1[...], r_.wf_in[:, cut]) + bias[0:1, cut]
        r_.qkv[:, cut] = value.astype(BF16)
        return carry

    lax.fori_loop(0, 3 * D // WT, qkv_step, 0)
    gather_z(1, OUT)

    low = iota((TP, LANES), 1) < HDIM
    key_ok = iota((TP, TP), 1) < T
    scale = HDIM ** (-0.5)

    def halves(value):
        zero = jnp.zeros_like(value)
        return jnp.where(low, value, zero), jnp.where(low, zero, value)

    def pair_cuts(i):
        return [pl.ds(pl.multiple_of(i * LANES + off, LANES), LANES) for off in (0, D, 2 * D)]

    def attend(i, carry):
        cut_q, cut_k, cut_v = pair_cuts(i)
        keys, values = r_.qkv[:, cut_k], r_.qkv[:, cut_v]
        found = []
        for a, query in enumerate(halves(r_.qkv[:, cut_q])):
            scores = dot_nt(query, keys) * scale
            weight = jnp.where(key_ok, jnp.exp(scores), 0.0)
            probs = weight * (1.0 / jnp.sum(weight, axis=-1, keepdims=True))
            r_.probs[2 * i + a] = probs
            found.append(dot(probs.astype(BF16), values))
        r_.ctx[:, cut_q] = jnp.where(low, found[0], found[1]).astype(BF16)
        return carry

    pairs = HEADS // 2
    lax.fori_loop(0, pairs // 2, attend, 0)
    for distance in range(2, Z):
        gather_z(distance, OUT)
        gather_y(distance - 2, OUT)
    lax.fori_loop(pairs // 2, pairs, attend, 0)
    for distance in range(max(Z - 2, 0), Z):
        gather_y(distance, OUT)
    gather_end(OUT)
    for j in range(D // WT):
        cut = slice(j * WT, (j + 1) * WT)
        resid[:, cut] += dot(r_.ctx[...], r_.wf_out[:, cut]) + vector(4)[:, cut]
    normed_two, inv_two = normalise(resid[...])
    n2[...] = normed_two
    r_.hid[...] = (normed_two * vector(5) + vector(6)).astype(BF16)
    pack_tokens(r_.hid, r_.hbuf)
    rows_wait(r_.cbuf, r_.cland, r_.c_sem)
    rows_start(r_.hbuf, r_.hland, r_.h_sem)
    cot_copies = replicas_copies(r_.cland, r_.coth, r_.cx_sem)
    for copy in cot_copies:
        copy.start()

    def gates_of(rows):
        logits = dot(rows, r_.smf[...])
        weight = jnp.where(iota(logits.shape, 1) < E, jnp.exp(logits), 0.0)
        return weight / jnp.sum(weight, axis=-1, keepdims=True)

    gates = gates_of(r_.hid[...])
    lanes = iota((TP, LANES), 1)
    pair_gate = [
        jnp.sum(jnp.where(lanes == ids_v[:, k : k + 1], gates, 0.0), axis=-1, keepdims=True)
        for k in range(2)
    ]

    FT = 256
    load_up.wait()
    load_down.wait()
    up, down = r_.up, r_.down
    unpack(r_.cland[...], r_.yrow)

    def early(j, carry):
        cut = pl.ds(pl.multiple_of(j * FT, FT), FT)
        r_.ga[:, cut] = dot_nt(r_.yrow[...], down[cut, :]).astype(BF16)
        return carry

    lax.fori_loop(0, FF // FT, early, 0)

    rows_wait(r_.hbuf, r_.hland, r_.h_sem)
    hid_copies = replicas_copies(r_.hland, r_.hoth, r_.hx_sem)
    for copy in hid_copies:
        copy.start()
    unpack(r_.hland[...], r_.xrow)
    slot_lane = iota((N, LANES), 1)
    own_gates = gates_of(r_.xrow[...])
    own_gate = jnp.sum(jnp.where(slot_lane == me, own_gates, 0.0), axis=-1, keepdims=True)
    r_.gbrow[...] = (own_gate * r_.yrow[...].astype(F32)).astype(BF16)

    def gelu_kernel(pre):
        cumul = 0.5 * (1.0 + lax.erf(pre * SQRT_HALF))
        return pre * cumul, cumul + pre * jnp.exp(-0.5 * pre * pre) * INV_ROOT_TWO_PI

    r_.gacc[...] = jnp.zeros((N, D), F32)
    r_.ggate[...] = jnp.zeros((N, LANES), F32)
    r_.gatec[...] = jnp.broadcast_to(own_gate, (N, LANES))

    def middle(j, carry):
        cut = pl.ds(pl.multiple_of(j * FT, FT), FT)
        pre = dot(r_.xrow[...], up[:, cut]) + r_.upb[:, cut].astype(F32)
        act_val, slope = gelu_kernel(pre)
        grad_act = r_.ga[:, cut].astype(F32)
        r_.act[:, cut] = act_val.astype(BF16)
        grad_pre = (r_.gatec[:, 0:1] * grad_act * slope).astype(BF16)
        r_.gp[:, cut] = grad_pre
        r_.gacc[...] += dot_nt(grad_pre, up[:, cut])
        both = act_val * grad_act
        r_.ggate[...] += sum(both[:, f : f + LANES] for f in range(0, FT, LANES))
        return carry

    lax.fori_loop(0, FF // FT, middle, 0)
    gate_grad = jnp.sum(r_.ggate[...], axis=-1, keepdims=True) + jnp.sum(
        r_.yrow[...].astype(F32) * r_.downb[...].astype(F32), axis=-1, keepdims=True
    )
    picked = jnp.where(slot_lane == me, 1.0, 0.0)
    contrib = (own_gates * (picked - own_gate) * gate_grad).astype(BF16)
    r_.gacc[...] += dot_nt(contrib, r_.smf[...])
    rows_drain(r_.hbuf, r_.hland, r_.h_sem)
    pack_slots(r_.gacc[...].astype(BF16), r_.rbuf)
    rows_start(r_.rbuf, r_.rland, r_.r_sem)
    r_.rterm[...] = dot_tn(r_.xrow[...], contrib)

    for j in range(D // WT):
        cut = slice(j * WT, (j + 1) * WT)
        r_.gacc[:, cut] = dot(r_.act[...], down[:, cut]) + r_.downb[:, cut].astype(F32)
    rows_drain(r_.cbuf, r_.cland, r_.c_sem)
    pack_slots(r_.gacc[...].astype(BF16), r_.obuf)

    for copy in cot_copies + hid_copies:
        copy.wait_recv()
    unpack(r_.coth[0], r_.yo)
    unpack(r_.hoth[0], r_.xo)
    far_gates = gates_of(r_.xo[...])
    far_gate = jnp.sum(jnp.where(slot_lane == me, far_gates, 0.0), axis=-1, keepdims=True)
    r_.yo[...] = (far_gate * r_.yo[...].astype(F32)).astype(BF16)

    def far(j, carry):
        cut = pl.ds(pl.multiple_of(j * FT, FT), FT)
        whole = pl.ds(pl.multiple_of(mine * part + j * FT, LANES), FT)
        pre = dot(r_.xo[...], up[:, whole]) + r_.upb[:, whole].astype(F32)
        act_val, slope = gelu_kernel(pre)
        r_.act_o[:, cut] = act_val.astype(BF16)
        grad_act = dot_nt(r_.yo[...], down[whole, :])
        r_.gp_o[:, cut] = (grad_act * slope).astype(BF16)
        return carry

    lax.fori_loop(0, part // FT, far, 0)

    half = D // 2
    pieces = [(True, row, lane) for lane in range(0, part, D) for row in range(0, D, half)]
    pieces += [(False, row, 0) for row in range(0, part, half)]
    kept = []

    def weight_grads(count):
        for is_up, row, lane in pieces[len(kept) : len(kept) + count]:
            if is_up:
                there = pl.ds(pl.multiple_of(mine * part + lane, LANES), D)
                own_gp, far_gp = r_.gp[:, there], r_.gp_o[:, lane : lane + D]
                value = dot_tn(r_.xrow[:, row : row + half], own_gp)
                value = value + dot_tn(r_.xo[:, row : row + half], far_gp)
                dst = r_.o_up.at[row : row + half, lane : lane + D]
                if row == 0:
                    r_.o_upb[:, lane : lane + D] = jnp.sum(
                        own_gp.astype(F32), axis=0, keepdims=True
                    ) + jnp.sum(far_gp.astype(F32), axis=0, keepdims=True)
            else:
                there = pl.ds(pl.multiple_of(mine * part + row, LANES), half)
                value = dot_tn(r_.act[:, there], r_.gbrow[...])
                value = value + dot_tn(r_.act_o[:, row : row + half], r_.yo[...])
                dst = r_.o_down.at[row : row + half]
            at = len(kept)
            slot = r_.stage.at[at % 2, 0:half]
            if at >= 2:
                kept[at - 2].wait()
            slot[...] = value
            copy = pltpu.make_async_copy(slot, dst, r_.keep_sem.at[at])
            copy.start()
            kept.append(copy)

    pending = []

    def launch(copies):
        for copy in copies:
            copy.start()
        pending.extend(copies)
        return copies

    def core_start(tag):
        own, from_core, _, _, _, sems = tag
        return launch(
            [
                copy_to(
                    own.at[other_core], from_core, sems.at[0], sems.at[1],
                    shard=shard_of(at_z, at_y, other_core),
                )
            ]
        )

    def y_start(tag, before):
        own, from_core, from_y, _, _, sems = tag
        for copy in before:
            copy.wait_recv()
        for y in range(Y):
            own[core, y] = (own[core, y].astype(F32) + from_core[y].astype(F32)).astype(BF16)
        return launch(
            [
                copy_to(
                    own.at[core, turn(at_y, dy, Y)], from_y.at[dy - 1], sems.at[2 * dy],
                    sems.at[2 * dy + 1], shard=shard_of(at_z, turn(at_y, dy, Y), core),
                )
                for dy in range(1, Y)
            ]
        )

    def z_start(tag, before):
        own, _, from_y, from_z, _, sems = tag
        for copy in before:
            copy.wait_recv()
        total = own[core, at_y].astype(F32)
        for dy in range(1, Y):
            total = total + from_y[dy - 1].astype(F32)
        own[core, at_y] = total.astype(BF16)
        base = 2 * Y
        return launch(
            [
                copy_to(
                    own.at[core, at_y, turn(at_z, dz, Z)], from_z.at[dz - 1], sems.at[base + 2 * dz - 2],
                    sems.at[base + 2 * dz - 1], shard=shard_of(turn(at_z, dz, Z), at_y, core),
                )
                for dz in range(1, Z)
            ]
        )

    def x_start(tag, before):
        own, _, _, from_z, from_x, sems = tag
        for copy in before:
            copy.wait_recv()
        total = own[core, at_y, at_z].astype(F32)
        for dz in range(1, Z):
            total = total + from_z[dz - 1].astype(F32)
        own[core, at_y, at_z] = total.astype(BF16)
        base = 2 * Y + 2 * Z - 2
        return launch(
            [
                copy_to(
                    own.at[core, at_y, at_z], from_x.at[dx - 1], sems.at[base + 2 * dx - 2],
                    sems.at[base + 2 * dx - 1], replica=turn(mine, dx, R),
                )
                for dx in range(1, R)
            ]
        )

    def finish(tag, before, out):
        own, _, _, _, from_x, _ = tag
        for copy in before:
            copy.wait_recv()
        total = own[core, at_y, at_z].astype(F32)
        for dx in range(1, R):
            total = total + from_x[dx - 1].astype(F32)
        out[...] = total

    def put_part(tag, lane_at, value):
        own = tag[0]
        wide = value.shape[1]
        low_value = value.astype(BF16)
        for z in range(Z):
            for y in range(Y):
                for c in range(2):
                    s = (z * Y + y) * 2 + c
                    own[c, y, z, :, lane_at : lane_at + wide] = low_value[s * K : (s + 1) * K, :]

    vecs = r_.vecs
    vecs[...] = jnp.zeros((LANES, D), F32)

    def put_vector(i, value):
        vecs[E + i : E + i + 1, :] = value

    rows_wait(r_.rbuf, r_.rland, r_.r_sem)
    rows_start(r_.obuf, r_.oland, r_.o_sem)
    flat_back = r_.rland[...].reshape(SB, LW)
    for i in range(q):
        r_.gn[:, i * LW : (i + 1) * LW] = dot(r_.place[0, i] + r_.place[1, i], flat_back)

    def norm_grad(grad_rows, normed, inv, gain, at_gain, at_bias):
        scaled = grad_rows * gain
        inner = (
            scaled
            - jnp.mean(scaled, axis=-1, keepdims=True)
            - normed * jnp.mean(scaled * normed, axis=-1, keepdims=True)
        )
        put_vector(at_gain, jnp.sum(grad_rows * normed, axis=0, keepdims=True))
        put_vector(at_bias, jnp.sum(grad_rows, axis=0, keepdims=True))
        return inner * inv

    gres[...] = cotf[...] + norm_grad(r_.gn[...], n2[...], inv_two, vector(5), 5, 6)
    put_vector(4, jnp.sum(gres[...], axis=0, keepdims=True))
    r_.tmpb[...] = gres[...].astype(BF16)
    for j in range(D // WT):
        cut = slice(j * WT, (j + 1) * WT)
        put_part(r_.rs_o, j * WT, dot_tn(r_.ctx[...], r_.tmpb[:, cut]))
    stage_o = core_start(r_.rs_o)
    for j in range(D // WT):
        cut = slice(j * WT, (j + 1) * WT)
        r_.gctx[:, cut] = dot_nt(r_.tmpb[...], r_.wf_out[cut, :]).astype(BF16)

    def attend_back(i, carry):
        cut_q, cut_k, cut_v = pair_cuts(i)
        query, keys, values = r_.qkv[:, cut_q], r_.qkv[:, cut_k], r_.qkv[:, cut_v]
        query_half, key_half, grad_half = halves(query), halves(keys), halves(r_.gctx[:, cut_q])
        grad_q = grad_k = grad_v = None
        for a in range(2):
            probs = r_.probs[2 * i + a]
            grad_probs = dot_nt(grad_half[a], values)
            inner = jnp.sum(probs * grad_probs, axis=-1, keepdims=True)
            grad_scores = (probs * (grad_probs - inner) * scale).astype(BF16)
            terms = (
                dot(grad_scores, key_half[a]),
                dot_tn(grad_scores, query_half[a]),
                dot_tn(probs.astype(BF16), grad_half[a]),
            )
            if a == 0:
                grad_q, grad_k, grad_v = terms
            else:
                grad_q, grad_k, grad_v = grad_q + terms[0], grad_k + terms[1], grad_v + terms[2]
        r_.gm[:, cut_q] = grad_q.astype(BF16)
        r_.gm[:, cut_k] = grad_k.astype(BF16)
        r_.gm[:, cut_v] = grad_v.astype(BF16)
        vecs[E + 2 : E + 3, cut_q] = jnp.sum(grad_q, axis=0, keepdims=True)
        vecs[E + 3 : E + 4, cut_q] = jnp.sum(grad_v, axis=0, keepdims=True)
        return carry

    lax.fori_loop(0, pairs, attend_back, 0)
    stage_o = y_start(r_.rs_o, stage_o)

    def proj_part(tag, at):
        for j in range(D // WT):
            put_part(
                tag, j * WT, dot_tn(r_.act1[...], r_.gm[:, at + j * WT : at + (j + 1) * WT])
            )
        return core_start(tag)

    stage_v = proj_part(r_.rs_v, 2 * D)
    stage_k = proj_part(r_.rs_k, D)
    stage_o = z_start(r_.rs_o, stage_o)
    stage_v = y_start(r_.rs_v, stage_v)
    stage_q = proj_part(r_.rs_q, 0)
    stage_k = y_start(r_.rs_k, stage_k)
    for j in range(D // WT):
        cut = slice(j * WT, (j + 1) * WT)
        r_.gn[:, cut] = dot_nt(r_.gm[...], r_.wf_in[cut, :])
    stage_q = y_start(r_.rs_q, stage_q)
    grad_tok = gres[...] + norm_grad(r_.gn[...], n1[...], inv_one, vector(0), 0, 1)
    r_.o_grad[...] = grad_tok[0:T].astype(BF16)
    put_part(r_.rs_s, 0, vecs[...].T + r_.rterm[...])
    stage_s = core_start(r_.rs_s)
    stage_o = x_start(r_.rs_o, stage_o)
    stage_v = z_start(r_.rs_v, stage_v)
    stage_s = y_start(r_.rs_s, stage_s)

    rows_wait(r_.obuf, r_.oland, r_.o_sem)
    flat_out = r_.oland[...].reshape(SB, LW)
    for i in range(q):
        cut = slice(i * LW, (i + 1) * LW)
        total = resid[:, cut]
        for k in range(2):
            total = total + pair_gate[k] * dot(r_.place[k, i], flat_out)
        r_.o_rows[:, cut] = total[0:T].astype(BF16)

    weight_grads(2)
    stage_k = z_start(r_.rs_k, stage_k)
    finish(r_.rs_o, stage_o, r_.o_out)
    weight_grads(2)
    stage_v = x_start(r_.rs_v, stage_v)
    stage_q = z_start(r_.rs_q, stage_q)
    stage_s = z_start(r_.rs_s, stage_s)
    weight_grads(2)
    stage_k = x_start(r_.rs_k, stage_k)
    finish(r_.rs_v, stage_v, r_.o_proj.at[:, 2 * D : 3 * D])
    weight_grads(len(pieces) - len(kept))
    total_grad = jnp.sum(r_.gbrow[...].astype(F32), axis=0, keepdims=True)
    total_grad = total_grad + jnp.sum(r_.yo[...].astype(F32), axis=0, keepdims=True)
    bias[0:1, 0:D] = total_grad
    r_.o_downb[...] = bias[0:1, pl.ds(pl.multiple_of(mine * (D // R), LANES), D // R)]
    stage_q = x_start(r_.rs_q, stage_q)
    stage_s = x_start(r_.rs_s, stage_s)
    finish(r_.rs_k, stage_k, r_.o_proj.at[:, D : 2 * D])
    finish(r_.rs_q, stage_q, r_.o_proj.at[:, 0:D])
    finish(r_.rs_s, stage_s, turned.at[0:K])
    r_.o_small[...] = turned[...].T[0 : r_.o_small.shape[0], 0:K]

    state.drain = True
    for a in (SMALL, BOTH, OWN, OUT):
        gather_start(a)
    to_core(FAR, me, r_.w_in.at[:, far_lanes])
    gather_lines(SMALL, BOTH, OWN, OUT)
    gather_x()
    rows_drain(r_.rbuf, r_.rland, r_.r_sem)
    rows_drain(r_.obuf, r_.oland, r_.o_sem)
    for copy in cot_copies + hid_copies + pending:
        copy.wait_send()
    for copy in kept[-2:]:
        copy.wait()


def call_block(plan, *arrays):
    S, R, TP, FF, E = plan.S, plan.R, plan.TP, plan.FF, plan.E
    K, q, BR, LW, SB, N, Z, Y, part = (
        plan.K, plan.q, plan.BR, plan.LW, plan.SB, plan.N, plan.Z, plan.Y, plan.part,
    )
    vmem = pl.BlockSpec(memory_space=pltpu.VMEM)
    anyw = pl.BlockSpec(memory_space=pl.ANY)
    outs = dict(
        o_rows=((plan.T, D), BF16, vmem),
        o_grad=((plan.T, D), BF16, vmem),
        o_proj=((K, 3 * D), F32, vmem),
        o_out=((K, D), F32, vmem),
        o_small=((-(-(E + VECTORS) // 8) * 8, K), F32, vmem),
        o_up=((D, part), F32, anyw),
        o_upb=((1, part), F32, vmem),
        o_down=((part, D), F32, anyw),
        o_downb=((1, D // R), F32, vmem),
    )

    def landing(wide):
        return (
            pltpu.VMEM((2, Y, Z, K, wide), BF16),
            pltpu.VMEM((Y, Z, K, wide), BF16),
            pltpu.VMEM((max(Y - 1, 1), Z, K, wide), BF16),
            pltpu.VMEM((max(Z - 1, 1), K, wide), BF16),
            pltpu.VMEM((max(R - 1, 1), K, wide), BF16),
            pltpu.SemaphoreType.DMA((2 * (Y + Z + R),)),
        )

    def pairs_of(*extent):
        return pltpu.SemaphoreType.DMA(extent)

    rows = pltpu.VMEM((S, BR, LW), BF16)
    far_rows = pltpu.VMEM((R - 1, S, BR, LW), BF16)
    wide_rows = pltpu.VMEM((TP, D), F32)
    half_rows = pltpu.VMEM((TP, D), BF16)
    slot_rows = pltpu.VMEM((N, D), BF16)
    scratch = dict(
        up=pltpu.VMEM((D, FF), BF16),
        down=pltpu.VMEM((FF, D), BF16),
        wf_in=pltpu.VMEM((D, 3 * D), BF16),
        wf_out=pltpu.VMEM((D, D), BF16),
        smf=pltpu.VMEM((D, LANES), BF16),
        smt=pltpu.VMEM((LANES, D), F32),
        turned=pltpu.VMEM((LANES, LANES), F32),
        small=pltpu.VMEM((K, LANES), BF16),
        pairs_at=pltpu.VMEM((LANES, -(-TP // LANES) * LANES), F32),
        place=pltpu.VMEM((2, q, TP, SB), BF16),
        unroll=pltpu.VMEM((q, N, SB), BF16),
        cotf=wide_rows, n1=wide_rows, n2=wide_rows, resid=wide_rows, gres=wide_rows,
        gn=wide_rows,
        tmpb=half_rows, act1=half_rows, hid=half_rows, ctx=half_rows,
        bias=pltpu.VMEM((8, 3 * D), F32),
        qkv=pltpu.VMEM((TP, 3 * D), BF16),
        gm=pltpu.VMEM((TP, 3 * D), BF16),
        probs=pltpu.VMEM((HEADS, TP, TP), F32),
        cbuf=rows, cland=rows, hbuf=rows, hland=rows, rland=rows, oland=rows,
        coth=far_rows, hoth=far_rows,
        yrow=slot_rows, xrow=slot_rows, gbrow=slot_rows,
        xo=slot_rows,
        ga=pltpu.VMEM((N, FF), BF16),
        act=pltpu.VMEM((N, FF), BF16),
        gp=pltpu.VMEM((N, FF), BF16),
        act_o=pltpu.VMEM((N, part), BF16),
        gp_o=pltpu.VMEM((N, part), BF16),
        stage=pltpu.VMEM((2, N, D), F32),
        ggate=pltpu.VMEM((N, LANES), F32),
        gatec=pltpu.VMEM((N, LANES), F32),
        rterm=pltpu.VMEM((D, LANES), F32),
        vecs=pltpu.VMEM((LANES, D), F32),
        rs_o=landing(D), rs_v=landing(D), rs_k=landing(D), rs_q=landing(D), rs_s=landing(LANES),
        load_sem=pairs_of(2),
        ag_send=pairs_of(5, 3 + Y, S),
        ag_recv=pairs_of(5, S),
        c_sem=pairs_of(2, S),
        h_sem=pairs_of(2, S),
        r_sem=pairs_of(2, S),
        o_sem=pairs_of(2, S),
        cx_sem=pairs_of(2, R),
        hx_sem=pairs_of(2, R),
        keep_sem=pairs_of(2 * (part // D) + 2 * part // D),
    )
    return pl.pallas_call(
        functools.partial(block_kernel, plan, list(outs)),
        out_shape=[jax.ShapeDtypeStruct(o[0], o[1]) for o in outs.values()],
        in_specs=[vmem] * (9 + VECTORS) + [anyw] * 2,
        out_specs=[o[2] for o in outs.values()],
        scratch_shapes=scratch,
        compiler_params=pltpu.CompilerParams(
            collective_id=0, has_side_effects=True, vmem_limit_bytes=60 * 1024 * 1024
        ),
        cost_estimate=pl.CostEstimate(
            flops=12 * N * D * FF, bytes_accessed=4 * D * FF, transcendentals=2 * N * FF
        ),
    )(*arrays)


def outputs_kernel(plan, count, *refs):
    srcs, small, rest = refs[:count], refs[count], refs[count + 1 :]
    dsts, vectors, router = rest[:count], rest[count : count + VECTORS], rest[count + VECTORS]
    lands, sems = rest[count + VECTORS + 1 : -1], rest[-1]
    steps = []
    for src, land, dst in zip(srcs, lands, dsts):
        cuts = 4 if src.shape[0] % 64 == 0 else 1
        rows = src.shape[0] // cuts
        for cut in range(cuts):
            part = pl.ds(cut * rows, rows)
            at = len(steps)
            fetch = pltpu.make_async_copy(src.at[part], land.at[part], sems.at[0, at])
            fetch.start()
            steps.append((fetch, pltpu.make_async_copy(land.at[part], dst.at[part], sems.at[1, at])))
    for i, vector in enumerate(vectors):
        vector[...] = small[plan.E + i : plan.E + i + 1, :].reshape(plan.K)
    router[...] = small[0 : plan.E, :]
    for fetch, store in steps:
        fetch.wait()
        store.start()
    for _, store in steps:
        store.wait()


def call_outputs(plan, arrays, small):
    vmem = pl.BlockSpec(memory_space=pltpu.VMEM)
    anyw = pl.BlockSpec(memory_space=pl.ANY)
    count = len(arrays)
    return pl.pallas_call(
        functools.partial(outputs_kernel, plan, count),
        out_shape=[jax.ShapeDtypeStruct(a.shape, a.dtype) for a in arrays]
        + [jax.ShapeDtypeStruct((plan.K,), F32)] * VECTORS
        + [jax.ShapeDtypeStruct((plan.E, plan.K), F32)],
        in_specs=[anyw] * count + [vmem],
        out_specs=[anyw] * count + [vmem] * (VECTORS + 1),
        scratch_shapes=[pltpu.VMEM(a.shape, a.dtype) for a in arrays]
        + [pltpu.SemaphoreType.DMA((2, 4 * count))],
        compiler_params=pltpu.CompilerParams(vmem_limit_bytes=60 * 1024 * 1024),
    )(*arrays, small)


def body(
    tokens, cotangent, norm1_gain, norm1_bias, proj_in, query_bias, value_bias, proj_out, out_bias,
    norm2_gain, norm2_bias, router, up_weight, up_bias, down_weight, down_bias, expert_ids, slot_ids,
):
    shards, replicas = lax.axis_size("shard"), lax.axis_size("replica")
    rows = tokens.shape[0] * tokens.shape[1]
    plan = Plan(shards, replicas, rows, up_weight.shape[2], up_weight.shape[0])
    if plan.part % D or plan.N < D // 2 or up_weight.shape[0] != 1 or tokens.shape[0] != 1:
        return plain_body(
            tokens, cotangent, norm1_gain, norm1_bias, proj_in, query_bias, value_bias, proj_out,
            out_bias, norm2_gain, norm2_bias, router, up_weight, up_bias, down_weight, down_bias,
            expert_ids, slot_ids,
        )
    (o_rows, o_grad, o_proj, o_out, o_small, o_up, o_upb, o_down, o_downb) = call_block(
        plan, tokens.reshape(rows, D), cotangent.reshape(rows, D), proj_in, proj_out, router.T,
        expert_ids.T, slot_ids.T, up_bias, down_bias, norm1_gain, norm1_bias, query_bias, value_bias,
        out_bias, norm2_gain, norm2_bias, up_weight[0], down_weight[0],
    )
    (o_up, o_down, o_rows, o_grad, o_proj, o_out, o_upb, o_downb, *vec, o_router) = call_outputs(
        plan, [o_up, o_down, o_rows, o_grad, o_proj, o_out, o_upb, o_downb], o_small
    )
    return (
        o_rows.reshape(tokens.shape),
        o_grad.reshape(tokens.shape),
        vec[0], vec[1], o_proj, vec[2], vec[3], o_out, vec[4], vec[5], vec[6], o_router.T,
        o_up[None], o_upb, o_down[None], o_downb,
    )


def fits_kernel(mesh):
    shards, replicas = mesh.shape["shard"], mesh.shape["replica"]
    return shards % 2 == 0 and D % shards == 0 and (D // shards) % 16 == 0 and replicas == 2


def solution(mesh):
    in_specs = (
        P(("replica", "shard"), None, None),
        P(("replica", "shard"), None, None),
        P("shard"),
        P("shard"),
        P("shard", None),
        P("shard"),
        P("shard"),
        P("shard", None),
        P("shard"),
        P("shard"),
        P("shard"),
        P("shard", None),
        P("shard", None, None),
        P("shard", None),
        P("shard", None, None),
        P("shard", None),
        P(("replica", "shard"), None),
        P(("replica", "shard"), None),
    )
    out_specs = (
        P(("replica", "shard"), None, None),
        P(("replica", "shard"), None, None),
        P("shard"),
        P("shard"),
        P("shard", None),
        P("shard"),
        P("shard"),
        P("shard", None),
        P("shard"),
        P("shard"),
        P("shard"),
        P("shard", None),
        P("shard", None, "replica"),
        P("shard", "replica"),
        P("shard", "replica", None),
        P("shard", "replica"),
    )
    chosen = body if fits_kernel(mesh) else plain_body
    return jax.shard_map(chosen, mesh=mesh, in_specs=in_specs, out_specs=out_specs, check_vma=False)
```

```python
import functools
from types import SimpleNamespace

import jax
import jax.numpy as jnp
from jax import lax
from jax.experimental import pallas as pl
from jax.experimental.pallas import tpu as pltpu
from jax.sharding import PartitionSpec as P

D = 768
HEADS = 12
HDIM = 64
SEQ = 197


EPS = 1e-06
SQRT_HALF = 0.7071067811865476
INV_ROOT_TWO_PI = 0.3989422804014327


def layer_norm(rows_in, norm_gain, norm_shift):
    average = jnp.mean(rows_in, axis=-1, keepdims=True)
    centred = rows_in - average
    inv_std = lax.rsqrt(jnp.mean(centred * centred, axis=-1, keepdims=True) + EPS)
    normed = centred * inv_std
    return (normed, inv_std, normed * norm_gain + norm_shift)


def norm_back(grad_rows, normed, inv_std, norm_gain):
    scaled = grad_rows * norm_gain
    inner = (
        scaled
        - jnp.mean(scaled, axis=-1, keepdims=True)
        - normed * jnp.mean(scaled * normed, axis=-1, keepdims=True)
    )
    return (inner * inv_std, jnp.sum(grad_rows * normed, axis=0), jnp.sum(grad_rows, axis=0))


def gelu_parts(pre_act):
    cumul = 0.5 * (1.0 + lax.erf(pre_act * SQRT_HALF))
    return (pre_act * cumul, cumul + pre_act * jnp.exp(-0.5 * pre_act * pre_act) * INV_ROOT_TWO_PI)


def route_table(expert_ids, slot_ids, experts, capacity):
    positions = jnp.arange(experts * capacity, dtype=jnp.int32)
    tables = []
    for choose in range(2):
        kept = slot_ids[:, choose] < capacity
        target = jnp.where(kept, expert_ids[:, choose] * capacity + slot_ids[:, choose], -1)
        tables.append((target[:, None] == positions[None, :]).astype(jnp.bfloat16))
    return tables


def pick_table(expert_ids, experts):
    labels = jnp.arange(experts, dtype=jnp.int32)
    return [
        (expert_ids[:, choose][:, None] == labels[None, :]).astype(jnp.float32)
        for choose in range(2)
    ]


def lane_pad(blocks):
    rows = blocks[0].shape[0]
    spare = -sum(block.shape[1] for block in blocks) % 128
    return jnp.concatenate(blocks + [jnp.zeros((rows, spare), blocks[0].dtype)], axis=1)


def other_replicas(value):
    size = lax.axis_size("replica")
    return [
        lax.ppermute(value, "replica", [(at, (at + step) % size) for at in range(size)])
        for step in range(1, size)
    ]


def to_expert(value, local_experts, capacity):
    shards, width = value.shape[0], value.shape[-1]
    return (
        value.reshape(shards, local_experts, capacity, width)
        .swapaxes(0, 1)
        .reshape(local_experts, shards * capacity, width)
    )


def from_expert(value, shards, capacity):
    local_experts, width = value.shape[0], value.shape[-1]
    return (
        value.reshape(local_experts, shards, capacity, width)
        .swapaxes(0, 1)
        .reshape(shards, local_experts * capacity, width)
    )


def expert_middle(rows, grad_rows, up_weight, up_bias, down_weight):
    expert_pre = (
        jnp.einsum("ecd,edf->ecf", rows, up_weight, preferred_element_type=jnp.float32)
        + up_bias.astype(jnp.float32)[:, None, :]
    )
    act_val, slope = gelu_parts(expert_pre)
    grad_active = jnp.einsum(
        "ecd,efd->ecf", grad_rows, down_weight, preferred_element_type=jnp.float32
    )
    return (act_val.astype(jnp.bfloat16), (grad_active * slope).astype(jnp.bfloat16))


def plain_body(
    tokens,
    cotangent,
    norm1_gain,
    norm1_bias,
    proj_in,
    query_bias,
    value_bias,
    proj_out,
    out_bias,
    norm2_gain,
    norm2_bias,
    router,
    up_weight,
    up_bias,
    down_weight,
    down_bias,
    expert_ids,
    slot_ids,
):
    images = tokens.shape[0]
    small = jnp.stack(
        [norm1_gain, norm1_bias, query_bias, value_bias, out_bias, norm2_gain, norm2_bias],
        axis=1,
    )
    width_in, width_small = proj_in.shape[1], small.shape[1] + router.shape[1]
    first = lax.all_gather(
        lane_pad([proj_in, proj_out, small, router]), "shard", axis=0, tiled=True
    )
    width_both = width_in + proj_out.shape[1]
    proj_full = first[:, :width_in]
    outproj_full = first[:, width_in:width_both]
    small_full = first[:, width_both : width_both + small.shape[1]]
    router_full = first[:, width_both + small.shape[1] : width_both + width_small]
    (
        gain_one,
        shift_one,
        query_shift,
        value_shift,
        out_shift,
        gain_two,
        shift_two,
    ) = [row for row in small_full.T]
    tok_rows = tokens.reshape(-1, D).astype(jnp.float32)
    normed_one, inv_one, pre_one = layer_norm(
        tok_rows, gain_one.astype(jnp.float32), shift_one.astype(jnp.float32)
    )
    act_one = pre_one.astype(jnp.bfloat16)
    mixed = jnp.dot(act_one, proj_full, preferred_element_type=jnp.float32)
    query_part = (mixed[:, :D] + query_shift.astype(jnp.float32)).astype(jnp.bfloat16)
    key_part = mixed[:, D : 2 * D].astype(jnp.bfloat16)
    value_part = (mixed[:, 2 * D :] + value_shift.astype(jnp.float32)).astype(jnp.bfloat16)
    query_heads = query_part.reshape(images, SEQ, HEADS, HDIM)
    key_heads = key_part.reshape(images, SEQ, HEADS, HDIM)
    value_heads = value_part.reshape(images, SEQ, HEADS, HDIM)
    scores = jnp.einsum(
        "ishd,ithd->ihst", query_heads, key_heads, preferred_element_type=jnp.float32
    ) * HDIM ** (-0.5)
    log_total = jnp.log(jnp.sum(jnp.exp(scores), axis=-1))
    attn_probs = jnp.exp(scores - log_total[..., None]).astype(jnp.bfloat16)
    context = (
        jnp.einsum("ihst,ithd->ishd", attn_probs, value_heads, preferred_element_type=jnp.float32)
        .reshape(-1, D)
        .astype(jnp.bfloat16)
    )
    resid = (
        tok_rows
        + jnp.dot(context, outproj_full, preferred_element_type=jnp.float32)
        + out_shift.astype(jnp.float32)
    )
    normed_two, inv_two, pre_two = layer_norm(
        resid, gain_two.astype(jnp.float32), shift_two.astype(jnp.float32)
    )
    hidden = pre_two.astype(jnp.bfloat16)
    logits = jnp.dot(hidden, router_full, preferred_element_type=jnp.float32)
    exp_logits = jnp.exp(logits)
    gate_probs = exp_logits / jnp.sum(exp_logits, axis=-1, keepdims=True)
    local_experts = up_weight.shape[0]
    experts = local_experts * lax.axis_size("shard")
    capacity = 2 * tok_rows.shape[0] // experts
    routes = route_table(expert_ids, slot_ids, experts, capacity)
    picks = pick_table(expert_ids, experts)
    both = jnp.concatenate(routes, axis=0)
    either = routes[0] + routes[1]
    gate_pair = [jnp.sum(gate_probs * pick, axis=-1) for pick in picks]
    grad_out = cotangent.reshape(-1, D).astype(jnp.float32)
    sent = jnp.concatenate(
        [(gate[:, None] * grad_out).astype(jnp.bfloat16) for gate in gate_pair], axis=0
    )
    buffer = jnp.dot(either.T, hidden, preferred_element_type=jnp.float32)
    grad_buffer = jnp.dot(both.T, sent, preferred_element_type=jnp.float32)
    shards = lax.axis_size("shard")
    outgoing = (
        jnp.concatenate([buffer, grad_buffer], axis=1)
        .astype(jnp.bfloat16)
        .reshape(shards, local_experts * capacity, 2 * D)
    )
    landed = to_expert(
        lax.all_to_all(outgoing, "shard", split_axis=0, concat_axis=0, tiled=True),
        local_experts,
        capacity,
    )
    arrived, grad_arrived = landed[..., :D], landed[..., D:]
    others = other_replicas(landed)
    active, grad_pre = expert_middle(arrived, grad_arrived, up_weight, up_bias, down_weight)
    expert_out = (
        jnp.einsum("ecf,efd->ecd", active, down_weight, preferred_element_type=jnp.float32)
        + down_bias.astype(jnp.float32)[:, None, :]
    ).astype(jnp.bfloat16)
    grad_in = jnp.einsum(
        "ecf,edf->ecd", grad_pre, up_weight, preferred_element_type=jnp.float32
    ).astype(jnp.bfloat16)
    answer = from_expert(jnp.concatenate([expert_out, grad_in], axis=2), shards, capacity)
    back = lax.all_to_all(answer, "shard", split_axis=0, concat_axis=0, tiled=True).reshape(
        experts * capacity, 2 * D
    )
    returned, grad_back = back[:, :D], back[:, D:]

    replicas = lax.axis_size("replica")
    ours = lax.axis_index("replica")
    part = up_weight.shape[2] // replicas
    up_part = lax.dynamic_slice_in_dim(up_weight, ours * part, part, axis=2)
    up_bias_part = lax.dynamic_slice_in_dim(up_bias, ours * part, part, axis=1)
    down_part = lax.dynamic_slice_in_dim(down_weight, ours * part, part, axis=1)
    active_parts = [lax.dynamic_slice_in_dim(active, ours * part, part, axis=2)]
    grad_pre_parts = [lax.dynamic_slice_in_dim(grad_pre, ours * part, part, axis=2)]
    for other in others:
        other_active, other_pre = expert_middle(
            other[..., :D], other[..., D:], up_part, up_bias_part, down_part
        )
        active_parts.append(other_active)
        grad_pre_parts.append(other_pre)
    all_rows = jnp.concatenate([landed] + others, axis=1)
    all_active = jnp.concatenate(active_parts, axis=1)
    all_pre = jnp.concatenate(grad_pre_parts, axis=1)
    width_part = D // replicas
    expert_grads = (
        jnp.einsum("ecd,ecf->edf", all_rows[..., :D], all_pre, preferred_element_type=jnp.float32),
        jnp.sum(all_pre, axis=1, dtype=jnp.float32),
        jnp.einsum(
            "ecf,ecd->efd", all_active, all_rows[..., D:], preferred_element_type=jnp.float32
        ),
        lax.dynamic_slice_in_dim(
            jnp.sum(all_rows[..., D:], axis=1, dtype=jnp.float32),
            ours * width_part,
            width_part,
            axis=1,
        ),
    )

    rows_here = tok_rows.shape[0]
    gathered_both = jnp.dot(both, returned, preferred_element_type=jnp.float32)
    gathered_pair = [gathered_both[:rows_here], gathered_both[rows_here:]]
    moe_sum = gate_pair[0][:, None] * gathered_pair[0] + gate_pair[1][:, None] * gathered_pair[1]
    block_out = (resid + moe_sum).astype(jnp.bfloat16).reshape(tokens.shape)
    grad_gate = [jnp.sum(grad_out * part_k, axis=-1) for part_k in gathered_pair]
    back_gain_one, back_proj, back_outproj, back_gain_two, back_router = (
        gain_one,
        proj_full,
        outproj_full,
        gain_two,
        router_full,
    )
    grad_moe = jnp.dot(either, grad_back, preferred_element_type=jnp.float32)
    grad_gates = picks[0] * grad_gate[0][:, None] + picks[1] * grad_gate[1][:, None]
    grad_logits = (
        gate_probs * (grad_gates - jnp.sum(gate_probs * grad_gates, axis=-1, keepdims=True))
    ).astype(jnp.bfloat16)
    router_term = jnp.dot(hidden.T, grad_logits, preferred_element_type=jnp.float32)
    grad_norm_two = grad_moe + jnp.dot(
        grad_logits, back_router.T, preferred_element_type=jnp.float32
    )
    grad_resid_two, gain_two_term, shift_two_term = norm_back(
        grad_norm_two, normed_two, inv_two, back_gain_two.astype(jnp.float32)
    )
    grad_resid = grad_out + grad_resid_two
    resid_bf = grad_resid.astype(jnp.bfloat16)
    out_shift_term = jnp.sum(grad_resid, axis=0)
    outproj_term = jnp.dot(context.T, resid_bf, preferred_element_type=jnp.float32)
    grad_context = (
        jnp.dot(resid_bf, back_outproj.T, preferred_element_type=jnp.float32)
        .astype(jnp.bfloat16)
        .reshape(images, SEQ, HEADS, HDIM)
    )
    scores_again = jnp.einsum(
        "ishd,ithd->ihst", query_heads, key_heads, preferred_element_type=jnp.float32
    ) * HDIM ** (-0.5)
    probs_full = jnp.exp(scores_again - log_total[..., None])
    grad_probs = jnp.einsum(
        "ishd,ithd->ihst", grad_context, value_heads, preferred_element_type=jnp.float32
    )
    grad_scores = (
        probs_full
        * (grad_probs - jnp.sum(probs_full * grad_probs, axis=-1, keepdims=True))
        * HDIM ** (-0.5)
    ).astype(jnp.bfloat16)
    probs_bf = probs_full.astype(jnp.bfloat16)
    grad_value = jnp.einsum(
        "ihst,ishd->ithd", probs_bf, grad_context, preferred_element_type=jnp.float32
    ).reshape(-1, D)
    grad_query = jnp.einsum(
        "ihst,ithd->ishd", grad_scores, key_heads, preferred_element_type=jnp.float32
    ).reshape(-1, D)
    grad_key = jnp.einsum(
        "ihst,ishd->ithd", grad_scores, query_heads, preferred_element_type=jnp.float32
    ).reshape(-1, D)
    grad_mixed = jnp.concatenate([grad_query, grad_key, grad_value], axis=1).astype(jnp.bfloat16)
    proj_term = jnp.dot(act_one.T, grad_mixed, preferred_element_type=jnp.float32)
    grad_act = jnp.dot(grad_mixed, back_proj.T, preferred_element_type=jnp.float32)
    grad_tok_norm, gain_one_term, shift_one_term = norm_back(
        grad_act, normed_one, inv_one, back_gain_one.astype(jnp.float32)
    )
    tokens_grad = (grad_resid + grad_tok_norm).astype(jnp.bfloat16).reshape(tokens.shape)
    query_shift_term = jnp.sum(grad_query, axis=0)
    value_shift_term = jnp.sum(grad_value, axis=0)
    column_sums = [
        gain_one_term,
        shift_one_term,
        query_shift_term,
        value_shift_term,
        out_shift_term,
        gain_two_term,
        shift_two_term,
    ]
    summed = lax.psum_scatter(
        lane_pad(
            [
                proj_term.astype(jnp.bfloat16),
                outproj_term.astype(jnp.bfloat16),
                lax.optimization_barrier(
                    lane_pad(
                        [
                            jnp.stack(column_sums, axis=0).astype(jnp.bfloat16).T,
                            router_term.astype(jnp.bfloat16),
                        ]
                    )
                ),
            ]
        ),
        "shard",
        scatter_dimension=0,
        tiled=True,
    )
    total = summed.astype(jnp.float32)
    for other in other_replicas(summed):
        total = total + other.astype(jnp.float32)
    small_total = total[:, width_both:]
    columns = len(column_sums)
    dense_grads = (
        small_total[:, 0],
        small_total[:, 1],
        total[:, :width_in],
        small_total[:, 2],
        small_total[:, 3],
        total[:, width_in:width_both],
        small_total[:, 4],
        small_total[:, 5],
        small_total[:, 6],
        small_total[:, columns : columns + experts],
    )
    return (
        block_out,
        tokens_grad,
        dense_grads[0],
        dense_grads[1],
        dense_grads[2],
        dense_grads[3],
        dense_grads[4],
        dense_grads[5],
        dense_grads[6],
        dense_grads[7],
        dense_grads[8],
        dense_grads[9],
        expert_grads[0],
        expert_grads[1],
        expert_grads[2],
        expert_grads[3],
    )


F32 = jnp.float32
BF16 = jnp.bfloat16
LANES = 128
VECTORS = 7


def dot(left, right):
    return jnp.dot(left, right, preferred_element_type=F32)


def dot_nt(left, right):
    return lax.dot_general(left, right, (((1,), (1,)), ((), ())), preferred_element_type=F32)


def dot_tn(left, right):
    return lax.dot_general(left, right, (((0,), (0,)), ((), ())), preferred_element_type=F32)


def iota(shape, axis):
    return lax.broadcasted_iota(jnp.int32, shape, axis)


class Plan:
    def __init__(self, shards, replicas, rows, hidden_units, local_experts):
        self.S, self.R, self.T, self.FF = shards, replicas, rows, hidden_units
        self.E = local_experts * shards
        self.C = 2 * rows // self.E
        self.TP = -(-rows // 16) * 16
        self.K = D // shards
        self.q = 2 if self.C % 16 and (2 * self.C) % 16 == 0 else 1
        self.CR = self.C if self.q == 2 else -(-self.C // 16) * 16
        self.BR = self.CR * self.q
        self.LW = D // self.q
        self.SB = shards * self.BR
        self.N = shards * self.CR
        self.part = hidden_units // replicas
        self.core = 2
        chips = shards // 2
        self.Z = 4 if chips % 4 == 0 else chips
        self.Y = chips // self.Z


def block_kernel(
    plan, out_names, tok, cot, w_in, w_out, router, ids, slots, upb, downb, *refs, **scratch
):
    vectors, (up_h, down_h), refs = refs[:VECTORS], refs[VECTORS : VECTORS + 2], refs[VECTORS + 2 :]
    r_ = SimpleNamespace(
        tok=tok, cot=cot, w_in=w_in, w_out=w_out, ids=ids, slots=slots, upb=upb,
        downb=downb, up_h=up_h, down_h=down_h, **dict(zip(out_names, refs)), **scratch,
    )
    r_.rbuf, r_.obuf, r_.gctx, r_.yo, r_.gacc = r_.hbuf, r_.cbuf, r_.hid, r_.yrow, r_.stage.at[0]
    S, R, T, TP, FF, E, C = plan.S, plan.R, plan.T, plan.TP, plan.FF, plan.E, plan.C
    K, q, CR, BR, LW, SB, N, Z, Y = (
        plan.K, plan.q, plan.CR, plan.BR, plan.LW, plan.SB, plan.N, plan.Z, plan.Y,
    )
    part = plan.part
    me = lax.axis_index("shard")
    mine = lax.axis_index("replica")
    core = lax.rem(me, 2)
    at_y = lax.rem(lax.div(me, 2), Y)
    at_z = lax.div(me, 2 * Y)
    other_core = 1 - core

    def shard_of(z, y, c):
        return (z * Y + y) * 2 + c

    def turn(base, step, size):
        return lax.rem(base + step, size)

    def copy_to(src, dst, send, recv, **device):
        return pltpu.make_async_remote_copy(
            src_ref=src, dst_ref=dst, send_sem=send, recv_sem=recv,
            device_id=device, device_id_type=pl.DeviceIdType.MESH,
        )

    load_up = pltpu.make_async_copy(r_.up_h, r_.up, r_.load_sem.at[0])
    load_down = pltpu.make_async_copy(r_.down_h, r_.down, r_.load_sem.at[1])
    load_up.start()
    load_down.start()

    turned = r_.turned
    turned[...] = jnp.zeros((LANES, LANES), F32)
    turned[0:E, 0:K] = router[...].astype(F32)
    for i, vector_ref in enumerate(vectors):
        turned[E + i : E + i + 1, 0:K] = vector_ref[...].astype(F32).reshape(1, K)
    r_.small[...] = turned[...].T[0:K, :].astype(BF16)

    barrier = pltpu.get_barrier_semaphore()
    for step in range(1, S):
        pl.semaphore_signal(
            barrier, inc=1, device_id={"shard": turn(me, step, S)}, device_id_type=pl.DeviceIdType.MESH
        )
    for step in range(1, R):
        pl.semaphore_signal(
            barrier, inc=1, device_id={"replica": turn(mine, step, R)}, device_id_type=pl.DeviceIdType.MESH
        )
    pl.semaphore_wait(barrier, S - 1 + R - 1)

    both_lanes, own_lanes = pl.ds(2 * D, D), pl.ds(pl.multiple_of(mine * D, LANES), D)
    far_lanes = pl.ds(pl.multiple_of((1 - mine) * D, LANES), D)
    every = slice(None)
    SMALL, BOTH, OWN, FAR, OUT = range(5)
    gathers = [
        (r_.small, r_.smf, every),
        (r_.w_in, r_.wf_in, both_lanes),
        (r_.w_in, r_.wf_in, own_lanes),
        (r_.w_in, r_.wf_in, far_lanes),
        (r_.w_out, r_.wf_out, every),
    ]
    UP, DOWN, CORE, REPLICA, ACROSS = range(5)
    state = SimpleNamespace(drain=False)

    def rows_of(s):
        return pl.ds(pl.multiple_of(s * K, 16), K)

    def block_of(a, s):
        return gathers[a][1].at[rows_of(s), gathers[a][2]]

    def send_block(a, s, src, way, lands=None, **device):
        copy = copy_to(
            src, block_of(a, s), r_.ag_send.at[a, way, s],
            r_.ag_recv.at[a if lands is None else lands, s], **device,
        )
        if state.drain:
            copy.wait_send()
        else:
            copy.start()

    def wait_block(a, s):
        if not state.drain:
            copy_to(
                block_of(a, s), block_of(a, s), r_.ag_send.at[a, CORE, s], r_.ag_recv.at[a, s],
                shard=s,
            ).wait_recv()

    def to_core(a, s, src):
        send_block(a, s, src, CORE, shard=shard_of(at_z, at_y, other_core))

    def to_replica(a, s, src):
        if a == OWN:
            send_block(OWN, s, src, REPLICA, lands=FAR, replica=1 - mine)

    def along(a, s, src, up):
        @pl.when(at_z < Z - 1 if up else at_z > 0)
        def _():
            send_block(
                a, s, src, UP if up else DOWN,
                shard=shard_of(at_z + 1 if up else at_z - 1, at_y, core),
            )

    def across(a, s, src):
        for dy in range(1, Y):
            send_block(a, s, src, ACROSS + dy - 1, shard=shard_of(at_z, turn(at_y, dy, Y), core))

    def gather_start(a):
        src = gathers[a][0].at[:, gathers[a][2]]
        along(a, me, src, True)
        along(a, me, src, False)
        across(a, me, src)
        to_core(a, me, src)

    def at_distance(distance, go):
        if distance == 0:
            go(at_z, None)
            return

        @pl.when(at_z >= distance)
        def _():
            go(at_z - distance, True)

        @pl.when(at_z + distance < Z)
        def _():
            go(at_z + distance, False)

    def gather_z(distance, *which):
        def go(z, up):
            s = shard_of(z, at_y, core)
            for a in which:
                wait_block(a, s)
                src = block_of(a, s)
                along(a, s, src, up)
                across(a, s, src)
                to_replica(a, s, src)
                to_core(a, s, src)

        at_distance(distance, go)

    def gather_y(distance, *which):
        def go(z, up):
            for dy in range(1, Y):
                s = shard_of(z, turn(at_y, dy, Y), core)
                for a in which:
                    wait_block(a, s)
                    to_replica(a, s, block_of(a, s))
                    to_core(a, s, block_of(a, s))

        at_distance(distance, go)

    def gather_lines(*which):
        for distance in range(1, Z):
            gather_z(distance, *which)
            gather_y(distance - 1, *which)
        gather_y(Z - 1, *which)

    def gather_x():
        for distance in range(Z):

            def go(z, up):
                for dy in range(Y):
                    if distance or dy:
                        s = shard_of(z, turn(at_y, dy, Y), core)
                        wait_block(FAR, s)
                        to_core(FAR, s, block_of(FAR, s))

            at_distance(distance, go)

    def gather_end(*which):
        for dz in range(Z):
            for dy in range(Y):
                for a in which:
                    wait_block(a, shard_of(turn(at_z, dz, Z), turn(at_y, dy, Y), other_core))

    gather_start(SMALL)
    gather_start(BOTH)
    gather_start(OWN)
    to_core(FAR, me, r_.w_in.at[:, far_lanes])
    for src, dst in ((r_.small, r_.smf), (r_.w_in, r_.wf_in), (r_.w_out, r_.wf_out)):
        dst[rows_of(me), :] = src[...]

    def gather_step(distance, *which):
        if distance < Z:
            gather_z(distance, *which)
        gather_y(distance - 1, *which)

    first = (SMALL, BOTH, OWN)

    def rows_start(buf, land, sems):
        land[me] = buf[me]

        def go(step, carry):
            peer = turn(me, step, S)
            copy_to(
                buf.at[peer], land.at[me], sems.at[0, step], sems.at[1, me], shard=peer
            ).start()
            return carry

        lax.fori_loop(1, S, go, 0)

    def rows_wait(buf, land, sems):
        def go(step, carry):
            src = turn(me, step, S)
            copy_to(
                buf.at[src], land.at[src], sems.at[0, step], sems.at[1, src], shard=src
            ).wait_recv()
            return carry

        lax.fori_loop(1, S, go, 0)

    def rows_drain(buf, land, sems):
        def go(step, carry):
            peer = turn(me, step, S)
            copy_to(
                buf.at[peer], land.at[me], sems.at[0, step], sems.at[1, me], shard=peer
            ).wait_send()
            return carry

        lax.fori_loop(1, S, go, 0)

    def replicas_copies(land, others, sems):
        return [
            copy_to(
                land, others.at[step - 1], sems.at[0, step], sems.at[1, step],
                replica=turn(mine, step, R),
            )
            for step in range(1, R)
        ]

    cotf, n1, n2, resid, gres = r_.cotf, r_.n1, r_.n2, r_.resid, r_.gres
    resid[T - T % 8 :, :] = jnp.zeros((TP - (T - T % 8), D), F32)
    cotf[T - T % 8 :, :] = jnp.zeros((TP - (T - T % 8), D), F32)
    resid[0:T, :] = r_.tok[...].astype(F32)
    cotf[0:T, :] = r_.cot[...].astype(F32)

    def normalise(rows):
        average = jnp.mean(rows, axis=-1, keepdims=True)
        centred = rows - average
        inv = lax.rsqrt(jnp.mean(centred * centred, axis=-1, keepdims=True) + EPS)
        return centred * inv, inv

    normed_one, inv_one = normalise(resid[...])
    n1[...] = normed_one

    gather_step(1, *first)

    pairs_at = r_.pairs_at
    pairs_at[...] = jnp.full(pairs_at.shape, C, F32)
    pairs_at[0:2, 0:T] = r_.ids[...].astype(F32)
    pairs_at[2:4, 0:T] = r_.slots[...].astype(F32)
    pair_columns = pairs_at[...].T[0:TP, :].astype(jnp.int32)
    ids_v, slots_v = pair_columns[:, 0:2], pair_columns[:, 2:4]
    columns = iota((TP, SB), 1)
    for k in range(2):
        base = jnp.where(
            slots_v[:, k : k + 1] < C, ids_v[:, k : k + 1] * BR + slots_v[:, k : k + 1], -4 * SB
        )
        for i in range(q):
            r_.place[k, i] = jnp.where(columns == base + i * CR, 1.0, 0.0).astype(BF16)

    gather_step(2, *first)
    slot_row = iota((N, SB), 0)
    slot_peer = lax.shift_right_logical(slot_row * (65536 // CR + 1), 16)
    slot_col = slot_peer * BR + (slot_row - slot_peer * CR)
    for i in range(q):
        r_.unroll[i] = jnp.where(iota((N, SB), 1) == slot_col + i * CR, 1.0, 0.0).astype(BF16)

    def pack_tokens(src, dst):
        acc = None
        for i in range(q):
            table = r_.place[0, i] + r_.place[1, i]
            term = dot_tn(table, src[:, i * LW : (i + 1) * LW])
            acc = term if acc is None else acc + term
        dst[...] = acc.astype(BF16).reshape(S, BR, LW)

    def unpack(land, dst):
        flat = land.reshape(SB, LW)
        for i in range(q):
            dst[:, i * LW : (i + 1) * LW] = dot(r_.unroll[i], flat).astype(BF16)

    def pack_slots(value, dst):
        acc = None
        for i in range(q):
            term = dot_tn(r_.unroll[i], value[:, i * LW : (i + 1) * LW])
            acc = term if acc is None else acc + term
        dst[...] = acc.astype(BF16).reshape(S, BR, LW)

    for distance in range(3, Z):
        gather_step(distance, *first)
    gather_start(OUT)
    r_.tmpb[...] = cotf[...].astype(BF16)
    pack_tokens(r_.tmpb, r_.cbuf)
    gather_step(Z, *first)
    rows_start(r_.cbuf, r_.cland, r_.c_sem)
    gather_x()
    gather_end(SMALL)
    r_.smt[...] = r_.smf[...].astype(F32).T
    smt = r_.smt

    def vector(i):
        return smt[E + i : E + i + 1, :]

    r_.act1[...] = (n1[...] * vector(0) + vector(1)).astype(BF16)
    bias = r_.bias
    bias[:, 0:D] = jnp.broadcast_to(vector(2), (8, D))
    bias[:, D : 2 * D] = jnp.zeros((8, D), F32)
    bias[:, 2 * D : 3 * D] = jnp.broadcast_to(vector(3), (8, D))
    gather_end(BOTH)

    WT = D

    def qkv_step(j, carry):
        cut = pl.ds(pl.multiple_of(j * WT, WT), WT)
        value = dot(r_.act1[...], r_.wf_in[:, cut]) + bias[0:1, cut]
        r_.qkv[:, cut] = value.astype(BF16)
        return carry

    lax.fori_loop(2 * D // WT, 3 * D // WT, qkv_step, 0)
    gather_step(1, OUT)
    gather_end(OWN, FAR)
    lax.fori_loop(0, 2 * D // WT, qkv_step, 0)
    gather_step(2, OUT)

    low = iota((TP, LANES), 1) < HDIM
    key_ok = iota((TP, TP), 1) < T
    scale = HDIM ** (-0.5)

    def halves(value):
        zero = jnp.zeros_like(value)
        return jnp.where(low, value, zero), jnp.where(low, zero, value)

    def pair_cuts(i):
        return [pl.ds(pl.multiple_of(i * LANES + off, LANES), LANES) for off in (0, D, 2 * D)]

    def attend(i, carry):
        cut_q, cut_k, cut_v = pair_cuts(i)
        keys, values = r_.qkv[:, cut_k], r_.qkv[:, cut_v]
        found = []
        for a, query in enumerate(halves(r_.qkv[:, cut_q])):
            scores = dot_nt(query, keys) * scale
            weight = jnp.where(key_ok, jnp.exp(scores), 0.0)
            probs = weight * (1.0 / jnp.sum(weight, axis=-1, keepdims=True))
            r_.probs[2 * i + a] = probs
            found.append(dot(probs.astype(BF16), values))
        r_.ctx[:, cut_q] = jnp.where(low, found[0], found[1]).astype(BF16)
        return carry

    pairs = HEADS // 2
    lax.fori_loop(0, pairs // 2, attend, 0)
    for distance in range(3, Z):
        gather_step(distance, OUT)
    lax.fori_loop(pairs // 2, pairs, attend, 0)
    gather_step(Z, OUT)
    gather_end(OUT)
    for j in range(D // WT):
        cut = slice(j * WT, (j + 1) * WT)
        resid[:, cut] += dot(r_.ctx[...], r_.wf_out[:, cut]) + vector(4)[:, cut]
    normed_two, inv_two = normalise(resid[...])
    n2[...] = normed_two
    r_.hid[...] = (normed_two * vector(5) + vector(6)).astype(BF16)
    pack_tokens(r_.hid, r_.hbuf)
    rows_start(r_.hbuf, r_.hland, r_.h_sem)
    rows_wait(r_.cbuf, r_.cland, r_.c_sem)
    cot_copies = replicas_copies(r_.cland, r_.coth, r_.cx_sem)
    for copy in cot_copies:
        copy.start()

    def gates_of(rows):
        logits = dot(rows, r_.smf[...])
        weight = jnp.where(iota(logits.shape, 1) < E, jnp.exp(logits), 0.0)
        return weight / jnp.sum(weight, axis=-1, keepdims=True)

    gates = gates_of(r_.hid[...])
    lanes = iota((TP, LANES), 1)
    pair_gate = [
        jnp.sum(jnp.where(lanes == ids_v[:, k : k + 1], gates, 0.0), axis=-1, keepdims=True)
        for k in range(2)
    ]

    FT = D
    load_up.wait()
    load_down.wait()
    up, down = r_.up, r_.down
    unpack(r_.cland[...], r_.yrow)

    def early(j, carry):
        cut = pl.ds(pl.multiple_of(j * FT, FT), FT)
        r_.ga[:, cut] = dot_nt(r_.yrow[...], down[cut, :]).astype(BF16)
        return carry

    lax.fori_loop(0, FF // FT, early, 0)

    rows_wait(r_.hbuf, r_.hland, r_.h_sem)
    hid_copies = replicas_copies(r_.hland, r_.hoth, r_.hx_sem)
    for copy in hid_copies:
        copy.start()
    unpack(r_.hland[...], r_.xrow)
    slot_lane = iota((N, LANES), 1)
    own_gates = gates_of(r_.xrow[...])
    own_gate = jnp.sum(jnp.where(slot_lane == me, own_gates, 0.0), axis=-1, keepdims=True)
    r_.gbrow[...] = (own_gate * r_.yrow[...].astype(F32)).astype(BF16)

    def gelu_kernel(pre):
        cumul = 0.5 * (1.0 + lax.erf(pre * SQRT_HALF))
        return pre * cumul, cumul + pre * jnp.exp(-0.5 * pre * pre) * INV_ROOT_TWO_PI

    r_.gacc[...] = jnp.zeros((N, D), F32)
    r_.ggate[...] = jnp.zeros((N, LANES), F32)
    r_.gatec[...] = jnp.broadcast_to(own_gate, (N, LANES))

    def middle(j, carry):
        cut = pl.ds(pl.multiple_of(j * FT, FT), FT)
        pre = dot(r_.xrow[...], up[:, cut]) + r_.upb[:, cut].astype(F32)
        act_val, slope = gelu_kernel(pre)
        grad_act = r_.ga[:, cut].astype(F32)
        r_.act[:, cut] = act_val.astype(BF16)
        grad_pre = (r_.gatec[:, 0:1] * grad_act * slope).astype(BF16)
        r_.gp[:, cut] = grad_pre
        r_.gacc[...] += dot_nt(grad_pre, up[:, cut])
        both = act_val * grad_act
        r_.ggate[...] += sum(both[:, f : f + LANES] for f in range(0, FT, LANES))
        return carry

    lax.fori_loop(0, FF // FT, middle, 0)
    gate_grad = jnp.sum(r_.ggate[...], axis=-1, keepdims=True) + jnp.sum(
        r_.yrow[...].astype(F32) * r_.downb[...].astype(F32), axis=-1, keepdims=True
    )
    picked = jnp.where(slot_lane == me, 1.0, 0.0)
    contrib = (own_gates * (picked - own_gate) * gate_grad).astype(BF16)
    r_.gacc[...] += dot_nt(contrib, r_.smf[...])
    rows_drain(r_.hbuf, r_.hland, r_.h_sem)
    pack_slots(r_.gacc[...].astype(BF16), r_.rbuf)
    rows_start(r_.rbuf, r_.rland, r_.r_sem)
    r_.rterm[...] = dot_tn(r_.xrow[...], contrib)

    for j in range(D // WT):
        cut = slice(j * WT, (j + 1) * WT)
        r_.gacc[:, cut] = dot(r_.act[...], down[:, cut]) + r_.downb[:, cut].astype(F32)
    rows_drain(r_.cbuf, r_.cland, r_.c_sem)
    pack_slots(r_.gacc[...].astype(BF16), r_.obuf)

    for copy in cot_copies + hid_copies:
        copy.wait_recv()
    unpack(r_.coth[0], r_.yo)
    unpack(r_.hoth[0], r_.xo)
    far_gates = gates_of(r_.xo[...])
    far_gate = jnp.sum(jnp.where(slot_lane == me, far_gates, 0.0), axis=-1, keepdims=True)
    r_.yo[...] = (far_gate * r_.yo[...].astype(F32)).astype(BF16)

    def far(j, carry):
        cut = pl.ds(pl.multiple_of(j * FT, FT), FT)
        whole = pl.ds(pl.multiple_of(mine * part + j * FT, LANES), FT)
        pre = dot(r_.xo[...], up[:, whole]) + r_.upb[:, whole].astype(F32)
        act_val, slope = gelu_kernel(pre)
        r_.act_o[:, cut] = act_val.astype(BF16)
        grad_act = dot_nt(r_.yo[...], down[whole, :])
        r_.gp_o[:, cut] = (grad_act * slope).astype(BF16)
        return carry

    lax.fori_loop(0, part // FT, far, 0)

    half = D // 2
    pieces = [(True, row, lane) for lane in range(0, part, D) for row in range(0, D, half)]
    pieces += [(False, row, 0) for row in range(0, part, half)]
    kept, depth = [], FF // D

    def weight_grads(count):
        for is_up, row, lane in pieces[len(kept) : len(kept) + count]:
            if is_up:
                there = pl.ds(pl.multiple_of(mine * part + lane, LANES), D)
                own_gp, far_gp = r_.gp[:, there], r_.gp_o[:, lane : lane + D]
                value = dot_tn(r_.xrow[:, row : row + half], own_gp)
                value = value + dot_tn(r_.xo[:, row : row + half], far_gp)
                dst = r_.o_up.at[row : row + half, lane : lane + D]
                if row == 0:
                    r_.o_upb[:, lane : lane + D] = jnp.sum(
                        own_gp.astype(F32), axis=0, keepdims=True
                    ) + jnp.sum(far_gp.astype(F32), axis=0, keepdims=True)
            else:
                there = pl.ds(pl.multiple_of(mine * part + row, LANES), half)
                value = dot_tn(r_.act[:, there], r_.gbrow[...])
                value = value + dot_tn(r_.act_o[:, row : row + half], r_.yo[...])
                dst = r_.o_down.at[row : row + half]
            at = len(kept)
            slot = r_.ga.at[0:half, at % depth * D : (at % depth + 1) * D]
            if at >= depth:
                kept[at - depth].wait()
            slot[...] = value.astype(BF16)
            copy = pltpu.make_async_copy(slot, dst, r_.keep_sem.at[at])
            copy.start()
            kept.append(copy)

    pending = []

    def launch(copies):
        for copy in copies:
            copy.start()
        pending.extend(copies)
        return copies

    def core_start(tag):
        own, from_core, _, _, _, sems = tag
        return launch(
            [
                copy_to(
                    own.at[other_core], from_core, sems.at[0], sems.at[1],
                    shard=shard_of(at_z, at_y, other_core),
                )
            ]
        )

    def y_start(tag, before):
        own, from_core, from_y, _, _, sems = tag
        for copy in before:
            copy.wait_recv()
        for y in range(Y):
            own[core, y] = (own[core, y].astype(F32) + from_core[y].astype(F32)).astype(BF16)
        return launch(
            [
                copy_to(
                    own.at[core, turn(at_y, dy, Y)], from_y.at[dy - 1], sems.at[2 * dy],
                    sems.at[2 * dy + 1], shard=shard_of(at_z, turn(at_y, dy, Y), core),
                )
                for dy in range(1, Y)
            ]
        )

    def z_start(tag, before):
        own, _, from_y, from_z, _, sems = tag
        for copy in before:
            copy.wait_recv()
        total = own[core, at_y].astype(F32)
        for dy in range(1, Y):
            total = total + from_y[dy - 1].astype(F32)
        own[core, at_y] = total.astype(BF16)
        base = 2 * Y
        return launch(
            [
                copy_to(
                    own.at[core, at_y, turn(at_z, dz, Z)], from_z.at[dz - 1], sems.at[base + 2 * dz - 2],
                    sems.at[base + 2 * dz - 1], shard=shard_of(turn(at_z, dz, Z), at_y, core),
                )
                for dz in range(1, Z)
            ]
        )

    def x_start(tag, before):
        own, _, _, from_z, from_x, sems = tag
        for copy in before:
            copy.wait_recv()
        total = own[core, at_y, at_z].astype(F32)
        for dz in range(1, Z):
            total = total + from_z[dz - 1].astype(F32)
        own[core, at_y, at_z] = total.astype(BF16)
        base = 2 * Y + 2 * Z - 2
        return launch(
            [
                copy_to(
                    own.at[core, at_y, at_z], from_x.at[dx - 1], sems.at[base + 2 * dx - 2],
                    sems.at[base + 2 * dx - 1], replica=turn(mine, dx, R),
                )
                for dx in range(1, R)
            ]
        )

    def finish(tag, before, out):
        own, _, _, _, from_x, _ = tag
        for copy in before:
            copy.wait_recv()
        total = own[core, at_y, at_z].astype(F32)
        for dx in range(1, R):
            total = total + from_x[dx - 1].astype(F32)
        out[...] = total

    def put_part(tag, lane_at, value):
        own = tag[0]
        wide = value.shape[1]
        low_value = value.astype(BF16)
        for z in range(Z):
            for y in range(Y):
                for c in range(2):
                    s = (z * Y + y) * 2 + c
                    own[c, y, z, :, lane_at : lane_at + wide] = low_value[s * K : (s + 1) * K, :]

    vecs = r_.vecs
    vecs[...] = jnp.zeros((LANES, D), F32)

    def put_vector(i, value):
        vecs[E + i : E + i + 1, :] = value

    rows_wait(r_.rbuf, r_.rland, r_.r_sem)
    rows_start(r_.obuf, r_.oland, r_.o_sem)
    flat_back = r_.rland[...].reshape(SB, LW)
    for i in range(q):
        r_.gn[:, i * LW : (i + 1) * LW] = dot(r_.place[0, i] + r_.place[1, i], flat_back)

    def norm_grad(grad_rows, normed, inv, gain, at_gain, at_bias):
        scaled = grad_rows * gain
        inner = (
            scaled
            - jnp.mean(scaled, axis=-1, keepdims=True)
            - normed * jnp.mean(scaled * normed, axis=-1, keepdims=True)
        )
        put_vector(at_gain, jnp.sum(grad_rows * normed, axis=0, keepdims=True))
        put_vector(at_bias, jnp.sum(grad_rows, axis=0, keepdims=True))
        return inner * inv

    gres[...] = cotf[...] + norm_grad(r_.gn[...], n2[...], inv_two, vector(5), 5, 6)
    put_vector(4, jnp.sum(gres[...], axis=0, keepdims=True))
    r_.tmpb[...] = gres[...].astype(BF16)
    for j in range(D // WT):
        cut = slice(j * WT, (j + 1) * WT)
        put_part(r_.rs_o, j * WT, dot_tn(r_.ctx[...], r_.tmpb[:, cut]))
    stage_o = core_start(r_.rs_o)
    for j in range(D // WT):
        cut = slice(j * WT, (j + 1) * WT)
        r_.gctx[:, cut] = dot_nt(r_.tmpb[...], r_.wf_out[cut, :]).astype(BF16)

    def attend_back(i, carry):
        cut_q, cut_k, cut_v = pair_cuts(i)
        query, keys, values = r_.qkv[:, cut_q], r_.qkv[:, cut_k], r_.qkv[:, cut_v]
        query_half, key_half, grad_half = halves(query), halves(keys), halves(r_.gctx[:, cut_q])
        grad_q = grad_k = grad_v = None
        for a in range(2):
            probs = r_.probs[2 * i + a]
            grad_probs = dot_nt(grad_half[a], values)
            inner = jnp.sum(probs * grad_probs, axis=-1, keepdims=True)
            grad_scores = (probs * (grad_probs - inner) * scale).astype(BF16)
            terms = (
                dot(grad_scores, key_half[a]),
                dot_tn(grad_scores, query_half[a]),
                dot_tn(probs.astype(BF16), grad_half[a]),
            )
            if a == 0:
                grad_q, grad_k, grad_v = terms
            else:
                grad_q, grad_k, grad_v = grad_q + terms[0], grad_k + terms[1], grad_v + terms[2]
        r_.gm[:, cut_q] = grad_q.astype(BF16)
        r_.gm[:, cut_k] = grad_k.astype(BF16)
        r_.gm[:, cut_v] = grad_v.astype(BF16)
        vecs[E + 2 : E + 3, cut_q] = jnp.sum(grad_q, axis=0, keepdims=True)
        vecs[E + 3 : E + 4, cut_q] = jnp.sum(grad_v, axis=0, keepdims=True)
        return carry

    lax.fori_loop(0, pairs, attend_back, 0)
    stage_o = y_start(r_.rs_o, stage_o)

    def proj_part(tag, at):
        wide = tag[0].shape[-1]
        step = WT if wide % WT == 0 else wide
        for j in range(0, wide, step):
            put_part(tag, j, dot_tn(r_.act1[...], r_.gm[:, at + j : at + j + step]))
        return core_start(tag)

    stage_v = proj_part(r_.rs_v, 2 * D)
    stage_k = proj_part(r_.rs_k, D)
    stage_o = z_start(r_.rs_o, stage_o)
    stage_v = y_start(r_.rs_v, stage_v)
    stage_q = proj_part(r_.rs_q, 0)
    stage_p = proj_part(r_.rs_p, D // 2)
    stage_k = y_start(r_.rs_k, stage_k)
    for j in range(D // WT):
        cut = slice(j * WT, (j + 1) * WT)
        r_.gn[:, cut] = dot_nt(r_.gm[...], r_.wf_in[cut, :])
    stage_q = y_start(r_.rs_q, stage_q)
    stage_p = y_start(r_.rs_p, stage_p)
    grad_tok = gres[...] + norm_grad(r_.gn[...], n1[...], inv_one, vector(0), 0, 1)
    r_.o_grad[...] = grad_tok[0:T].astype(BF16)
    put_part(r_.rs_s, 0, vecs[...].T + r_.rterm[...])
    stage_s = core_start(r_.rs_s)
    stage_o = x_start(r_.rs_o, stage_o)
    stage_v = z_start(r_.rs_v, stage_v)
    stage_s = y_start(r_.rs_s, stage_s)

    rows_wait(r_.obuf, r_.oland, r_.o_sem)
    flat_out = r_.oland[...].reshape(SB, LW)
    for i in range(q):
        cut = slice(i * LW, (i + 1) * LW)
        total = resid[:, cut]
        for k in range(2):
            total = total + pair_gate[k] * dot(r_.place[k, i], flat_out)
        r_.o_rows[:, cut] = total[0:T].astype(BF16)

    weight_grads(2)
    stage_k = z_start(r_.rs_k, stage_k)
    finish(r_.rs_o, stage_o, r_.o_out)
    weight_grads(2)
    stage_v = x_start(r_.rs_v, stage_v)
    weight_grads(1)
    stage_q = z_start(r_.rs_q, stage_q)
    stage_k = x_start(r_.rs_k, stage_k)
    finish(r_.rs_v, stage_v, r_.o_proj.at[:, 2 * D : 3 * D])
    weight_grads(len(pieces) - len(kept))
    stage_p = z_start(r_.rs_p, stage_p)
    stage_s = z_start(r_.rs_s, stage_s)
    total_grad = jnp.sum(r_.gbrow[...].astype(F32), axis=0, keepdims=True)
    total_grad = total_grad + jnp.sum(r_.yo[...].astype(F32), axis=0, keepdims=True)
    bias[0:1, 0:D] = total_grad
    r_.o_downb[...] = bias[0:1, pl.ds(pl.multiple_of(mine * (D // R), LANES), D // R)]
    stage_q = x_start(r_.rs_q, stage_q)
    stage_p = x_start(r_.rs_p, stage_p)
    stage_s = x_start(r_.rs_s, stage_s)
    finish(r_.rs_k, stage_k, r_.o_proj.at[:, D : 2 * D])
    finish(r_.rs_q, stage_q, r_.o_proj.at[:, 0 : D // 2])
    finish(r_.rs_p, stage_p, r_.o_proj.at[:, D // 2 : D])
    finish(r_.rs_s, stage_s, turned.at[0:K])
    r_.o_small[...] = turned[...].T[0 : r_.o_small.shape[0], 0:K]

    state.drain = True
    for a in (SMALL, BOTH, OWN, OUT):
        gather_start(a)
    to_core(FAR, me, r_.w_in.at[:, far_lanes])
    gather_lines(SMALL, BOTH, OWN, OUT)
    gather_x()
    rows_drain(r_.rbuf, r_.rland, r_.r_sem)
    rows_drain(r_.obuf, r_.oland, r_.o_sem)
    for copy in cot_copies + hid_copies + pending:
        copy.wait_send()
    for copy in kept[-depth:]:
        copy.wait()


def call_block(plan, *arrays):
    S, R, TP, FF, E = plan.S, plan.R, plan.TP, plan.FF, plan.E
    K, q, BR, LW, SB, N, Z, Y, part = (
        plan.K, plan.q, plan.BR, plan.LW, plan.SB, plan.N, plan.Z, plan.Y, plan.part,
    )
    vmem = pl.BlockSpec(memory_space=pltpu.VMEM)
    anyw = pl.BlockSpec(memory_space=pl.ANY)
    outs = dict(
        o_rows=((plan.T, D), BF16, vmem),
        o_grad=((plan.T, D), BF16, vmem),
        o_proj=((K, 3 * D), F32, vmem),
        o_out=((K, D), F32, vmem),
        o_small=((-(-(E + VECTORS) // 8) * 8, K), F32, vmem),
        o_up=((D, part), BF16, anyw),
        o_upb=((1, part), F32, vmem),
        o_down=((part, D), BF16, anyw),
        o_downb=((1, D // R), F32, vmem),
    )

    def landing(wide):
        return (
            pltpu.VMEM((2, Y, Z, K, wide), BF16),
            pltpu.VMEM((Y, Z, K, wide), BF16),
            pltpu.VMEM((max(Y - 1, 1), Z, K, wide), BF16),
            pltpu.VMEM((max(Z - 1, 1), K, wide), BF16),
            pltpu.VMEM((max(R - 1, 1), K, wide), BF16),
            pltpu.SemaphoreType.DMA((2 * (Y + Z + R),)),
        )

    def pairs_of(*extent):
        return pltpu.SemaphoreType.DMA(extent)

    rows = pltpu.VMEM((S, BR, LW), BF16)
    far_rows = pltpu.VMEM((R - 1, S, BR, LW), BF16)
    wide_rows = pltpu.VMEM((TP, D), F32)
    half_rows = pltpu.VMEM((TP, D), BF16)
    slot_rows = pltpu.VMEM((N, D), BF16)
    scratch = dict(
        up=pltpu.VMEM((D, FF), BF16),
        down=pltpu.VMEM((FF, D), BF16),
        wf_in=pltpu.VMEM((D, 3 * D), BF16),
        wf_out=pltpu.VMEM((D, D), BF16),
        smf=pltpu.VMEM((D, LANES), BF16),
        smt=pltpu.VMEM((LANES, D), F32),
        turned=pltpu.VMEM((LANES, LANES), F32),
        small=pltpu.VMEM((K, LANES), BF16),
        pairs_at=pltpu.VMEM((LANES, -(-TP // LANES) * LANES), F32),
        place=pltpu.VMEM((2, q, TP, SB), BF16),
        unroll=pltpu.VMEM((q, N, SB), BF16),
        cotf=wide_rows, n1=wide_rows, n2=wide_rows, resid=wide_rows, gres=wide_rows,
        gn=wide_rows,
        tmpb=half_rows, act1=half_rows, hid=half_rows, ctx=half_rows,
        bias=pltpu.VMEM((8, 3 * D), F32),
        qkv=pltpu.VMEM((TP, 3 * D), BF16),
        gm=pltpu.VMEM((TP, 3 * D), BF16),
        probs=pltpu.VMEM((HEADS, TP, TP), F32),
        cbuf=rows, cland=rows, hbuf=rows, hland=rows, rland=rows, oland=rows,
        coth=far_rows, hoth=far_rows,
        yrow=slot_rows, xrow=slot_rows, gbrow=slot_rows,
        xo=slot_rows,
        ga=pltpu.VMEM((N, FF), BF16),
        act=pltpu.VMEM((N, FF), BF16),
        gp=pltpu.VMEM((N, FF), BF16),
        act_o=pltpu.VMEM((N, part), BF16),
        gp_o=pltpu.VMEM((N, part), BF16),
        stage=pltpu.VMEM((1, N, D), F32),
        ggate=pltpu.VMEM((N, LANES), F32),
        gatec=pltpu.VMEM((N, LANES), F32),
        rterm=pltpu.VMEM((D, LANES), F32),
        vecs=pltpu.VMEM((LANES, D), F32),
        rs_o=landing(D), rs_v=landing(D), rs_k=landing(D), rs_q=landing(D // 2), rs_p=landing(D // 2), rs_s=landing(LANES),
        load_sem=pairs_of(2),
        ag_send=pairs_of(5, 3 + Y, S),
        ag_recv=pairs_of(5, S),
        c_sem=pairs_of(2, S),
        h_sem=pairs_of(2, S),
        r_sem=pairs_of(2, S),
        o_sem=pairs_of(2, S),
        cx_sem=pairs_of(2, R),
        hx_sem=pairs_of(2, R),
        keep_sem=pairs_of(2 * (part // D) + 2 * part // D),
    )
    return pl.pallas_call(
        functools.partial(block_kernel, plan, list(outs)),
        out_shape=[jax.ShapeDtypeStruct(o[0], o[1]) for o in outs.values()],
        in_specs=[vmem] * (9 + VECTORS) + [anyw] * 2,
        out_specs=[o[2] for o in outs.values()],
        scratch_shapes=scratch,
        compiler_params=pltpu.CompilerParams(
            collective_id=0, has_side_effects=True, vmem_limit_bytes=60 * 1024 * 1024
        ),
        cost_estimate=pl.CostEstimate(
            flops=12 * N * D * FF, bytes_accessed=4 * D * FF, transcendentals=2 * N * FF
        ),
    )(*arrays)


def outputs_kernel(plan, count, *refs):
    srcs, small, rest = refs[:count], refs[count], refs[count + 1 :]
    dsts, vectors, router = rest[:count], rest[count : count + VECTORS], rest[count + VECTORS]
    lands, wides, sems = rest[count + VECTORS + 1 : 2 * count + VECTORS + 1], rest[-3:-1], rest[-1]
    steps = []
    for n, (src, land, dst) in enumerate(zip(srcs, lands, dsts)):
        cuts = 6 if n < 2 else 1
        rows = src.shape[0] // cuts
        wide = wides[n] if n < 2 else land
        for cut in range(cuts):
            part = pl.ds(cut * rows, rows)
            at = len(steps)
            fetch = pltpu.make_async_copy(src.at[part], land.at[part], sems.at[0, at])
            fetch.start()
            store = pltpu.make_async_copy(wide.at[part], dst.at[part], sems.at[1, at])
            steps.append((fetch, land, wide, part, store))
    for i, vector in enumerate(vectors):
        vector[...] = small[plan.E + i : plan.E + i + 1, :].reshape(plan.K)
    router[...] = small[0 : plan.E, :]
    for fetch, land, wide, part, store in steps:
        fetch.wait()
        if wide is not land:
            wide[part, :] = land[part, :].astype(F32)
        store.start()
    for step in steps:
        step[-1].wait()


def call_outputs(plan, arrays, small):
    vmem = pl.BlockSpec(memory_space=pltpu.VMEM)
    anyw = pl.BlockSpec(memory_space=pl.ANY)
    count = len(arrays)
    return pl.pallas_call(
        functools.partial(outputs_kernel, plan, count),
        out_shape=[jax.ShapeDtypeStruct(a.shape, F32 if n < 2 else a.dtype) for n, a in enumerate(arrays)]
        + [jax.ShapeDtypeStruct((plan.K,), F32)] * VECTORS
        + [jax.ShapeDtypeStruct((plan.E, plan.K), F32)],
        in_specs=[anyw] * count + [vmem],
        out_specs=[anyw] * count + [vmem] * (VECTORS + 1),
        scratch_shapes=[pltpu.VMEM(a.shape, a.dtype) for a in arrays]
        + [pltpu.VMEM(a.shape, F32) for a in arrays[:2]]
        + [pltpu.SemaphoreType.DMA((2, 12 + count))],
        compiler_params=pltpu.CompilerParams(vmem_limit_bytes=60 * 1024 * 1024),
    )(*arrays, small)


def body(
    tokens, cotangent, norm1_gain, norm1_bias, proj_in, query_bias, value_bias, proj_out, out_bias,
    norm2_gain, norm2_bias, router, up_weight, up_bias, down_weight, down_bias, expert_ids, slot_ids,
):
    shards, replicas = lax.axis_size("shard"), lax.axis_size("replica")
    rows = tokens.shape[0] * tokens.shape[1]
    plan = Plan(shards, replicas, rows, up_weight.shape[2], up_weight.shape[0])
    if plan.part % D or plan.N < D // 2 or up_weight.shape[0] != 1 or tokens.shape[0] != 1:
        return plain_body(
            tokens, cotangent, norm1_gain, norm1_bias, proj_in, query_bias, value_bias, proj_out,
            out_bias, norm2_gain, norm2_bias, router, up_weight, up_bias, down_weight, down_bias,
            expert_ids, slot_ids,
        )
    (o_rows, o_grad, o_proj, o_out, o_small, o_up, o_upb, o_down, o_downb) = call_block(
        plan, tokens.reshape(rows, D), cotangent.reshape(rows, D), proj_in, proj_out, router.T,
        expert_ids.T, slot_ids.T, up_bias, down_bias, norm1_gain, norm1_bias, query_bias, value_bias,
        out_bias, norm2_gain, norm2_bias, up_weight[0], down_weight[0],
    )
    (o_up, o_down, o_rows, o_grad, o_proj, o_out, o_upb, o_downb, *vec, o_router) = call_outputs(
        plan, [o_up, o_down, o_rows, o_grad, o_proj, o_out, o_upb, o_downb], o_small
    )
    return (
        o_rows.reshape(tokens.shape),
        o_grad.reshape(tokens.shape),
        vec[0], vec[1], o_proj, vec[2], vec[3], o_out, vec[4], vec[5], vec[6], o_router.T,
        o_up[None], o_upb, o_down[None], o_downb,
    )


def fits_kernel(mesh):
    shards, replicas = mesh.shape["shard"], mesh.shape["replica"]
    return shards % 2 == 0 and D % shards == 0 and (D // shards) % 16 == 0 and replicas == 2


def solution(mesh):
    in_specs = (
        P(("replica", "shard"), None, None),
        P(("replica", "shard"), None, None),
        P("shard"),
        P("shard"),
        P("shard", None),
        P("shard"),
        P("shard"),
        P("shard", None),
        P("shard"),
        P("shard"),
        P("shard"),
        P("shard", None),
        P("shard", None, None),
        P("shard", None),
        P("shard", None, None),
        P("shard", None),
        P(("replica", "shard"), None),
        P(("replica", "shard"), None),
    )
    out_specs = (
        P(("replica", "shard"), None, None),
        P(("replica", "shard"), None, None),
        P("shard"),
        P("shard"),
        P("shard", None),
        P("shard"),
        P("shard"),
        P("shard", None),
        P("shard"),
        P("shard"),
        P("shard"),
        P("shard", None),
        P("shard", None, "replica"),
        P("shard", "replica"),
        P("shard", "replica", None),
        P("shard", "replica"),
    )
    chosen = body if fits_kernel(mesh) else plain_body
    return jax.shard_map(chosen, mesh=mesh, in_specs=in_specs, out_specs=out_specs, check_vma=False)
```

```python
import functools
from types import SimpleNamespace

import jax
import jax.numpy as jnp
from jax import lax
from jax.experimental import pallas as pl
from jax.experimental.pallas import tpu as pltpu
from jax.sharding import PartitionSpec as P

D = 768
HEADS = 12
HDIM = 64
SEQ = 197


EPS = 1e-06
SQRT_HALF = 0.7071067811865476
INV_ROOT_TWO_PI = 0.3989422804014327


def layer_norm(rows_in, norm_gain, norm_shift):
    average = jnp.mean(rows_in, axis=-1, keepdims=True)
    centred = rows_in - average
    inv_std = lax.rsqrt(jnp.mean(centred * centred, axis=-1, keepdims=True) + EPS)
    normed = centred * inv_std
    return (normed, inv_std, normed * norm_gain + norm_shift)


def norm_back(grad_rows, normed, inv_std, norm_gain):
    scaled = grad_rows * norm_gain
    inner = (
        scaled
        - jnp.mean(scaled, axis=-1, keepdims=True)
        - normed * jnp.mean(scaled * normed, axis=-1, keepdims=True)
    )
    return (inner * inv_std, jnp.sum(grad_rows * normed, axis=0), jnp.sum(grad_rows, axis=0))


def gelu_parts(pre_act):
    cumul = 0.5 * (1.0 + lax.erf(pre_act * SQRT_HALF))
    return (pre_act * cumul, cumul + pre_act * jnp.exp(-0.5 * pre_act * pre_act) * INV_ROOT_TWO_PI)


def route_table(expert_ids, slot_ids, experts, capacity):
    positions = jnp.arange(experts * capacity, dtype=jnp.int32)
    tables = []
    for choose in range(2):
        kept = slot_ids[:, choose] < capacity
        target = jnp.where(kept, expert_ids[:, choose] * capacity + slot_ids[:, choose], -1)
        tables.append((target[:, None] == positions[None, :]).astype(jnp.bfloat16))
    return tables


def pick_table(expert_ids, experts):
    labels = jnp.arange(experts, dtype=jnp.int32)
    return [
        (expert_ids[:, choose][:, None] == labels[None, :]).astype(jnp.float32)
        for choose in range(2)
    ]


def lane_pad(blocks):
    rows = blocks[0].shape[0]
    spare = -sum(block.shape[1] for block in blocks) % 128
    return jnp.concatenate(blocks + [jnp.zeros((rows, spare), blocks[0].dtype)], axis=1)


def other_replicas(value):
    size = lax.axis_size("replica")
    return [
        lax.ppermute(value, "replica", [(at, (at + step) % size) for at in range(size)])
        for step in range(1, size)
    ]


def to_expert(value, local_experts, capacity):
    shards, width = value.shape[0], value.shape[-1]
    return (
        value.reshape(shards, local_experts, capacity, width)
        .swapaxes(0, 1)
        .reshape(local_experts, shards * capacity, width)
    )


def from_expert(value, shards, capacity):
    local_experts, width = value.shape[0], value.shape[-1]
    return (
        value.reshape(local_experts, shards, capacity, width)
        .swapaxes(0, 1)
        .reshape(shards, local_experts * capacity, width)
    )


def expert_middle(rows, grad_rows, up_weight, up_bias, down_weight):
    expert_pre = (
        jnp.einsum("ecd,edf->ecf", rows, up_weight, preferred_element_type=jnp.float32)
        + up_bias.astype(jnp.float32)[:, None, :]
    )
    act_val, slope = gelu_parts(expert_pre)
    grad_active = jnp.einsum(
        "ecd,efd->ecf", grad_rows, down_weight, preferred_element_type=jnp.float32
    )
    return (act_val.astype(jnp.bfloat16), (grad_active * slope).astype(jnp.bfloat16))


def plain_body(
    tokens,
    cotangent,
    norm1_gain,
    norm1_bias,
    proj_in,
    query_bias,
    value_bias,
    proj_out,
    out_bias,
    norm2_gain,
    norm2_bias,
    router,
    up_weight,
    up_bias,
    down_weight,
    down_bias,
    expert_ids,
    slot_ids,
):
    images = tokens.shape[0]
    small = jnp.stack(
        [norm1_gain, norm1_bias, query_bias, value_bias, out_bias, norm2_gain, norm2_bias],
        axis=1,
    )
    width_in, width_small = proj_in.shape[1], small.shape[1] + router.shape[1]
    first = lax.all_gather(
        lane_pad([proj_in, proj_out, small, router]), "shard", axis=0, tiled=True
    )
    width_both = width_in + proj_out.shape[1]
    proj_full = first[:, :width_in]
    outproj_full = first[:, width_in:width_both]
    small_full = first[:, width_both : width_both + small.shape[1]]
    router_full = first[:, width_both + small.shape[1] : width_both + width_small]
    (
        gain_one,
        shift_one,
        query_shift,
        value_shift,
        out_shift,
        gain_two,
        shift_two,
    ) = [row for row in small_full.T]
    tok_rows = tokens.reshape(-1, D).astype(jnp.float32)
    normed_one, inv_one, pre_one = layer_norm(
        tok_rows, gain_one.astype(jnp.float32), shift_one.astype(jnp.float32)
    )
    act_one = pre_one.astype(jnp.bfloat16)
    mixed = jnp.dot(act_one, proj_full, preferred_element_type=jnp.float32)
    query_part = (mixed[:, :D] + query_shift.astype(jnp.float32)).astype(jnp.bfloat16)
    key_part = mixed[:, D : 2 * D].astype(jnp.bfloat16)
    value_part = (mixed[:, 2 * D :] + value_shift.astype(jnp.float32)).astype(jnp.bfloat16)
    query_heads = query_part.reshape(images, SEQ, HEADS, HDIM)
    key_heads = key_part.reshape(images, SEQ, HEADS, HDIM)
    value_heads = value_part.reshape(images, SEQ, HEADS, HDIM)
    scores = jnp.einsum(
        "ishd,ithd->ihst", query_heads, key_heads, preferred_element_type=jnp.float32
    ) * HDIM ** (-0.5)
    log_total = jnp.log(jnp.sum(jnp.exp(scores), axis=-1))
    attn_probs = jnp.exp(scores - log_total[..., None]).astype(jnp.bfloat16)
    context = (
        jnp.einsum("ihst,ithd->ishd", attn_probs, value_heads, preferred_element_type=jnp.float32)
        .reshape(-1, D)
        .astype(jnp.bfloat16)
    )
    resid = (
        tok_rows
        + jnp.dot(context, outproj_full, preferred_element_type=jnp.float32)
        + out_shift.astype(jnp.float32)
    )
    normed_two, inv_two, pre_two = layer_norm(
        resid, gain_two.astype(jnp.float32), shift_two.astype(jnp.float32)
    )
    hidden = pre_two.astype(jnp.bfloat16)
    logits = jnp.dot(hidden, router_full, preferred_element_type=jnp.float32)
    exp_logits = jnp.exp(logits)
    gate_probs = exp_logits / jnp.sum(exp_logits, axis=-1, keepdims=True)
    local_experts = up_weight.shape[0]
    experts = local_experts * lax.axis_size("shard")
    capacity = 2 * tok_rows.shape[0] // experts
    routes = route_table(expert_ids, slot_ids, experts, capacity)
    picks = pick_table(expert_ids, experts)
    both = jnp.concatenate(routes, axis=0)
    either = routes[0] + routes[1]
    gate_pair = [jnp.sum(gate_probs * pick, axis=-1) for pick in picks]
    grad_out = cotangent.reshape(-1, D).astype(jnp.float32)
    sent = jnp.concatenate(
        [(gate[:, None] * grad_out).astype(jnp.bfloat16) for gate in gate_pair], axis=0
    )
    buffer = jnp.dot(either.T, hidden, preferred_element_type=jnp.float32)
    grad_buffer = jnp.dot(both.T, sent, preferred_element_type=jnp.float32)
    shards = lax.axis_size("shard")
    outgoing = (
        jnp.concatenate([buffer, grad_buffer], axis=1)
        .astype(jnp.bfloat16)
        .reshape(shards, local_experts * capacity, 2 * D)
    )
    landed = to_expert(
        lax.all_to_all(outgoing, "shard", split_axis=0, concat_axis=0, tiled=True),
        local_experts,
        capacity,
    )
    arrived, grad_arrived = landed[..., :D], landed[..., D:]
    others = other_replicas(landed)
    active, grad_pre = expert_middle(arrived, grad_arrived, up_weight, up_bias, down_weight)
    expert_out = (
        jnp.einsum("ecf,efd->ecd", active, down_weight, preferred_element_type=jnp.float32)
        + down_bias.astype(jnp.float32)[:, None, :]
    ).astype(jnp.bfloat16)
    grad_in = jnp.einsum(
        "ecf,edf->ecd", grad_pre, up_weight, preferred_element_type=jnp.float32
    ).astype(jnp.bfloat16)
    answer = from_expert(jnp.concatenate([expert_out, grad_in], axis=2), shards, capacity)
    back = lax.all_to_all(answer, "shard", split_axis=0, concat_axis=0, tiled=True).reshape(
        experts * capacity, 2 * D
    )
    returned, grad_back = back[:, :D], back[:, D:]

    replicas = lax.axis_size("replica")
    ours = lax.axis_index("replica")
    part = up_weight.shape[2] // replicas
    up_part = lax.dynamic_slice_in_dim(up_weight, ours * part, part, axis=2)
    up_bias_part = lax.dynamic_slice_in_dim(up_bias, ours * part, part, axis=1)
    down_part = lax.dynamic_slice_in_dim(down_weight, ours * part, part, axis=1)
    active_parts = [lax.dynamic_slice_in_dim(active, ours * part, part, axis=2)]
    grad_pre_parts = [lax.dynamic_slice_in_dim(grad_pre, ours * part, part, axis=2)]
    for other in others:
        other_active, other_pre = expert_middle(
            other[..., :D], other[..., D:], up_part, up_bias_part, down_part
        )
        active_parts.append(other_active)
        grad_pre_parts.append(other_pre)
    all_rows = jnp.concatenate([landed] + others, axis=1)
    all_active = jnp.concatenate(active_parts, axis=1)
    all_pre = jnp.concatenate(grad_pre_parts, axis=1)
    width_part = D // replicas
    expert_grads = (
        jnp.einsum("ecd,ecf->edf", all_rows[..., :D], all_pre, preferred_element_type=jnp.float32),
        jnp.sum(all_pre, axis=1, dtype=jnp.float32),
        jnp.einsum(
            "ecf,ecd->efd", all_active, all_rows[..., D:], preferred_element_type=jnp.float32
        ),
        lax.dynamic_slice_in_dim(
            jnp.sum(all_rows[..., D:], axis=1, dtype=jnp.float32),
            ours * width_part,
            width_part,
            axis=1,
        ),
    )

    rows_here = tok_rows.shape[0]
    gathered_both = jnp.dot(both, returned, preferred_element_type=jnp.float32)
    gathered_pair = [gathered_both[:rows_here], gathered_both[rows_here:]]
    moe_sum = gate_pair[0][:, None] * gathered_pair[0] + gate_pair[1][:, None] * gathered_pair[1]
    block_out = (resid + moe_sum).astype(jnp.bfloat16).reshape(tokens.shape)
    grad_gate = [jnp.sum(grad_out * part_k, axis=-1) for part_k in gathered_pair]
    back_gain_one, back_proj, back_outproj, back_gain_two, back_router = (
        gain_one,
        proj_full,
        outproj_full,
        gain_two,
        router_full,
    )
    grad_moe = jnp.dot(either, grad_back, preferred_element_type=jnp.float32)
    grad_gates = picks[0] * grad_gate[0][:, None] + picks[1] * grad_gate[1][:, None]
    grad_logits = (
        gate_probs * (grad_gates - jnp.sum(gate_probs * grad_gates, axis=-1, keepdims=True))
    ).astype(jnp.bfloat16)
    router_term = jnp.dot(hidden.T, grad_logits, preferred_element_type=jnp.float32)
    grad_norm_two = grad_moe + jnp.dot(
        grad_logits, back_router.T, preferred_element_type=jnp.float32
    )
    grad_resid_two, gain_two_term, shift_two_term = norm_back(
        grad_norm_two, normed_two, inv_two, back_gain_two.astype(jnp.float32)
    )
    grad_resid = grad_out + grad_resid_two
    resid_bf = grad_resid.astype(jnp.bfloat16)
    out_shift_term = jnp.sum(grad_resid, axis=0)
    outproj_term = jnp.dot(context.T, resid_bf, preferred_element_type=jnp.float32)
    grad_context = (
        jnp.dot(resid_bf, back_outproj.T, preferred_element_type=jnp.float32)
        .astype(jnp.bfloat16)
        .reshape(images, SEQ, HEADS, HDIM)
    )
    scores_again = jnp.einsum(
        "ishd,ithd->ihst", query_heads, key_heads, preferred_element_type=jnp.float32
    ) * HDIM ** (-0.5)
    probs_full = jnp.exp(scores_again - log_total[..., None])
    grad_probs = jnp.einsum(
        "ishd,ithd->ihst", grad_context, value_heads, preferred_element_type=jnp.float32
    )
    grad_scores = (
        probs_full
        * (grad_probs - jnp.sum(probs_full * grad_probs, axis=-1, keepdims=True))
        * HDIM ** (-0.5)
    ).astype(jnp.bfloat16)
    probs_bf = probs_full.astype(jnp.bfloat16)
    grad_value = jnp.einsum(
        "ihst,ishd->ithd", probs_bf, grad_context, preferred_element_type=jnp.float32
    ).reshape(-1, D)
    grad_query = jnp.einsum(
        "ihst,ithd->ishd", grad_scores, key_heads, preferred_element_type=jnp.float32
    ).reshape(-1, D)
    grad_key = jnp.einsum(
        "ihst,ishd->ithd", grad_scores, query_heads, preferred_element_type=jnp.float32
    ).reshape(-1, D)
    grad_mixed = jnp.concatenate([grad_query, grad_key, grad_value], axis=1).astype(jnp.bfloat16)
    proj_term = jnp.dot(act_one.T, grad_mixed, preferred_element_type=jnp.float32)
    grad_act = jnp.dot(grad_mixed, back_proj.T, preferred_element_type=jnp.float32)
    grad_tok_norm, gain_one_term, shift_one_term = norm_back(
        grad_act, normed_one, inv_one, back_gain_one.astype(jnp.float32)
    )
    tokens_grad = (grad_resid + grad_tok_norm).astype(jnp.bfloat16).reshape(tokens.shape)
    query_shift_term = jnp.sum(grad_query, axis=0)
    value_shift_term = jnp.sum(grad_value, axis=0)
    column_sums = [
        gain_one_term,
        shift_one_term,
        query_shift_term,
        value_shift_term,
        out_shift_term,
        gain_two_term,
        shift_two_term,
    ]
    summed = lax.psum_scatter(
        lane_pad(
            [
                proj_term.astype(jnp.bfloat16),
                outproj_term.astype(jnp.bfloat16),
                lax.optimization_barrier(
                    lane_pad(
                        [
                            jnp.stack(column_sums, axis=0).astype(jnp.bfloat16).T,
                            router_term.astype(jnp.bfloat16),
                        ]
                    )
                ),
            ]
        ),
        "shard",
        scatter_dimension=0,
        tiled=True,
    )
    total = summed.astype(jnp.float32)
    for other in other_replicas(summed):
        total = total + other.astype(jnp.float32)
    small_total = total[:, width_both:]
    columns = len(column_sums)
    dense_grads = (
        small_total[:, 0],
        small_total[:, 1],
        total[:, :width_in],
        small_total[:, 2],
        small_total[:, 3],
        total[:, width_in:width_both],
        small_total[:, 4],
        small_total[:, 5],
        small_total[:, 6],
        small_total[:, columns : columns + experts],
    )
    return (
        block_out,
        tokens_grad,
        dense_grads[0],
        dense_grads[1],
        dense_grads[2],
        dense_grads[3],
        dense_grads[4],
        dense_grads[5],
        dense_grads[6],
        dense_grads[7],
        dense_grads[8],
        dense_grads[9],
        expert_grads[0],
        expert_grads[1],
        expert_grads[2],
        expert_grads[3],
    )


F32 = jnp.float32
BF16 = jnp.bfloat16
LANES = 128
VECTORS = 7


def dot(left, right):
    return jnp.dot(left, right, preferred_element_type=F32)


def dot_nt(left, right):
    return lax.dot_general(left, right, (((1,), (1,)), ((), ())), preferred_element_type=F32)


def dot_tn(left, right):
    return lax.dot_general(left, right, (((0,), (0,)), ((), ())), preferred_element_type=F32)


def iota(shape, axis):
    return lax.broadcasted_iota(jnp.int32, shape, axis)


class Plan:
    def __init__(self, shards, replicas, rows, hidden_units, local_experts):
        self.S, self.R, self.T, self.FF = shards, replicas, rows, hidden_units
        self.E = local_experts * shards
        self.C = 2 * rows // self.E
        self.TP = -(-rows // 16) * 16
        self.K = D // shards
        self.q = 2 if self.C % 16 and (2 * self.C) % 16 == 0 else 1
        self.CR = self.C if self.q == 2 else -(-self.C // 16) * 16
        self.BR = self.CR * self.q
        self.LW = D // self.q
        self.SB = shards * self.BR
        self.N = shards * self.CR
        self.part = hidden_units // replicas
        self.core = 2
        chips = shards // 2
        self.Z = 4 if chips % 4 == 0 else chips
        self.Y = chips // self.Z


def block_kernel(
    plan, out_names, tok, cot, w_in, w_out, router, ids, slots, upb, downb, *refs, **scratch
):
    vectors, (up_h, down_h), refs = refs[:VECTORS], refs[VECTORS : VECTORS + 2], refs[VECTORS + 2 :]
    r_ = SimpleNamespace(
        tok=tok, cot=cot, w_in=w_in, w_out=w_out, ids=ids, slots=slots, upb=upb,
        downb=downb, up_h=up_h, down_h=down_h, **dict(zip(out_names, refs)), **scratch,
    )
    r_.rbuf, r_.obuf, r_.gctx, r_.yo, r_.gacc = r_.hbuf, r_.cbuf, r_.hid, r_.yrow, r_.stage.at[0]
    S, R, T, TP, FF, E, C = plan.S, plan.R, plan.T, plan.TP, plan.FF, plan.E, plan.C
    K, q, CR, BR, LW, SB, N, Z, Y = (
        plan.K, plan.q, plan.CR, plan.BR, plan.LW, plan.SB, plan.N, plan.Z, plan.Y,
    )
    part = plan.part
    me = lax.axis_index("shard")
    mine = lax.axis_index("replica")
    core = lax.rem(me, 2)
    at_y = lax.rem(lax.div(me, 2), Y)
    at_z = lax.div(me, 2 * Y)
    other_core = 1 - core

    def shard_of(z, y, c):
        return (z * Y + y) * 2 + c

    def turn(base, step, size):
        return lax.rem(base + step, size)

    def copy_to(src, dst, send, recv, **device):
        return pltpu.make_async_remote_copy(
            src_ref=src, dst_ref=dst, send_sem=send, recv_sem=recv,
            device_id=device, device_id_type=pl.DeviceIdType.MESH,
        )

    load_up = pltpu.make_async_copy(r_.up_h, r_.up, r_.load_sem.at[0])
    load_down = pltpu.make_async_copy(r_.down_h, r_.down, r_.load_sem.at[1])
    load_up.start()
    load_down.start()

    turned = r_.turned
    turned[...] = jnp.zeros((LANES, LANES), F32)
    turned[0:E, 0:K] = router[...].astype(F32)
    for i, vector_ref in enumerate(vectors):
        turned[E + i : E + i + 1, 0:K] = vector_ref[...].astype(F32).reshape(1, K)
    r_.small[...] = turned[...].T[0:K, :].astype(BF16)

    barrier = pltpu.get_barrier_semaphore()
    for step in range(1, S):
        pl.semaphore_signal(
            barrier, inc=1, device_id={"shard": turn(me, step, S)}, device_id_type=pl.DeviceIdType.MESH
        )
    for step in range(1, R):
        pl.semaphore_signal(
            barrier, inc=1, device_id={"replica": turn(mine, step, R)}, device_id_type=pl.DeviceIdType.MESH
        )
    pl.semaphore_wait(barrier, S - 1 + R - 1)

    both_lanes, own_lanes = pl.ds(2 * D, D), pl.ds(pl.multiple_of(mine * D, LANES), D)
    far_lanes = pl.ds(pl.multiple_of((1 - mine) * D, LANES), D)
    every = slice(None)
    SMALL, BOTH, OWN, FAR, OUT = range(5)
    gathers = [
        (r_.small, r_.smf, every),
        (r_.w_in, r_.wf_in, both_lanes),
        (r_.w_in, r_.wf_in, own_lanes),
        (r_.w_in, r_.wf_in, far_lanes),
        (r_.w_out, r_.wf_out, every),
    ]
    UP, DOWN, CORE, REPLICA, ACROSS = range(5)
    state = SimpleNamespace(drain=False)

    def rows_of(s):
        return pl.ds(pl.multiple_of(s * K, 16), K)

    def block_of(a, s):
        return gathers[a][1].at[rows_of(s), gathers[a][2]]

    def send_block(a, s, src, way, lands=None, **device):
        copy = copy_to(
            src, block_of(a, s), r_.ag_send.at[a, way, s],
            r_.ag_recv.at[a if lands is None else lands, s], **device,
        )
        if state.drain:
            copy.wait_send()
        else:
            copy.start()

    def wait_block(a, s):
        if not state.drain:
            copy_to(
                block_of(a, s), block_of(a, s), r_.ag_send.at[a, CORE, s], r_.ag_recv.at[a, s],
                shard=s,
            ).wait_recv()

    def to_core(a, s, src):
        send_block(a, s, src, CORE, shard=shard_of(at_z, at_y, other_core))

    def to_replica(a, s, src):
        if a == OWN:
            send_block(OWN, s, src, REPLICA, lands=FAR, replica=1 - mine)

    def along(a, s, src, up):
        @pl.when(at_z < Z - 1 if up else at_z > 0)
        def _():
            send_block(
                a, s, src, UP if up else DOWN,
                shard=shard_of(at_z + 1 if up else at_z - 1, at_y, core),
            )

    def across(a, s, src):
        for dy in range(1, Y):
            send_block(a, s, src, ACROSS + dy - 1, shard=shard_of(at_z, turn(at_y, dy, Y), core))

    def gather_start(a):
        src = gathers[a][0].at[:, gathers[a][2]]
        along(a, me, src, True)
        along(a, me, src, False)
        across(a, me, src)
        to_core(a, me, src)

    def at_distance(distance, go):
        if distance == 0:
            go(at_z, None)
            return

        @pl.when(at_z >= distance)
        def _():
            go(at_z - distance, True)

        @pl.when(at_z + distance < Z)
        def _():
            go(at_z + distance, False)

    def gather_z(distance, *which):
        def go(z, up):
            s = shard_of(z, at_y, core)
            for a in which:
                wait_block(a, s)
                src = block_of(a, s)
                along(a, s, src, up)
                across(a, s, src)
                to_replica(a, s, src)
                to_core(a, s, src)

        at_distance(distance, go)

    def gather_y(distance, *which):
        def go(z, up):
            for dy in range(1, Y):
                s = shard_of(z, turn(at_y, dy, Y), core)
                for a in which:
                    wait_block(a, s)
                    to_replica(a, s, block_of(a, s))
                    to_core(a, s, block_of(a, s))

        at_distance(distance, go)

    def gather_lines(*which):
        for distance in range(1, Z):
            gather_z(distance, *which)
            gather_y(distance - 1, *which)
        gather_y(Z - 1, *which)

    def gather_x():
        for distance in range(Z):

            def go(z, up):
                for dy in range(Y):
                    if distance or dy:
                        s = shard_of(z, turn(at_y, dy, Y), core)
                        wait_block(FAR, s)
                        to_core(FAR, s, block_of(FAR, s))

            at_distance(distance, go)

    def gather_end(*which):
        for dz in range(Z):
            for dy in range(Y):
                for a in which:
                    wait_block(a, shard_of(turn(at_z, dz, Z), turn(at_y, dy, Y), other_core))

    gather_start(SMALL)
    gather_start(BOTH)
    gather_start(OWN)
    to_core(FAR, me, r_.w_in.at[:, far_lanes])
    for src, dst in ((r_.small, r_.smf), (r_.w_in, r_.wf_in), (r_.w_out, r_.wf_out)):
        dst[rows_of(me), :] = src[...]

    def gather_step(distance, *which):
        if distance < Z:
            gather_z(distance, *which)
        gather_y(distance - 1, *which)

    first = (SMALL, BOTH, OWN)

    def rows_start(buf, land, sems):
        land[me] = buf[me]

        def go(step, carry):
            peer = turn(me, step, S)
            copy_to(
                buf.at[peer], land.at[me], sems.at[0, step], sems.at[1, me], shard=peer
            ).start()
            return carry

        lax.fori_loop(1, S, go, 0)

    def rows_wait(buf, land, sems):
        def go(step, carry):
            src = turn(me, step, S)
            copy_to(
                buf.at[src], land.at[src], sems.at[0, step], sems.at[1, src], shard=src
            ).wait_recv()
            return carry

        lax.fori_loop(1, S, go, 0)

    def rows_drain(buf, land, sems):
        def go(step, carry):
            peer = turn(me, step, S)
            copy_to(
                buf.at[peer], land.at[me], sems.at[0, step], sems.at[1, me], shard=peer
            ).wait_send()
            return carry

        lax.fori_loop(1, S, go, 0)

    def replicas_copies(land, others, sems):
        return [
            copy_to(
                land, others.at[step - 1], sems.at[0, step], sems.at[1, step],
                replica=turn(mine, step, R),
            )
            for step in range(1, R)
        ]

    cotf, n1, n2, resid, gres = r_.cotf, r_.n1, r_.n2, r_.resid, r_.gres
    resid[T - T % 8 :, :] = jnp.zeros((TP - (T - T % 8), D), F32)
    cotf[T - T % 8 :, :] = jnp.zeros((TP - (T - T % 8), D), F32)
    resid[0:T, :] = r_.tok[...].astype(F32)
    cotf[0:T, :] = r_.cot[...].astype(F32)

    def normalise(rows):
        average = jnp.mean(rows, axis=-1, keepdims=True)
        centred = rows - average
        inv = lax.rsqrt(jnp.mean(centred * centred, axis=-1, keepdims=True) + EPS)
        return centred * inv, inv

    normed_one, inv_one = normalise(resid[...])
    n1[...] = normed_one

    gather_step(1, *first)

    pairs_at = r_.pairs_at
    pairs_at[...] = jnp.full(pairs_at.shape, C, F32)
    pairs_at[0:2, 0:T] = r_.ids[...].astype(F32)
    pairs_at[2:4, 0:T] = r_.slots[...].astype(F32)
    pair_columns = pairs_at[...].T[0:TP, :].astype(jnp.int32)
    ids_v, slots_v = pair_columns[:, 0:2], pair_columns[:, 2:4]
    columns = iota((TP, SB), 1)
    for k in range(2):
        base = jnp.where(
            slots_v[:, k : k + 1] < C, ids_v[:, k : k + 1] * BR + slots_v[:, k : k + 1], -4 * SB
        )
        for i in range(q):
            r_.place[k, i] = jnp.where(columns == base + i * CR, 1.0, 0.0).astype(BF16)

    gather_step(2, *first)
    slot_row = iota((N, SB), 0)
    slot_peer = lax.shift_right_logical(slot_row * (65536 // CR + 1), 16)
    slot_col = slot_peer * BR + (slot_row - slot_peer * CR)
    for i in range(q):
        r_.unroll[i] = jnp.where(iota((N, SB), 1) == slot_col + i * CR, 1.0, 0.0).astype(BF16)

    def pack_tokens(src, dst):
        acc = None
        for i in range(q):
            table = r_.place[0, i] + r_.place[1, i]
            term = dot_tn(table, src[:, i * LW : (i + 1) * LW])
            acc = term if acc is None else acc + term
        dst[...] = acc.astype(BF16).reshape(S, BR, LW)

    def unpack(land, dst):
        flat = land.reshape(SB, LW)
        for i in range(q):
            dst[:, i * LW : (i + 1) * LW] = dot(r_.unroll[i], flat).astype(BF16)

    def pack_slots(value, dst):
        acc = None
        for i in range(q):
            term = dot_tn(r_.unroll[i], value[:, i * LW : (i + 1) * LW])
            acc = term if acc is None else acc + term
        dst[...] = acc.astype(BF16).reshape(S, BR, LW)

    for distance in range(3, Z):
        gather_step(distance, *first)
    gather_start(OUT)
    r_.tmpb[...] = cotf[...].astype(BF16)
    pack_tokens(r_.tmpb, r_.cbuf)
    gather_step(Z, *first)
    rows_start(r_.cbuf, r_.cland, r_.c_sem)
    gather_x()
    gather_end(SMALL)
    r_.smt[...] = r_.smf[...].astype(F32).T
    smt = r_.smt

    def vector(i):
        return smt[E + i : E + i + 1, :]

    r_.act1[...] = (n1[...] * vector(0) + vector(1)).astype(BF16)
    bias = r_.bias
    bias[:, 0:D] = jnp.broadcast_to(vector(2), (8, D))
    bias[:, D : 2 * D] = jnp.zeros((8, D), F32)
    bias[:, 2 * D : 3 * D] = jnp.broadcast_to(vector(3), (8, D))
    gather_end(BOTH)

    WT = D

    def qkv_step(j, carry):
        cut = pl.ds(pl.multiple_of(j * WT, WT), WT)
        value = dot(r_.act1[...], r_.wf_in[:, cut]) + bias[0:1, cut]
        r_.qkv[:, cut] = value.astype(BF16)
        return carry

    lax.fori_loop(2 * D // WT, 3 * D // WT, qkv_step, 0)
    gather_step(1, OUT)
    gather_end(OWN, FAR)
    lax.fori_loop(0, 2 * D // WT, qkv_step, 0)
    gather_step(2, OUT)

    low = iota((TP, LANES), 1) < HDIM
    key_ok = iota((TP, TP), 1) < T
    scale = HDIM ** (-0.5)

    def halves(value):
        zero = jnp.zeros_like(value)
        return jnp.where(low, value, zero), jnp.where(low, zero, value)

    def pair_cuts(i):
        return [pl.ds(pl.multiple_of(i * LANES + off, LANES), LANES) for off in (0, D, 2 * D)]

    def attend(i, carry):
        cut_q, cut_k, cut_v = pair_cuts(i)
        keys, values = r_.qkv[:, cut_k], r_.qkv[:, cut_v]
        found = []
        for a, query in enumerate(halves(r_.qkv[:, cut_q])):
            scores = dot_nt(query, keys) * scale
            weight = jnp.where(key_ok, jnp.exp(scores), 0.0)
            probs = weight * (1.0 / jnp.sum(weight, axis=-1, keepdims=True))
            r_.probs[2 * i + a] = probs
            found.append(dot(probs.astype(BF16), values))
        r_.ctx[:, cut_q] = jnp.where(low, found[0], found[1]).astype(BF16)
        return carry

    pairs = HEADS // 2
    lax.fori_loop(0, pairs // 2, attend, 0)
    for distance in range(3, Z):
        gather_step(distance, OUT)
    lax.fori_loop(pairs // 2, pairs, attend, 0)
    gather_step(Z, OUT)
    gather_end(OUT)
    for j in range(D // WT):
        cut = slice(j * WT, (j + 1) * WT)
        resid[:, cut] += dot(r_.ctx[...], r_.wf_out[:, cut]) + vector(4)[:, cut]
    normed_two, inv_two = normalise(resid[...])
    n2[...] = normed_two
    r_.hid[...] = (normed_two * vector(5) + vector(6)).astype(BF16)
    pack_tokens(r_.hid, r_.hbuf)
    rows_start(r_.hbuf, r_.hland, r_.h_sem)
    rows_wait(r_.cbuf, r_.cland, r_.c_sem)
    cot_copies = replicas_copies(r_.cland, r_.coth, r_.cx_sem)
    for copy in cot_copies:
        copy.start()

    def gates_of(rows):
        logits = dot(rows, r_.smf[...])
        weight = jnp.where(iota(logits.shape, 1) < E, jnp.exp(logits), 0.0)
        return weight / jnp.sum(weight, axis=-1, keepdims=True)

    gates = gates_of(r_.hid[...])
    lanes = iota((TP, LANES), 1)
    pair_gate = [
        jnp.sum(jnp.where(lanes == ids_v[:, k : k + 1], gates, 0.0), axis=-1, keepdims=True)
        for k in range(2)
    ]

    FT = D
    load_up.wait()
    load_down.wait()
    up, down = r_.up, r_.down
    unpack(r_.cland[...], r_.yrow)

    def early(j, carry):
        cut = pl.ds(pl.multiple_of(j * FT, FT), FT)
        r_.ga[:, cut] = dot_nt(r_.yrow[...], down[cut, :]).astype(BF16)
        return carry

    lax.fori_loop(0, FF // FT, early, 0)

    state.drain = True
    for a in (SMALL, BOTH, OWN, OUT):
        gather_start(a)
    to_core(FAR, me, r_.w_in.at[:, far_lanes])
    gather_lines(SMALL, BOTH, OWN, OUT)
    gather_x()
    rows_drain(r_.cbuf, r_.cland, r_.c_sem)
    rows_wait(r_.hbuf, r_.hland, r_.h_sem)
    hid_copies = replicas_copies(r_.hland, r_.hoth, r_.hx_sem)
    for copy in hid_copies:
        copy.start()
    unpack(r_.hland[...], r_.xrow)
    slot_lane = iota((N, LANES), 1)
    own_gates = gates_of(r_.xrow[...])
    own_gate = jnp.sum(jnp.where(slot_lane == me, own_gates, 0.0), axis=-1, keepdims=True)
    r_.gbrow[...] = (own_gate * r_.yrow[...].astype(F32)).astype(BF16)

    def gelu_kernel(pre):
        cumul = 0.5 * (1.0 + lax.erf(pre * SQRT_HALF))
        return pre * cumul, cumul + pre * jnp.exp(-0.5 * pre * pre) * INV_ROOT_TWO_PI

    r_.gacc[...] = jnp.zeros((N, D), F32)
    r_.ggate[...] = jnp.zeros((N, LANES), F32)
    r_.gatec[...] = jnp.broadcast_to(own_gate, (N, LANES))

    def middle(j, carry):
        cut = pl.ds(pl.multiple_of(j * FT, FT), FT)
        pre = dot(r_.xrow[...], up[:, cut]) + r_.upb[:, cut].astype(F32)
        act_val, slope = gelu_kernel(pre)
        grad_act = r_.ga[:, cut].astype(F32)
        r_.act[:, cut] = act_val.astype(BF16)
        grad_pre = (r_.gatec[:, 0:1] * grad_act * slope).astype(BF16)
        r_.gp[:, cut] = grad_pre
        r_.gacc[...] += dot_nt(grad_pre, up[:, cut])
        both = act_val * grad_act
        r_.ggate[...] += sum(both[:, f : f + LANES] for f in range(0, FT, LANES))
        return carry

    lax.fori_loop(0, FF // FT, middle, 0)
    gate_grad = jnp.sum(r_.ggate[...], axis=-1, keepdims=True) + jnp.sum(
        r_.yrow[...].astype(F32) * r_.downb[...].astype(F32), axis=-1, keepdims=True
    )
    picked = jnp.where(slot_lane == me, 1.0, 0.0)
    contrib = (own_gates * (picked - own_gate) * gate_grad).astype(BF16)
    r_.gacc[...] += dot_nt(contrib, r_.smf[...])
    rows_drain(r_.hbuf, r_.hland, r_.h_sem)
    pack_slots(r_.gacc[...].astype(BF16), r_.rbuf)
    rows_start(r_.rbuf, r_.rland, r_.r_sem)
    r_.rterm[...] = dot_tn(r_.xrow[...], contrib)

    for j in range(D // WT):
        cut = slice(j * WT, (j + 1) * WT)
        r_.gacc[:, cut] = dot(r_.act[...], down[:, cut]) + r_.downb[:, cut].astype(F32)
    pack_slots(r_.gacc[...].astype(BF16), r_.obuf)

    for copy in cot_copies + hid_copies:
        copy.wait_recv()
    unpack(r_.coth[0], r_.yo)
    unpack(r_.hoth[0], r_.xo)
    far_gates = gates_of(r_.xo[...])
    far_gate = jnp.sum(jnp.where(slot_lane == me, far_gates, 0.0), axis=-1, keepdims=True)
    r_.yo[...] = (far_gate * r_.yo[...].astype(F32)).astype(BF16)

    def far(j, carry):
        cut = pl.ds(pl.multiple_of(j * FT, FT), FT)
        whole = pl.ds(pl.multiple_of(mine * part + j * FT, LANES), FT)
        pre = dot(r_.xo[...], up[:, whole]) + r_.upb[:, whole].astype(F32)
        act_val, slope = gelu_kernel(pre)
        r_.act_o[:, cut] = act_val.astype(BF16)
        grad_act = dot_nt(r_.yo[...], down[whole, :])
        r_.gp_o[:, cut] = (grad_act * slope).astype(BF16)
        return carry

    lax.fori_loop(0, part // FT, far, 0)

    half = D // 2
    pieces = [(True, row, lane) for lane in range(0, part, D) for row in range(0, D, half)]
    pieces += [(False, row, 0) for row in range(0, part, half)]
    kept, depth = [], FF // D

    def weight_grads(count):
        for is_up, row, lane in pieces[len(kept) : len(kept) + count]:
            if is_up:
                there = pl.ds(pl.multiple_of(mine * part + lane, LANES), D)
                own_gp, far_gp = r_.gp[:, there], r_.gp_o[:, lane : lane + D]
                value = dot_tn(r_.xrow[:, row : row + half], own_gp)
                value = value + dot_tn(r_.xo[:, row : row + half], far_gp)
                dst = r_.o_up.at[row : row + half, lane : lane + D]
                if row == 0:
                    r_.o_upb[:, lane : lane + D] = jnp.sum(
                        own_gp.astype(F32), axis=0, keepdims=True
                    ) + jnp.sum(far_gp.astype(F32), axis=0, keepdims=True)
            else:
                there = pl.ds(pl.multiple_of(mine * part + row, LANES), half)
                value = dot_tn(r_.act[:, there], r_.gbrow[...])
                value = value + dot_tn(r_.act_o[:, row : row + half], r_.yo[...])
                dst = r_.o_down.at[row : row + half]
            at = len(kept)
            slot = r_.ga.at[0:half, at % depth * D : (at % depth + 1) * D]
            if at >= depth:
                kept[at - depth].wait()
            slot[...] = value.astype(BF16)
            copy = pltpu.make_async_copy(slot, dst, r_.keep_sem.at[at])
            copy.start()
            kept.append(copy)

    weight_grads(3)

    pending = []

    def launch(copies):
        for copy in copies:
            copy.start()
        pending.extend(copies)
        return copies

    def core_start(tag):
        own, from_core, _, _, _, sems = tag
        return launch(
            [
                copy_to(
                    own.at[other_core], from_core, sems.at[0], sems.at[1],
                    shard=shard_of(at_z, at_y, other_core),
                )
            ]
        )

    def y_start(tag, before):
        own, from_core, from_y, _, _, sems = tag
        for copy in before:
            copy.wait_recv()
        for y in range(Y):
            own[core, y] = (own[core, y].astype(F32) + from_core[y].astype(F32)).astype(BF16)
        return launch(
            [
                copy_to(
                    own.at[core, turn(at_y, dy, Y)], from_y.at[dy - 1], sems.at[2 * dy],
                    sems.at[2 * dy + 1], shard=shard_of(at_z, turn(at_y, dy, Y), core),
                )
                for dy in range(1, Y)
            ]
        )

    def z_start(tag, before):
        own, _, from_y, from_z, _, sems = tag
        for copy in before:
            copy.wait_recv()
        total = own[core, at_y].astype(F32)
        for dy in range(1, Y):
            total = total + from_y[dy - 1].astype(F32)
        own[core, at_y] = total.astype(BF16)
        base = 2 * Y
        return launch(
            [
                copy_to(
                    own.at[core, at_y, turn(at_z, dz, Z)], from_z.at[dz - 1], sems.at[base + 2 * dz - 2],
                    sems.at[base + 2 * dz - 1], shard=shard_of(turn(at_z, dz, Z), at_y, core),
                )
                for dz in range(1, Z)
            ]
        )

    def x_start(tag, before):
        own, _, _, from_z, from_x, sems = tag
        for copy in before:
            copy.wait_recv()
        total = own[core, at_y, at_z].astype(F32)
        for dz in range(1, Z):
            total = total + from_z[dz - 1].astype(F32)
        own[core, at_y, at_z] = total.astype(BF16)
        base = 2 * Y + 2 * Z - 2
        return launch(
            [
                copy_to(
                    own.at[core, at_y, at_z], from_x.at[dx - 1], sems.at[base + 2 * dx - 2],
                    sems.at[base + 2 * dx - 1], replica=turn(mine, dx, R),
                )
                for dx in range(1, R)
            ]
        )

    def finish(tag, before, out):
        own, _, _, _, from_x, _ = tag
        for copy in before:
            copy.wait_recv()
        total = own[core, at_y, at_z].astype(F32)
        for dx in range(1, R):
            total = total + from_x[dx - 1].astype(F32)
        out[...] = total

    def put_part(tag, lane_at, value):
        own = tag[0]
        wide = value.shape[1]
        low_value = value.astype(BF16)
        for z in range(Z):
            for y in range(Y):
                for c in range(2):
                    s = (z * Y + y) * 2 + c
                    own[c, y, z, :, lane_at : lane_at + wide] = low_value[s * K : (s + 1) * K, :]

    vecs = r_.vecs
    vecs[...] = jnp.zeros((LANES, D), F32)

    def put_vector(i, value):
        vecs[E + i : E + i + 1, :] = value

    rows_wait(r_.rbuf, r_.rland, r_.r_sem)
    rows_start(r_.obuf, r_.oland, r_.o_sem)
    flat_back = r_.rland[...].reshape(SB, LW)
    for i in range(q):
        r_.gn[:, i * LW : (i + 1) * LW] = dot(r_.place[0, i] + r_.place[1, i], flat_back)

    def norm_grad(grad_rows, normed, inv, gain, at_gain, at_bias):
        scaled = grad_rows * gain
        inner = (
            scaled
            - jnp.mean(scaled, axis=-1, keepdims=True)
            - normed * jnp.mean(scaled * normed, axis=-1, keepdims=True)
        )
        put_vector(at_gain, jnp.sum(grad_rows * normed, axis=0, keepdims=True))
        put_vector(at_bias, jnp.sum(grad_rows, axis=0, keepdims=True))
        return inner * inv

    gres[...] = cotf[...] + norm_grad(r_.gn[...], n2[...], inv_two, vector(5), 5, 6)
    put_vector(4, jnp.sum(gres[...], axis=0, keepdims=True))
    r_.tmpb[...] = gres[...].astype(BF16)
    for j in range(D // WT):
        cut = slice(j * WT, (j + 1) * WT)
        put_part(r_.rs_o, j * WT, dot_tn(r_.ctx[...], r_.tmpb[:, cut]))
    stage_o = core_start(r_.rs_o)
    for j in range(D // WT):
        cut = slice(j * WT, (j + 1) * WT)
        r_.gctx[:, cut] = dot_nt(r_.tmpb[...], r_.wf_out[cut, :]).astype(BF16)

    def attend_back(i, carry):
        cut_q, cut_k, cut_v = pair_cuts(i)
        query, keys, values = r_.qkv[:, cut_q], r_.qkv[:, cut_k], r_.qkv[:, cut_v]
        query_half, key_half, grad_half = halves(query), halves(keys), halves(r_.gctx[:, cut_q])
        grad_q = grad_k = grad_v = None
        for a in range(2):
            probs = r_.probs[2 * i + a]
            grad_probs = dot_nt(grad_half[a], values)
            inner = jnp.sum(probs * grad_probs, axis=-1, keepdims=True)
            grad_scores = (probs * (grad_probs - inner) * scale).astype(BF16)
            terms = (
                dot(grad_scores, key_half[a]),
                dot_tn(grad_scores, query_half[a]),
                dot_tn(probs.astype(BF16), grad_half[a]),
            )
            if a == 0:
                grad_q, grad_k, grad_v = terms
            else:
                grad_q, grad_k, grad_v = grad_q + terms[0], grad_k + terms[1], grad_v + terms[2]
        r_.gm[:, cut_q] = grad_q.astype(BF16)
        r_.gm[:, cut_k] = grad_k.astype(BF16)
        r_.gm[:, cut_v] = grad_v.astype(BF16)
        vecs[E + 2 : E + 3, cut_q] = jnp.sum(grad_q, axis=0, keepdims=True)
        vecs[E + 3 : E + 4, cut_q] = jnp.sum(grad_v, axis=0, keepdims=True)
        return carry

    lax.fori_loop(0, pairs, attend_back, 0)
    stage_o = y_start(r_.rs_o, stage_o)

    def proj_part(tag, at):
        wide = tag[0].shape[-1]
        step = WT if wide % WT == 0 else wide
        for j in range(0, wide, step):
            put_part(tag, j, dot_tn(r_.act1[...], r_.gm[:, at + j : at + j + step]))
        return core_start(tag)

    stage_v = proj_part(r_.rs_v, 2 * D)
    stage_k = proj_part(r_.rs_k, D)
    stage_o = z_start(r_.rs_o, stage_o)
    stage_v = y_start(r_.rs_v, stage_v)
    stage_q = proj_part(r_.rs_q, 0)
    stage_p = proj_part(r_.rs_p, D // 2)
    stage_k = y_start(r_.rs_k, stage_k)
    for j in range(D // WT):
        cut = slice(j * WT, (j + 1) * WT)
        r_.gn[:, cut] = dot_nt(r_.gm[...], r_.wf_in[cut, :])
    stage_q = y_start(r_.rs_q, stage_q)
    stage_p = y_start(r_.rs_p, stage_p)
    grad_tok = gres[...] + norm_grad(r_.gn[...], n1[...], inv_one, vector(0), 0, 1)
    r_.o_grad[...] = grad_tok[0:T].astype(BF16)
    put_part(r_.rs_s, 0, vecs[...].T + r_.rterm[...])
    stage_s = core_start(r_.rs_s)
    stage_o = x_start(r_.rs_o, stage_o)
    stage_v = z_start(r_.rs_v, stage_v)
    stage_s = y_start(r_.rs_s, stage_s)

    weight_grads(2)
    rows_wait(r_.obuf, r_.oland, r_.o_sem)
    flat_out = r_.oland[...].reshape(SB, LW)
    for i in range(q):
        cut = slice(i * LW, (i + 1) * LW)
        total = resid[:, cut]
        for k in range(2):
            total = total + pair_gate[k] * dot(r_.place[k, i], flat_out)
        r_.o_rows[:, cut] = total[0:T].astype(BF16)

    stage_k = z_start(r_.rs_k, stage_k)
    finish(r_.rs_o, stage_o, r_.o_out)
    rows_drain(r_.rbuf, r_.rland, r_.r_sem)
    weight_grads(1)
    stage_v = x_start(r_.rs_v, stage_v)
    stage_q = z_start(r_.rs_q, stage_q)
    stage_k = x_start(r_.rs_k, stage_k)
    finish(r_.rs_v, stage_v, r_.o_proj.at[:, 2 * D : 3 * D])
    weight_grads(len(pieces) - len(kept))
    stage_p = z_start(r_.rs_p, stage_p)
    stage_s = z_start(r_.rs_s, stage_s)
    total_grad = jnp.sum(r_.gbrow[...].astype(F32), axis=0, keepdims=True)
    total_grad = total_grad + jnp.sum(r_.yo[...].astype(F32), axis=0, keepdims=True)
    bias[0:1, 0:D] = total_grad
    r_.o_downb[...] = bias[0:1, pl.ds(pl.multiple_of(mine * (D // R), LANES), D // R)]
    rows_drain(r_.obuf, r_.oland, r_.o_sem)
    for copy in cot_copies + hid_copies:
        copy.wait_send()
    stage_q = x_start(r_.rs_q, stage_q)
    stage_p = x_start(r_.rs_p, stage_p)
    stage_s = x_start(r_.rs_s, stage_s)
    for copy in kept[-depth:]:
        copy.wait()
    for copy in pending:
        copy.wait_send()
    finish(r_.rs_k, stage_k, r_.o_proj.at[:, D : 2 * D])
    finish(r_.rs_q, stage_q, r_.o_proj.at[:, 0 : D // 2])
    finish(r_.rs_p, stage_p, r_.o_proj.at[:, D // 2 : D])
    finish(r_.rs_s, stage_s, turned.at[0:K])
    r_.o_small[...] = turned[...].T[0 : r_.o_small.shape[0], 0:K]


def call_block(plan, *arrays):
    S, R, TP, FF, E = plan.S, plan.R, plan.TP, plan.FF, plan.E
    K, q, BR, LW, SB, N, Z, Y, part = (
        plan.K, plan.q, plan.BR, plan.LW, plan.SB, plan.N, plan.Z, plan.Y, plan.part,
    )
    vmem = pl.BlockSpec(memory_space=pltpu.VMEM)
    anyw = pl.BlockSpec(memory_space=pl.ANY)
    outs = dict(
        o_rows=((plan.T, D), BF16, vmem),
        o_grad=((plan.T, D), BF16, vmem),
        o_proj=((K, 3 * D), F32, vmem),
        o_out=((K, D), F32, vmem),
        o_small=((-(-(E + VECTORS) // 8) * 8, K), F32, vmem),
        o_up=((D, part), BF16, anyw),
        o_upb=((1, part), F32, vmem),
        o_down=((part, D), BF16, anyw),
        o_downb=((1, D // R), F32, vmem),
    )

    def landing(wide):
        return (
            pltpu.VMEM((2, Y, Z, K, wide), BF16),
            pltpu.VMEM((Y, Z, K, wide), BF16),
            pltpu.VMEM((max(Y - 1, 1), Z, K, wide), BF16),
            pltpu.VMEM((max(Z - 1, 1), K, wide), BF16),
            pltpu.VMEM((max(R - 1, 1), K, wide), BF16),
            pltpu.SemaphoreType.DMA((2 * (Y + Z + R),)),
        )

    def pairs_of(*extent):
        return pltpu.SemaphoreType.DMA(extent)

    rows = pltpu.VMEM((S, BR, LW), BF16)
    far_rows = pltpu.VMEM((R - 1, S, BR, LW), BF16)
    wide_rows = pltpu.VMEM((TP, D), F32)
    half_rows = pltpu.VMEM((TP, D), BF16)
    slot_rows = pltpu.VMEM((N, D), BF16)
    scratch = dict(
        up=pltpu.VMEM((D, FF), BF16),
        down=pltpu.VMEM((FF, D), BF16),
        wf_in=pltpu.VMEM((D, 3 * D), BF16),
        wf_out=pltpu.VMEM((D, D), BF16),
        smf=pltpu.VMEM((D, LANES), BF16),
        smt=pltpu.VMEM((LANES, D), F32),
        turned=pltpu.VMEM((LANES, LANES), F32),
        small=pltpu.VMEM((K, LANES), BF16),
        pairs_at=pltpu.VMEM((LANES, -(-TP // LANES) * LANES), F32),
        place=pltpu.VMEM((2, q, TP, SB), BF16),
        unroll=pltpu.VMEM((q, N, SB), BF16),
        cotf=wide_rows, n1=wide_rows, n2=wide_rows, resid=wide_rows, gres=wide_rows,
        gn=wide_rows,
        tmpb=half_rows, act1=half_rows, hid=half_rows, ctx=half_rows,
        bias=pltpu.VMEM((8, 3 * D), F32),
        qkv=pltpu.VMEM((TP, 3 * D), BF16),
        gm=pltpu.VMEM((TP, 3 * D), BF16),
        probs=pltpu.VMEM((HEADS, TP, TP), F32),
        cbuf=rows, cland=rows, hbuf=rows, hland=rows, rland=rows, oland=rows,
        coth=far_rows, hoth=far_rows,
        yrow=slot_rows, xrow=slot_rows, gbrow=slot_rows,
        xo=slot_rows,
        ga=pltpu.VMEM((N, FF), BF16),
        act=pltpu.VMEM((N, FF), BF16),
        gp=pltpu.VMEM((N, FF), BF16),
        act_o=pltpu.VMEM((N, part), BF16),
        gp_o=pltpu.VMEM((N, part), BF16),
        stage=pltpu.VMEM((1, N, D), F32),
        ggate=pltpu.VMEM((N, LANES), F32),
        gatec=pltpu.VMEM((N, LANES), F32),
        rterm=pltpu.VMEM((D, LANES), F32),
        vecs=pltpu.VMEM((LANES, D), F32),
        rs_o=landing(D), rs_v=landing(D), rs_k=landing(D), rs_q=landing(D // 2), rs_p=landing(D // 2), rs_s=landing(LANES),
        load_sem=pairs_of(2),
        ag_send=pairs_of(5, 3 + Y, S),
        ag_recv=pairs_of(5, S),
        c_sem=pairs_of(2, S),
        h_sem=pairs_of(2, S),
        r_sem=pairs_of(2, S),
        o_sem=pairs_of(2, S),
        cx_sem=pairs_of(2, R),
        hx_sem=pairs_of(2, R),
        keep_sem=pairs_of(2 * (part // D) + 2 * part // D),
    )
    return pl.pallas_call(
        functools.partial(block_kernel, plan, list(outs)),
        out_shape=[jax.ShapeDtypeStruct(o[0], o[1]) for o in outs.values()],
        in_specs=[vmem] * (9 + VECTORS) + [anyw] * 2,
        out_specs=[o[2] for o in outs.values()],
        scratch_shapes=scratch,
        compiler_params=pltpu.CompilerParams(
            collective_id=0, has_side_effects=True, vmem_limit_bytes=60 * 1024 * 1024
        ),
        cost_estimate=pl.CostEstimate(
            flops=12 * N * D * FF, bytes_accessed=4 * D * FF, transcendentals=2 * N * FF
        ),
    )(*arrays)


def outputs_kernel(plan, count, *refs):
    srcs, small, rest = refs[:count], refs[count], refs[count + 1 :]
    dsts, vectors, router = rest[:count], rest[count : count + VECTORS], rest[count + VECTORS]
    lands, wides, sems = rest[count + VECTORS + 1 : 2 * count + VECTORS + 1], rest[-3:-1], rest[-1]
    steps = []
    for n, (src, land, dst) in enumerate(zip(srcs, lands, dsts)):
        cuts = 6 if n < 2 else 1
        rows = src.shape[0] // cuts
        wide = wides[n] if n < 2 else land
        for cut in range(cuts):
            part = pl.ds(cut * rows, rows)
            at = len(steps)
            fetch = pltpu.make_async_copy(src.at[part], land.at[part], sems.at[0, at])
            fetch.start()
            store = pltpu.make_async_copy(wide.at[part], dst.at[part], sems.at[1, at])
            steps.append((fetch, land, wide, part, store))
    for i, vector in enumerate(vectors):
        vector[...] = small[plan.E + i : plan.E + i + 1, :].reshape(plan.K)
    router[...] = small[0 : plan.E, :]
    for fetch, land, wide, part, store in steps:
        fetch.wait()
        if wide is not land:
            wide[part, :] = land[part, :].astype(F32)
        store.start()
    for step in steps:
        step[-1].wait()


def call_outputs(plan, arrays, small):
    vmem = pl.BlockSpec(memory_space=pltpu.VMEM)
    anyw = pl.BlockSpec(memory_space=pl.ANY)
    count = len(arrays)
    return pl.pallas_call(
        functools.partial(outputs_kernel, plan, count),
        out_shape=[jax.ShapeDtypeStruct(a.shape, F32 if n < 2 else a.dtype) for n, a in enumerate(arrays)]
        + [jax.ShapeDtypeStruct((plan.K,), F32)] * VECTORS
        + [jax.ShapeDtypeStruct((plan.E, plan.K), F32)],
        in_specs=[anyw] * count + [vmem],
        out_specs=[anyw] * count + [vmem] * (VECTORS + 1),
        scratch_shapes=[pltpu.VMEM(a.shape, a.dtype) for a in arrays]
        + [pltpu.VMEM(a.shape, F32) for a in arrays[:2]]
        + [pltpu.SemaphoreType.DMA((2, 12 + count))],
        compiler_params=pltpu.CompilerParams(vmem_limit_bytes=60 * 1024 * 1024),
    )(*arrays, small)


def body(
    tokens, cotangent, norm1_gain, norm1_bias, proj_in, query_bias, value_bias, proj_out, out_bias,
    norm2_gain, norm2_bias, router, up_weight, up_bias, down_weight, down_bias, expert_ids, slot_ids,
):
    shards, replicas = lax.axis_size("shard"), lax.axis_size("replica")
    rows = tokens.shape[0] * tokens.shape[1]
    plan = Plan(shards, replicas, rows, up_weight.shape[2], up_weight.shape[0])
    if plan.part % D or plan.N < D // 2 or up_weight.shape[0] != 1 or tokens.shape[0] != 1:
        return plain_body(
            tokens, cotangent, norm1_gain, norm1_bias, proj_in, query_bias, value_bias, proj_out,
            out_bias, norm2_gain, norm2_bias, router, up_weight, up_bias, down_weight, down_bias,
            expert_ids, slot_ids,
        )
    (o_rows, o_grad, o_proj, o_out, o_small, o_up, o_upb, o_down, o_downb) = call_block(
        plan, tokens.reshape(rows, D), cotangent.reshape(rows, D), proj_in, proj_out, router.T,
        expert_ids.T, slot_ids.T, up_bias, down_bias, norm1_gain, norm1_bias, query_bias, value_bias,
        out_bias, norm2_gain, norm2_bias, up_weight[0], down_weight[0],
    )
    (o_up, o_down, o_rows, o_grad, o_proj, o_out, o_upb, o_downb, *vec, o_router) = call_outputs(
        plan, [o_up, o_down, o_rows, o_grad, o_proj, o_out, o_upb, o_downb], o_small
    )
    return (
        o_rows.reshape(tokens.shape),
        o_grad.reshape(tokens.shape),
        vec[0], vec[1], o_proj, vec[2], vec[3], o_out, vec[4], vec[5], vec[6], o_router.T,
        o_up[None], o_upb, o_down[None], o_downb,
    )


def fits_kernel(mesh):
    shards, replicas = mesh.shape["shard"], mesh.shape["replica"]
    return shards % 2 == 0 and D % shards == 0 and (D // shards) % 16 == 0 and replicas == 2


def solution(mesh):
    in_specs = (
        P(("replica", "shard"), None, None),
        P(("replica", "shard"), None, None),
        P("shard"),
        P("shard"),
        P("shard", None),
        P("shard"),
        P("shard"),
        P("shard", None),
        P("shard"),
        P("shard"),
        P("shard"),
        P("shard", None),
        P("shard", None, None),
        P("shard", None),
        P("shard", None, None),
        P("shard", None),
        P(("replica", "shard"), None),
        P(("replica", "shard"), None),
    )
    out_specs = (
        P(("replica", "shard"), None, None),
        P(("replica", "shard"), None, None),
        P("shard"),
        P("shard"),
        P("shard", None),
        P("shard"),
        P("shard"),
        P("shard", None),
        P("shard"),
        P("shard"),
        P("shard"),
        P("shard", None),
        P("shard", None, "replica"),
        P("shard", "replica"),
        P("shard", "replica", None),
        P("shard", "replica"),
    )
    chosen = body if fits_kernel(mesh) else plain_body
    return jax.shard_map(chosen, mesh=mesh, in_specs=in_specs, out_specs=out_specs, check_vma=False)
```

```python
import functools
from types import SimpleNamespace

import jax
import jax.numpy as jnp
from jax import lax
from jax.experimental import pallas as pl
from jax.experimental.pallas import tpu as pltpu
from jax.sharding import PartitionSpec as P

D = 768
HEADS = 12
HDIM = 64
SEQ = 197


EPS = 1e-06
SQRT_HALF = 0.7071067811865476
INV_ROOT_TWO_PI = 0.3989422804014327


def layer_norm(rows_in, norm_gain, norm_shift):
    average = jnp.mean(rows_in, axis=-1, keepdims=True)
    centred = rows_in - average
    inv_std = lax.rsqrt(jnp.mean(centred * centred, axis=-1, keepdims=True) + EPS)
    normed = centred * inv_std
    return (normed, inv_std, normed * norm_gain + norm_shift)


def norm_back(grad_rows, normed, inv_std, norm_gain):
    scaled = grad_rows * norm_gain
    inner = (
        scaled
        - jnp.mean(scaled, axis=-1, keepdims=True)
        - normed * jnp.mean(scaled * normed, axis=-1, keepdims=True)
    )
    return (inner * inv_std, jnp.sum(grad_rows * normed, axis=0), jnp.sum(grad_rows, axis=0))


def gelu_parts(pre_act):
    cumul = 0.5 * (1.0 + lax.erf(pre_act * SQRT_HALF))
    return (pre_act * cumul, cumul + pre_act * jnp.exp(-0.5 * pre_act * pre_act) * INV_ROOT_TWO_PI)


def route_table(expert_ids, slot_ids, experts, capacity):
    positions = jnp.arange(experts * capacity, dtype=jnp.int32)
    tables = []
    for choose in range(2):
        kept = slot_ids[:, choose] < capacity
        target = jnp.where(kept, expert_ids[:, choose] * capacity + slot_ids[:, choose], -1)
        tables.append((target[:, None] == positions[None, :]).astype(jnp.bfloat16))
    return tables


def pick_table(expert_ids, experts):
    labels = jnp.arange(experts, dtype=jnp.int32)
    return [
        (expert_ids[:, choose][:, None] == labels[None, :]).astype(jnp.float32)
        for choose in range(2)
    ]


def lane_pad(blocks):
    rows = blocks[0].shape[0]
    spare = -sum(block.shape[1] for block in blocks) % 128
    return jnp.concatenate(blocks + [jnp.zeros((rows, spare), blocks[0].dtype)], axis=1)


def other_replicas(value):
    size = lax.axis_size("replica")
    return [
        lax.ppermute(value, "replica", [(at, (at + step) % size) for at in range(size)])
        for step in range(1, size)
    ]


def to_expert(value, local_experts, capacity):
    shards, width = value.shape[0], value.shape[-1]
    return (
        value.reshape(shards, local_experts, capacity, width)
        .swapaxes(0, 1)
        .reshape(local_experts, shards * capacity, width)
    )


def from_expert(value, shards, capacity):
    local_experts, width = value.shape[0], value.shape[-1]
    return (
        value.reshape(local_experts, shards, capacity, width)
        .swapaxes(0, 1)
        .reshape(shards, local_experts * capacity, width)
    )


def expert_middle(rows, grad_rows, up_weight, up_bias, down_weight):
    expert_pre = (
        jnp.einsum("ecd,edf->ecf", rows, up_weight, preferred_element_type=jnp.float32)
        + up_bias.astype(jnp.float32)[:, None, :]
    )
    act_val, slope = gelu_parts(expert_pre)
    grad_active = jnp.einsum(
        "ecd,efd->ecf", grad_rows, down_weight, preferred_element_type=jnp.float32
    )
    return (act_val.astype(jnp.bfloat16), (grad_active * slope).astype(jnp.bfloat16))


def plain_body(
    tokens,
    cotangent,
    norm1_gain,
    norm1_bias,
    proj_in,
    query_bias,
    value_bias,
    proj_out,
    out_bias,
    norm2_gain,
    norm2_bias,
    router,
    up_weight,
    up_bias,
    down_weight,
    down_bias,
    expert_ids,
    slot_ids,
):
    images = tokens.shape[0]
    small = jnp.stack(
        [norm1_gain, norm1_bias, query_bias, value_bias, out_bias, norm2_gain, norm2_bias],
        axis=1,
    )
    width_in, width_small = proj_in.shape[1], small.shape[1] + router.shape[1]
    first = lax.all_gather(
        lane_pad([proj_in, proj_out, small, router]), "shard", axis=0, tiled=True
    )
    width_both = width_in + proj_out.shape[1]
    proj_full = first[:, :width_in]
    outproj_full = first[:, width_in:width_both]
    small_full = first[:, width_both : width_both + small.shape[1]]
    router_full = first[:, width_both + small.shape[1] : width_both + width_small]
    (
        gain_one,
        shift_one,
        query_shift,
        value_shift,
        out_shift,
        gain_two,
        shift_two,
    ) = [row for row in small_full.T]
    tok_rows = tokens.reshape(-1, D).astype(jnp.float32)
    normed_one, inv_one, pre_one = layer_norm(
        tok_rows, gain_one.astype(jnp.float32), shift_one.astype(jnp.float32)
    )
    act_one = pre_one.astype(jnp.bfloat16)
    mixed = jnp.dot(act_one, proj_full, preferred_element_type=jnp.float32)
    query_part = (mixed[:, :D] + query_shift.astype(jnp.float32)).astype(jnp.bfloat16)
    key_part = mixed[:, D : 2 * D].astype(jnp.bfloat16)
    value_part = (mixed[:, 2 * D :] + value_shift.astype(jnp.float32)).astype(jnp.bfloat16)
    query_heads = query_part.reshape(images, SEQ, HEADS, HDIM)
    key_heads = key_part.reshape(images, SEQ, HEADS, HDIM)
    value_heads = value_part.reshape(images, SEQ, HEADS, HDIM)
    scores = jnp.einsum(
        "ishd,ithd->ihst", query_heads, key_heads, preferred_element_type=jnp.float32
    ) * HDIM ** (-0.5)
    log_total = jnp.log(jnp.sum(jnp.exp(scores), axis=-1))
    attn_probs = jnp.exp(scores - log_total[..., None]).astype(jnp.bfloat16)
    context = (
        jnp.einsum("ihst,ithd->ishd", attn_probs, value_heads, preferred_element_type=jnp.float32)
        .reshape(-1, D)
        .astype(jnp.bfloat16)
    )
    resid = (
        tok_rows
        + jnp.dot(context, outproj_full, preferred_element_type=jnp.float32)
        + out_shift.astype(jnp.float32)
    )
    normed_two, inv_two, pre_two = layer_norm(
        resid, gain_two.astype(jnp.float32), shift_two.astype(jnp.float32)
    )
    hidden = pre_two.astype(jnp.bfloat16)
    logits = jnp.dot(hidden, router_full, preferred_element_type=jnp.float32)
    exp_logits = jnp.exp(logits)
    gate_probs = exp_logits / jnp.sum(exp_logits, axis=-1, keepdims=True)
    local_experts = up_weight.shape[0]
    experts = local_experts * lax.axis_size("shard")
    capacity = 2 * tok_rows.shape[0] // experts
    routes = route_table(expert_ids, slot_ids, experts, capacity)
    picks = pick_table(expert_ids, experts)
    both = jnp.concatenate(routes, axis=0)
    either = routes[0] + routes[1]
    gate_pair = [jnp.sum(gate_probs * pick, axis=-1) for pick in picks]
    grad_out = cotangent.reshape(-1, D).astype(jnp.float32)
    sent = jnp.concatenate(
        [(gate[:, None] * grad_out).astype(jnp.bfloat16) for gate in gate_pair], axis=0
    )
    buffer = jnp.dot(either.T, hidden, preferred_element_type=jnp.float32)
    grad_buffer = jnp.dot(both.T, sent, preferred_element_type=jnp.float32)
    shards = lax.axis_size("shard")
    outgoing = (
        jnp.concatenate([buffer, grad_buffer], axis=1)
        .astype(jnp.bfloat16)
        .reshape(shards, local_experts * capacity, 2 * D)
    )
    landed = to_expert(
        lax.all_to_all(outgoing, "shard", split_axis=0, concat_axis=0, tiled=True),
        local_experts,
        capacity,
    )
    arrived, grad_arrived = landed[..., :D], landed[..., D:]
    others = other_replicas(landed)
    active, grad_pre = expert_middle(arrived, grad_arrived, up_weight, up_bias, down_weight)
    expert_out = (
        jnp.einsum("ecf,efd->ecd", active, down_weight, preferred_element_type=jnp.float32)
        + down_bias.astype(jnp.float32)[:, None, :]
    ).astype(jnp.bfloat16)
    grad_in = jnp.einsum(
        "ecf,edf->ecd", grad_pre, up_weight, preferred_element_type=jnp.float32
    ).astype(jnp.bfloat16)
    answer = from_expert(jnp.concatenate([expert_out, grad_in], axis=2), shards, capacity)
    back = lax.all_to_all(answer, "shard", split_axis=0, concat_axis=0, tiled=True).reshape(
        experts * capacity, 2 * D
    )
    returned, grad_back = back[:, :D], back[:, D:]

    replicas = lax.axis_size("replica")
    ours = lax.axis_index("replica")
    part = up_weight.shape[2] // replicas
    up_part = lax.dynamic_slice_in_dim(up_weight, ours * part, part, axis=2)
    up_bias_part = lax.dynamic_slice_in_dim(up_bias, ours * part, part, axis=1)
    down_part = lax.dynamic_slice_in_dim(down_weight, ours * part, part, axis=1)
    active_parts = [lax.dynamic_slice_in_dim(active, ours * part, part, axis=2)]
    grad_pre_parts = [lax.dynamic_slice_in_dim(grad_pre, ours * part, part, axis=2)]
    for other in others:
        other_active, other_pre = expert_middle(
            other[..., :D], other[..., D:], up_part, up_bias_part, down_part
        )
        active_parts.append(other_active)
        grad_pre_parts.append(other_pre)
    all_rows = jnp.concatenate([landed] + others, axis=1)
    all_active = jnp.concatenate(active_parts, axis=1)
    all_pre = jnp.concatenate(grad_pre_parts, axis=1)
    width_part = D // replicas
    expert_grads = (
        jnp.einsum("ecd,ecf->edf", all_rows[..., :D], all_pre, preferred_element_type=jnp.float32),
        jnp.sum(all_pre, axis=1, dtype=jnp.float32),
        jnp.einsum(
            "ecf,ecd->efd", all_active, all_rows[..., D:], preferred_element_type=jnp.float32
        ),
        lax.dynamic_slice_in_dim(
            jnp.sum(all_rows[..., D:], axis=1, dtype=jnp.float32),
            ours * width_part,
            width_part,
            axis=1,
        ),
    )

    rows_here = tok_rows.shape[0]
    gathered_both = jnp.dot(both, returned, preferred_element_type=jnp.float32)
    gathered_pair = [gathered_both[:rows_here], gathered_both[rows_here:]]
    moe_sum = gate_pair[0][:, None] * gathered_pair[0] + gate_pair[1][:, None] * gathered_pair[1]
    block_out = (resid + moe_sum).astype(jnp.bfloat16).reshape(tokens.shape)
    grad_gate = [jnp.sum(grad_out * part_k, axis=-1) for part_k in gathered_pair]
    back_gain_one, back_proj, back_outproj, back_gain_two, back_router = (
        gain_one,
        proj_full,
        outproj_full,
        gain_two,
        router_full,
    )
    grad_moe = jnp.dot(either, grad_back, preferred_element_type=jnp.float32)
    grad_gates = picks[0] * grad_gate[0][:, None] + picks[1] * grad_gate[1][:, None]
    grad_logits = (
        gate_probs * (grad_gates - jnp.sum(gate_probs * grad_gates, axis=-1, keepdims=True))
    ).astype(jnp.bfloat16)
    router_term = jnp.dot(hidden.T, grad_logits, preferred_element_type=jnp.float32)
    grad_norm_two = grad_moe + jnp.dot(
        grad_logits, back_router.T, preferred_element_type=jnp.float32
    )
    grad_resid_two, gain_two_term, shift_two_term = norm_back(
        grad_norm_two, normed_two, inv_two, back_gain_two.astype(jnp.float32)
    )
    grad_resid = grad_out + grad_resid_two
    resid_bf = grad_resid.astype(jnp.bfloat16)
    out_shift_term = jnp.sum(grad_resid, axis=0)
    outproj_term = jnp.dot(context.T, resid_bf, preferred_element_type=jnp.float32)
    grad_context = (
        jnp.dot(resid_bf, back_outproj.T, preferred_element_type=jnp.float32)
        .astype(jnp.bfloat16)
        .reshape(images, SEQ, HEADS, HDIM)
    )
    scores_again = jnp.einsum(
        "ishd,ithd->ihst", query_heads, key_heads, preferred_element_type=jnp.float32
    ) * HDIM ** (-0.5)
    probs_full = jnp.exp(scores_again - log_total[..., None])
    grad_probs = jnp.einsum(
        "ishd,ithd->ihst", grad_context, value_heads, preferred_element_type=jnp.float32
    )
    grad_scores = (
        probs_full
        * (grad_probs - jnp.sum(probs_full * grad_probs, axis=-1, keepdims=True))
        * HDIM ** (-0.5)
    ).astype(jnp.bfloat16)
    probs_bf = probs_full.astype(jnp.bfloat16)
    grad_value = jnp.einsum(
        "ihst,ishd->ithd", probs_bf, grad_context, preferred_element_type=jnp.float32
    ).reshape(-1, D)
    grad_query = jnp.einsum(
        "ihst,ithd->ishd", grad_scores, key_heads, preferred_element_type=jnp.float32
    ).reshape(-1, D)
    grad_key = jnp.einsum(
        "ihst,ishd->ithd", grad_scores, query_heads, preferred_element_type=jnp.float32
    ).reshape(-1, D)
    grad_mixed = jnp.concatenate([grad_query, grad_key, grad_value], axis=1).astype(jnp.bfloat16)
    proj_term = jnp.dot(act_one.T, grad_mixed, preferred_element_type=jnp.float32)
    grad_act = jnp.dot(grad_mixed, back_proj.T, preferred_element_type=jnp.float32)
    grad_tok_norm, gain_one_term, shift_one_term = norm_back(
        grad_act, normed_one, inv_one, back_gain_one.astype(jnp.float32)
    )
    tokens_grad = (grad_resid + grad_tok_norm).astype(jnp.bfloat16).reshape(tokens.shape)
    query_shift_term = jnp.sum(grad_query, axis=0)
    value_shift_term = jnp.sum(grad_value, axis=0)
    column_sums = [
        gain_one_term,
        shift_one_term,
        query_shift_term,
        value_shift_term,
        out_shift_term,
        gain_two_term,
        shift_two_term,
    ]
    summed = lax.psum_scatter(
        lane_pad(
            [
                proj_term.astype(jnp.bfloat16),
                outproj_term.astype(jnp.bfloat16),
                lax.optimization_barrier(
                    lane_pad(
                        [
                            jnp.stack(column_sums, axis=0).astype(jnp.bfloat16).T,
                            router_term.astype(jnp.bfloat16),
                        ]
                    )
                ),
            ]
        ),
        "shard",
        scatter_dimension=0,
        tiled=True,
    )
    total = summed.astype(jnp.float32)
    for other in other_replicas(summed):
        total = total + other.astype(jnp.float32)
    small_total = total[:, width_both:]
    columns = len(column_sums)
    dense_grads = (
        small_total[:, 0],
        small_total[:, 1],
        total[:, :width_in],
        small_total[:, 2],
        small_total[:, 3],
        total[:, width_in:width_both],
        small_total[:, 4],
        small_total[:, 5],
        small_total[:, 6],
        small_total[:, columns : columns + experts],
    )
    return (
        block_out,
        tokens_grad,
        dense_grads[0],
        dense_grads[1],
        dense_grads[2],
        dense_grads[3],
        dense_grads[4],
        dense_grads[5],
        dense_grads[6],
        dense_grads[7],
        dense_grads[8],
        dense_grads[9],
        expert_grads[0],
        expert_grads[1],
        expert_grads[2],
        expert_grads[3],
    )


F32 = jnp.float32
BF16 = jnp.bfloat16
LANES = 128
VECTORS = 7


def dot(left, right):
    return jnp.dot(left, right, preferred_element_type=F32)


def dot_nt(left, right):
    return lax.dot_general(left, right, (((1,), (1,)), ((), ())), preferred_element_type=F32)


def dot_tn(left, right):
    return lax.dot_general(left, right, (((0,), (0,)), ((), ())), preferred_element_type=F32)


def iota(shape, axis):
    return lax.broadcasted_iota(jnp.int32, shape, axis)


class Plan:
    def __init__(self, shards, replicas, rows, hidden_units, local_experts):
        self.S, self.R, self.T, self.FF = shards, replicas, rows, hidden_units
        self.E = local_experts * shards
        self.C = 2 * rows // self.E
        self.TP = -(-rows // 16) * 16
        self.K = D // shards
        self.q = 2 if self.C % 16 and (2 * self.C) % 16 == 0 else 1
        self.CR = self.C if self.q == 2 else -(-self.C // 16) * 16
        self.BR = self.CR * self.q
        self.LW = D // self.q
        self.SB = shards * self.BR
        self.N = shards * self.CR
        self.part = hidden_units // replicas
        self.core = 2
        chips = shards // 2
        self.Z = 4 if chips % 4 == 0 else chips
        self.Y = chips // self.Z


def block_kernel(
    plan, out_names, tok, cot, w_in, w_out, router, ids, slots, upb, downb, *refs, **scratch
):
    vectors, (up_h, down_h), refs = refs[:VECTORS], refs[VECTORS : VECTORS + 2], refs[VECTORS + 2 :]
    r_ = SimpleNamespace(
        tok=tok, cot=cot, w_in=w_in, w_out=w_out, ids=ids, slots=slots, upb=upb,
        downb=downb, up_h=up_h, down_h=down_h, **dict(zip(out_names, refs)), **scratch,
    )
    r_.rbuf, r_.obuf, r_.gctx, r_.yo, r_.gacc = r_.hbuf, r_.cbuf, r_.hid, r_.yrow, r_.stage.at[0]
    S, R, T, TP, FF, E, C = plan.S, plan.R, plan.T, plan.TP, plan.FF, plan.E, plan.C
    K, q, CR, BR, LW, SB, N, Z, Y = (
        plan.K, plan.q, plan.CR, plan.BR, plan.LW, plan.SB, plan.N, plan.Z, plan.Y,
    )
    part = plan.part
    me = lax.axis_index("shard")
    mine = lax.axis_index("replica")
    core = lax.rem(me, 2)
    at_y = lax.rem(lax.div(me, 2), Y)
    at_z = lax.div(me, 2 * Y)
    other_core = 1 - core

    def shard_of(z, y, c):
        return (z * Y + y) * 2 + c

    def turn(base, step, size):
        return lax.rem(base + step, size)

    def copy_to(src, dst, send, recv, **device):
        return pltpu.make_async_remote_copy(
            src_ref=src, dst_ref=dst, send_sem=send, recv_sem=recv,
            device_id=device, device_id_type=pl.DeviceIdType.MESH,
        )

    load_up = pltpu.make_async_copy(r_.up_h, r_.up, r_.load_sem.at[0])
    load_down = pltpu.make_async_copy(r_.down_h, r_.down, r_.load_sem.at[1])
    load_up.start()
    load_down.start()

    turned = r_.turned
    turned[...] = jnp.zeros((LANES, LANES), F32)
    turned[0:E, 0:K] = router[...].astype(F32)
    for i, vector_ref in enumerate(vectors):
        turned[E + i : E + i + 1, 0:K] = vector_ref[...].astype(F32).reshape(1, K)
    r_.small[...] = turned[...].T[0:K, :].astype(BF16)

    barrier = pltpu.get_barrier_semaphore()
    for step in range(1, S):
        pl.semaphore_signal(
            barrier, inc=1, device_id={"shard": turn(me, step, S)}, device_id_type=pl.DeviceIdType.MESH
        )
    for step in range(1, R):
        pl.semaphore_signal(
            barrier, inc=1, device_id={"replica": turn(mine, step, R)}, device_id_type=pl.DeviceIdType.MESH
        )
    pl.semaphore_wait(barrier, S - 1 + R - 1)

    both_lanes, own_lanes = pl.ds(2 * D, D), pl.ds(pl.multiple_of(mine * D, LANES), D)
    far_lanes = pl.ds(pl.multiple_of((1 - mine) * D, LANES), D)
    every = slice(None)
    SMALL, BOTH, OWN, FAR, OUT = range(5)
    gathers = [
        (r_.small, r_.smf, every),
        (r_.w_in, r_.wf_in, both_lanes),
        (r_.w_in, r_.wf_in, own_lanes),
        (r_.w_in, r_.wf_in, far_lanes),
        (r_.w_out, r_.wf_out, every),
    ]
    UP, DOWN, CORE, REPLICA, ACROSS = range(5)
    state = SimpleNamespace(drain=False)

    def rows_of(s):
        return pl.ds(pl.multiple_of(s * K, 16), K)

    def block_of(a, s):
        return gathers[a][1].at[rows_of(s), gathers[a][2]]

    def send_block(a, s, src, way, lands=None, **device):
        copy = copy_to(
            src, block_of(a, s), r_.ag_send.at[a, way, s],
            r_.ag_recv.at[a if lands is None else lands, s], **device,
        )
        if state.drain:
            copy.wait_send()
        else:
            copy.start()

    def wait_block(a, s):
        if not state.drain:
            copy_to(
                block_of(a, s), block_of(a, s), r_.ag_send.at[a, CORE, s], r_.ag_recv.at[a, s],
                shard=s,
            ).wait_recv()

    def to_core(a, s, src):
        send_block(a, s, src, CORE, shard=shard_of(at_z, at_y, other_core))

    def to_replica(a, s, src):
        if a == OWN:
            send_block(OWN, s, src, REPLICA, lands=FAR, replica=1 - mine)

    def along(a, s, src, up):
        @pl.when(at_z < Z - 1 if up else at_z > 0)
        def _():
            send_block(
                a, s, src, UP if up else DOWN,
                shard=shard_of(at_z + 1 if up else at_z - 1, at_y, core),
            )

    def across(a, s, src):
        for dy in range(1, Y):
            send_block(a, s, src, ACROSS + dy - 1, shard=shard_of(at_z, turn(at_y, dy, Y), core))

    def gather_start(a):
        src = gathers[a][0].at[:, gathers[a][2]]
        along(a, me, src, True)
        along(a, me, src, False)
        across(a, me, src)
        to_core(a, me, src)

    def at_distance(distance, go):
        if distance == 0:
            go(at_z, None)
            return

        @pl.when(at_z >= distance)
        def _():
            go(at_z - distance, True)

        @pl.when(at_z + distance < Z)
        def _():
            go(at_z + distance, False)

    def gather_z(distance, *which):
        def go(z, up):
            s = shard_of(z, at_y, core)
            for a in which:
                wait_block(a, s)
                src = block_of(a, s)
                along(a, s, src, up)
                across(a, s, src)
                to_replica(a, s, src)
                to_core(a, s, src)

        at_distance(distance, go)

    def gather_y(distance, *which):
        def go(z, up):
            for dy in range(1, Y):
                s = shard_of(z, turn(at_y, dy, Y), core)
                for a in which:
                    wait_block(a, s)
                    to_replica(a, s, block_of(a, s))
                    to_core(a, s, block_of(a, s))

        at_distance(distance, go)

    def gather_lines(*which):
        for distance in range(1, Z):
            gather_z(distance, *which)
            gather_y(distance - 1, *which)
        gather_y(Z - 1, *which)

    def gather_x():
        for distance in range(Z):

            def go(z, up):
                for dy in range(Y):
                    if distance or dy:
                        s = shard_of(z, turn(at_y, dy, Y), core)
                        wait_block(FAR, s)
                        to_core(FAR, s, block_of(FAR, s))

            at_distance(distance, go)

    def gather_end(*which):
        for dz in range(Z):
            for dy in range(Y):
                for a in which:
                    wait_block(a, shard_of(turn(at_z, dz, Z), turn(at_y, dy, Y), other_core))

    gather_start(SMALL)
    gather_start(BOTH)
    gather_start(OWN)
    to_core(FAR, me, r_.w_in.at[:, far_lanes])
    for src, dst in ((r_.small, r_.smf), (r_.w_in, r_.wf_in), (r_.w_out, r_.wf_out)):
        dst[rows_of(me), :] = src[...]

    def gather_step(distance, *which):
        if distance < Z:
            gather_z(distance, *which)
        gather_y(distance - 1, *which)

    first = (SMALL, BOTH, OWN)

    def rows_start(buf, land, sems):
        land[me] = buf[me]

        def go(step, carry):
            peer = turn(me, step, S)
            copy_to(
                buf.at[peer], land.at[me], sems.at[0, step], sems.at[1, me], shard=peer
            ).start()
            return carry

        lax.fori_loop(1, S, go, 0)

    def rows_wait(buf, land, sems):
        def go(step, carry):
            src = turn(me, step, S)
            copy_to(
                buf.at[src], land.at[src], sems.at[0, step], sems.at[1, src], shard=src
            ).wait_recv()
            return carry

        lax.fori_loop(1, S, go, 0)

    def rows_drain(buf, land, sems):
        def go(step, carry):
            peer = turn(me, step, S)
            copy_to(
                buf.at[peer], land.at[me], sems.at[0, step], sems.at[1, me], shard=peer
            ).wait_send()
            return carry

        lax.fori_loop(1, S, go, 0)

    def replicas_copies(land, others, sems):
        return [
            copy_to(
                land, others.at[step - 1], sems.at[0, step], sems.at[1, step],
                replica=turn(mine, step, R),
            )
            for step in range(1, R)
        ]

    cotf, n1, n2, resid, gres = r_.cotf, r_.n1, r_.n2, r_.resid, r_.gres
    resid[T - T % 8 :, :] = jnp.zeros((TP - (T - T % 8), D), F32)
    cotf[T - T % 8 :, :] = jnp.zeros((TP - (T - T % 8), D), F32)
    resid[0:T, :] = r_.tok[...].astype(F32)
    cotf[0:T, :] = r_.cot[...].astype(F32)

    def normalise(rows):
        average = jnp.mean(rows, axis=-1, keepdims=True)
        centred = rows - average
        inv = lax.rsqrt(jnp.mean(centred * centred, axis=-1, keepdims=True) + EPS)
        return centred * inv, inv

    normed_one, inv_one = normalise(resid[...])
    n1[...] = normed_one

    gather_step(1, *first)

    pairs_at = r_.pairs_at
    pairs_at[...] = jnp.full(pairs_at.shape, C, F32)
    pairs_at[0:2, 0:T] = r_.ids[...].astype(F32)
    pairs_at[2:4, 0:T] = r_.slots[...].astype(F32)
    pair_columns = pairs_at[...].T[0:TP, :].astype(jnp.int32)
    ids_v, slots_v = pair_columns[:, 0:2], pair_columns[:, 2:4]
    columns = iota((TP, SB), 1)
    for k in range(2):
        base = jnp.where(
            slots_v[:, k : k + 1] < C, ids_v[:, k : k + 1] * BR + slots_v[:, k : k + 1], -4 * SB
        )
        for i in range(q):
            r_.place[k, i] = jnp.where(columns == base + i * CR, 1.0, 0.0).astype(BF16)

    gather_step(2, *first)
    slot_row = iota((N, SB), 0)
    slot_peer = lax.shift_right_logical(slot_row * (65536 // CR + 1), 16)
    slot_col = slot_peer * BR + (slot_row - slot_peer * CR)
    for i in range(q):
        r_.unroll[i] = jnp.where(iota((N, SB), 1) == slot_col + i * CR, 1.0, 0.0).astype(BF16)

    def pack_tokens(src, dst):
        acc = None
        for i in range(q):
            table = r_.place[0, i] + r_.place[1, i]
            term = dot_tn(table, src[:, i * LW : (i + 1) * LW])
            acc = term if acc is None else acc + term
        dst[...] = acc.astype(BF16).reshape(S, BR, LW)

    def unpack(land, dst):
        flat = land.reshape(SB, LW)
        for i in range(q):
            dst[:, i * LW : (i + 1) * LW] = dot(r_.unroll[i], flat).astype(BF16)

    def pack_slots(value, dst):
        acc = None
        for i in range(q):
            term = dot_tn(r_.unroll[i], value[:, i * LW : (i + 1) * LW])
            acc = term if acc is None else acc + term
        dst[...] = acc.astype(BF16).reshape(S, BR, LW)

    for distance in range(3, Z):
        gather_step(distance, *first)
    gather_start(OUT)
    r_.tmpb[...] = cotf[...].astype(BF16)
    pack_tokens(r_.tmpb, r_.cbuf)
    gather_step(Z, *first)
    rows_start(r_.cbuf, r_.cland, r_.c_sem)
    gather_x()
    gather_end(SMALL)
    r_.smt[...] = r_.smf[...].astype(F32).T
    smt = r_.smt

    def vector(i):
        return smt[E + i : E + i + 1, :]

    r_.act1[...] = (n1[...] * vector(0) + vector(1)).astype(BF16)
    bias = r_.bias
    bias[:, 0:D] = jnp.broadcast_to(vector(2), (8, D))
    bias[:, D : 2 * D] = jnp.zeros((8, D), F32)
    bias[:, 2 * D : 3 * D] = jnp.broadcast_to(vector(3), (8, D))
    gather_end(BOTH)

    WT = D

    def qkv_step(j, carry):
        cut = pl.ds(pl.multiple_of(j * WT, WT), WT)
        value = dot(r_.act1[...], r_.wf_in[:, cut]) + bias[0:1, cut]
        r_.qkv[:, cut] = value.astype(BF16)
        return carry

    lax.fori_loop(2 * D // WT, 3 * D // WT, qkv_step, 0)
    gather_step(1, OUT)
    gather_end(OWN, FAR)
    lax.fori_loop(0, 2 * D // WT, qkv_step, 0)
    gather_step(2, OUT)

    low = iota((TP, LANES), 1) < HDIM
    key_ok = iota((TP, TP), 1) < T
    scale = HDIM ** (-0.5)

    def halves(value):
        zero = jnp.zeros_like(value)
        return jnp.where(low, value, zero), jnp.where(low, zero, value)

    def pair_cuts(i):
        return [pl.ds(pl.multiple_of(i * LANES + off, LANES), LANES) for off in (0, D, 2 * D)]

    def attend(i, carry):
        cut_q, cut_k, cut_v = pair_cuts(i)
        keys, values = r_.qkv[:, cut_k], r_.qkv[:, cut_v]
        found = []
        for a, query in enumerate(halves(r_.qkv[:, cut_q])):
            scores = dot_nt(query, keys) * scale
            weight = jnp.where(key_ok, jnp.exp(scores), 0.0)
            probs = weight * (1.0 / jnp.sum(weight, axis=-1, keepdims=True))
            r_.probs[2 * i + a] = probs
            found.append(dot(probs.astype(BF16), values))
        r_.ctx[:, cut_q] = jnp.where(low, found[0], found[1]).astype(BF16)
        return carry

    pairs = HEADS // 2
    lax.fori_loop(0, pairs // 2, attend, 0)
    for distance in range(3, Z):
        gather_step(distance, OUT)
    lax.fori_loop(pairs // 2, pairs, attend, 0)
    gather_step(Z, OUT)
    gather_end(OUT)
    for j in range(D // WT):
        cut = slice(j * WT, (j + 1) * WT)
        resid[:, cut] += dot(r_.ctx[...], r_.wf_out[:, cut]) + vector(4)[:, cut]
    normed_two, inv_two = normalise(resid[...])
    n2[...] = normed_two
    r_.hid[...] = (normed_two * vector(5) + vector(6)).astype(BF16)
    pack_tokens(r_.hid, r_.hbuf)
    rows_start(r_.hbuf, r_.hland, r_.h_sem)
    rows_wait(r_.cbuf, r_.cland, r_.c_sem)
    cot_copies = replicas_copies(r_.cland, r_.coth, r_.cx_sem)
    for copy in cot_copies:
        copy.start()

    def gates_of(rows):
        logits = dot(rows, r_.smf[...])
        weight = jnp.where(iota(logits.shape, 1) < E, jnp.exp(logits), 0.0)
        return weight / jnp.sum(weight, axis=-1, keepdims=True)

    gates = gates_of(r_.hid[...])
    lanes = iota((TP, LANES), 1)
    pair_gate = [
        jnp.sum(jnp.where(lanes == ids_v[:, k : k + 1], gates, 0.0), axis=-1, keepdims=True)
        for k in range(2)
    ]

    FT = D
    load_up.wait()
    load_down.wait()
    up, down = r_.up, r_.down
    unpack(r_.cland[...], r_.yrow)

    def early(j, carry):
        cut = pl.ds(pl.multiple_of(j * FT, FT), FT)
        r_.ga[:, cut] = dot_nt(r_.yrow[...], down[cut, :]).astype(BF16)
        return carry

    lax.fori_loop(0, FF // FT, early, 0)

    state.drain = True
    for a in (SMALL, BOTH, OWN, OUT):
        gather_start(a)
    to_core(FAR, me, r_.w_in.at[:, far_lanes])
    gather_lines(SMALL, BOTH, OWN, OUT)
    gather_x()
    rows_drain(r_.cbuf, r_.cland, r_.c_sem)
    rows_wait(r_.hbuf, r_.hland, r_.h_sem)
    hid_copies = replicas_copies(r_.hland, r_.hoth, r_.hx_sem)
    for copy in hid_copies:
        copy.start()
    unpack(r_.hland[...], r_.xrow)
    slot_lane = iota((N, LANES), 1)
    own_gates = gates_of(r_.xrow[...])
    own_gate = jnp.sum(jnp.where(slot_lane == me, own_gates, 0.0), axis=-1, keepdims=True)
    r_.gbrow[...] = (own_gate * r_.yrow[...].astype(F32)).astype(BF16)

    def gelu_kernel(pre):
        cumul = 0.5 * (1.0 + lax.erf(pre * SQRT_HALF))
        return pre * cumul, cumul + pre * jnp.exp(-0.5 * pre * pre) * INV_ROOT_TWO_PI

    r_.gacc[...] = jnp.zeros((N, D), F32)
    r_.ggate[...] = jnp.zeros((N, LANES), F32)
    r_.gatec[...] = jnp.broadcast_to(own_gate, (N, LANES))

    def middle(j, carry):
        cut = pl.ds(pl.multiple_of(j * FT, FT), FT)
        pre = dot(r_.xrow[...], up[:, cut]) + r_.upb[:, cut].astype(F32)
        act_val, slope = gelu_kernel(pre)
        grad_act = r_.ga[:, cut].astype(F32)
        r_.act[:, cut] = act_val.astype(BF16)
        grad_pre = (r_.gatec[:, 0:1] * grad_act * slope).astype(BF16)
        r_.gp[:, cut] = grad_pre
        r_.gacc[...] += dot_nt(grad_pre, up[:, cut])
        both = act_val * grad_act
        r_.ggate[...] += sum(both[:, f : f + LANES] for f in range(0, FT, LANES))
        return carry

    lax.fori_loop(0, FF // FT, middle, 0)
    gate_grad = jnp.sum(r_.ggate[...], axis=-1, keepdims=True) + jnp.sum(
        r_.yrow[...].astype(F32) * r_.downb[...].astype(F32), axis=-1, keepdims=True
    )
    picked = jnp.where(slot_lane == me, 1.0, 0.0)
    contrib = (own_gates * (picked - own_gate) * gate_grad).astype(BF16)
    r_.gacc[...] += dot_nt(contrib, r_.smf[...])
    rows_drain(r_.hbuf, r_.hland, r_.h_sem)
    pack_slots(r_.gacc[...].astype(BF16), r_.rbuf)
    rows_start(r_.rbuf, r_.rland, r_.r_sem)
    r_.rterm[...] = dot_tn(r_.xrow[...], contrib)

    for j in range(D // WT):
        cut = slice(j * WT, (j + 1) * WT)
        r_.gacc[:, cut] = dot(r_.act[...], down[:, cut]) + r_.downb[:, cut].astype(F32)
    pack_slots(r_.gacc[...].astype(BF16), r_.obuf)

    for copy in cot_copies + hid_copies:
        copy.wait_recv()
    unpack(r_.coth[0], r_.yo)
    unpack(r_.hoth[0], r_.xo)
    far_gates = gates_of(r_.xo[...])
    far_gate = jnp.sum(jnp.where(slot_lane == me, far_gates, 0.0), axis=-1, keepdims=True)
    r_.yo[...] = (far_gate * r_.yo[...].astype(F32)).astype(BF16)

    def far(j, carry):
        cut = pl.ds(pl.multiple_of(j * FT, FT), FT)
        whole = pl.ds(pl.multiple_of(mine * part + j * FT, LANES), FT)
        pre = dot(r_.xo[...], up[:, whole]) + r_.upb[:, whole].astype(F32)
        act_val, slope = gelu_kernel(pre)
        r_.act_o[:, cut] = act_val.astype(BF16)
        grad_act = dot_nt(r_.yo[...], down[whole, :])
        r_.gp_o[:, cut] = (grad_act * slope).astype(BF16)
        return carry

    lax.fori_loop(0, part // FT, far, 0)

    half = D // 2
    pieces = [(True, row, lane) for lane in range(0, part, D) for row in range(0, D, half)]
    pieces += [(False, row, 0) for row in range(0, part, half)]
    kept, depth = [], FF // D

    def weight_grads(count):
        for is_up, row, lane in pieces[len(kept) : len(kept) + count]:
            if is_up:
                there = pl.ds(pl.multiple_of(mine * part + lane, LANES), D)
                own_gp, far_gp = r_.gp[:, there], r_.gp_o[:, lane : lane + D]
                value = dot_tn(r_.xrow[:, row : row + half], own_gp)
                value = value + dot_tn(r_.xo[:, row : row + half], far_gp)
                dst = r_.o_up.at[row : row + half, lane : lane + D]
                if row == 0:
                    r_.o_upb[:, lane : lane + D] = jnp.sum(
                        own_gp.astype(F32), axis=0, keepdims=True
                    ) + jnp.sum(far_gp.astype(F32), axis=0, keepdims=True)
            else:
                there = pl.ds(pl.multiple_of(mine * part + row, LANES), half)
                value = dot_tn(r_.act[:, there], r_.gbrow[...])
                value = value + dot_tn(r_.act_o[:, row : row + half], r_.yo[...])
                dst = r_.o_down.at[row : row + half]
            at = len(kept)
            slot = r_.ga.at[0:half, at % depth * D : (at % depth + 1) * D]
            if at >= depth:
                kept[at - depth].wait()
            slot[...] = value.astype(BF16)
            copy = pltpu.make_async_copy(slot, dst, r_.keep_sem.at[at])
            copy.start()
            kept.append(copy)

    weight_grads(3)

    pending = []

    def launch(copies):
        for copy in copies:
            copy.start()
        pending.extend(copies)
        return copies

    def core_start(tag):
        own, from_core, _, _, _, _, sems = tag
        return launch(
            [
                copy_to(
                    own.at[other_core], from_core, sems.at[0], sems.at[1],
                    shard=shard_of(at_z, at_y, other_core),
                )
            ]
        )

    def y_start(tag, before):
        own, from_core, from_y, _, _, _, sems = tag
        for copy in before:
            copy.wait_recv()
        for y in range(Y):
            own[core, y] = (own[core, y].astype(F32) + from_core[y].astype(F32)).astype(BF16)
        return launch(
            [
                copy_to(
                    own.at[core, turn(at_y, dy, Y)], from_y.at[dy - 1], sems.at[2 * dy],
                    sems.at[2 * dy + 1], shard=shard_of(at_z, turn(at_y, dy, Y), core),
                )
                for dy in range(1, Y)
            ]
        )

    def lanes_of(tag, whose):
        wide = tag[0].shape[-1] // 2
        if wide % LANES:
            return slice(None)
        return pl.ds(pl.multiple_of(whose * wide, LANES), wide)

    def halved(tag):
        return tag[0].shape[-1] // 2 % LANES == 0

    def half_start(tag, before):
        own, _, from_y, _, _, from_half, sems = tag
        for copy in before:
            copy.wait_recv()
        total = own[core, at_y].astype(F32)
        for dy in range(1, Y):
            total = total + from_y[dy - 1].astype(F32)
        own[core, at_y] = total.astype(BF16)
        if not halved(tag):
            return []
        base = 2 * (Y + Z + R)
        return launch(
            [
                copy_to(
                    own.at[core, at_y, :, :, lanes_of(tag, 1 - mine)], from_half, sems.at[base],
                    sems.at[base + 1], replica=1 - mine,
                )
            ]
        )

    def z_start(tag, before):
        own, _, _, from_z, _, from_half, sems = tag
        mine_lanes = lanes_of(tag, mine)
        for copy in before:
            copy.wait_recv()
        if halved(tag):
            own[core, at_y, :, :, mine_lanes] = (
                own[core, at_y, :, :, mine_lanes].astype(F32) + from_half[...].astype(F32)
            ).astype(BF16)
        base = 2 * Y
        return launch(
            [
                copy_to(
                    own.at[core, at_y, turn(at_z, dz, Z), :, mine_lanes], from_z.at[dz - 1],
                    sems.at[base + 2 * dz - 2], sems.at[base + 2 * dz - 1],
                    shard=shard_of(turn(at_z, dz, Z), at_y, core),
                )
                for dz in range(1, Z)
            ]
        )

    def x_start(tag, before):
        own, _, _, from_z, from_x, _, sems = tag
        mine_lanes = lanes_of(tag, mine)
        for copy in before:
            copy.wait_recv()
        total = own[core, at_y, at_z, :, mine_lanes].astype(F32)
        for dz in range(1, Z):
            total = total + from_z[dz - 1].astype(F32)
        own[core, at_y, at_z, :, mine_lanes] = total.astype(BF16)
        base = 2 * Y + 2 * Z - 2
        return launch(
            [
                copy_to(
                    own.at[core, at_y, at_z, :, mine_lanes], from_x.at[0], sems.at[base],
                    sems.at[base + 1], replica=1 - mine,
                )
            ]
        )

    def finish(tag, before, out, lane_at=0):
        own, _, _, _, from_x, _, _ = tag
        for copy in before:
            copy.wait_recv()
        if halved(tag):
            wide = own.shape[-1] // 2
            here = pl.ds(pl.multiple_of(lane_at + mine * wide, LANES), wide)
            there = pl.ds(pl.multiple_of(lane_at + (1 - mine) * wide, LANES), wide)
            out[:, here] = own[core, at_y, at_z, :, lanes_of(tag, mine)].astype(F32)
            out[:, there] = from_x[0].astype(F32)
        else:
            out[0:K, :] = own[core, at_y, at_z].astype(F32) + from_x[0].astype(F32)

    def put_part(tag, lane_at, value):
        own = tag[0]
        wide = value.shape[1]
        low_value = value.astype(BF16)
        for z in range(Z):
            for y in range(Y):
                for c in range(2):
                    s = (z * Y + y) * 2 + c
                    own[c, y, z, :, lane_at : lane_at + wide] = low_value[s * K : (s + 1) * K, :]

    vecs = r_.vecs
    vecs[...] = jnp.zeros((LANES, D), F32)

    def put_vector(i, value):
        vecs[E + i : E + i + 1, :] = value

    rows_wait(r_.rbuf, r_.rland, r_.r_sem)
    rows_start(r_.obuf, r_.oland, r_.o_sem)
    flat_back = r_.rland[...].reshape(SB, LW)
    for i in range(q):
        r_.gn[:, i * LW : (i + 1) * LW] = dot(r_.place[0, i] + r_.place[1, i], flat_back)

    def norm_grad(grad_rows, normed, inv, gain, at_gain, at_bias):
        scaled = grad_rows * gain
        inner = (
            scaled
            - jnp.mean(scaled, axis=-1, keepdims=True)
            - normed * jnp.mean(scaled * normed, axis=-1, keepdims=True)
        )
        put_vector(at_gain, jnp.sum(grad_rows * normed, axis=0, keepdims=True))
        put_vector(at_bias, jnp.sum(grad_rows, axis=0, keepdims=True))
        return inner * inv

    gres[...] = cotf[...] + norm_grad(r_.gn[...], n2[...], inv_two, vector(5), 5, 6)
    put_vector(4, jnp.sum(gres[...], axis=0, keepdims=True))
    r_.tmpb[...] = gres[...].astype(BF16)
    for j in range(D // WT):
        cut = slice(j * WT, (j + 1) * WT)
        put_part(r_.rs_o, j * WT, dot_tn(r_.ctx[...], r_.tmpb[:, cut]))
    stage_o = core_start(r_.rs_o)
    for j in range(D // WT):
        cut = slice(j * WT, (j + 1) * WT)
        r_.gctx[:, cut] = dot_nt(r_.tmpb[...], r_.wf_out[cut, :]).astype(BF16)

    def attend_back(i, carry):
        cut_q, cut_k, cut_v = pair_cuts(i)
        query, keys, values = r_.qkv[:, cut_q], r_.qkv[:, cut_k], r_.qkv[:, cut_v]
        query_half, key_half, grad_half = halves(query), halves(keys), halves(r_.gctx[:, cut_q])
        grad_q = grad_k = grad_v = None
        for a in range(2):
            probs = r_.probs[2 * i + a]
            grad_probs = dot_nt(grad_half[a], values)
            inner = jnp.sum(probs * grad_probs, axis=-1, keepdims=True)
            grad_scores = (probs * (grad_probs - inner) * scale).astype(BF16)
            terms = (
                dot(grad_scores, key_half[a]),
                dot_tn(grad_scores, query_half[a]),
                dot_tn(probs.astype(BF16), grad_half[a]),
            )
            if a == 0:
                grad_q, grad_k, grad_v = terms
            else:
                grad_q, grad_k, grad_v = grad_q + terms[0], grad_k + terms[1], grad_v + terms[2]
        r_.gm[:, cut_q] = grad_q.astype(BF16)
        r_.gm[:, cut_k] = grad_k.astype(BF16)
        r_.gm[:, cut_v] = grad_v.astype(BF16)
        vecs[E + 2 : E + 3, cut_q] = jnp.sum(grad_q, axis=0, keepdims=True)
        vecs[E + 3 : E + 4, cut_q] = jnp.sum(grad_v, axis=0, keepdims=True)
        return carry

    lax.fori_loop(0, pairs, attend_back, 0)
    stage_o = y_start(r_.rs_o, stage_o)

    def proj_part(tag, at):
        wide = tag[0].shape[-1]
        step = WT if wide % WT == 0 else wide
        for j in range(0, wide, step):
            put_part(tag, j, dot_tn(r_.act1[...], r_.gm[:, at + j : at + j + step]))
        return core_start(tag)

    stage_v = proj_part(r_.rs_v, 2 * D)
    stage_k = proj_part(r_.rs_k, D)
    stage_o = half_start(r_.rs_o, stage_o)
    stage_v = y_start(r_.rs_v, stage_v)
    stage_q = proj_part(r_.rs_q, 0)
    stage_k = y_start(r_.rs_k, stage_k)
    stage_o = z_start(r_.rs_o, stage_o)
    for j in range(D // WT):
        cut = slice(j * WT, (j + 1) * WT)
        r_.gn[:, cut] = dot_nt(r_.gm[...], r_.wf_in[cut, :])
    stage_q = y_start(r_.rs_q, stage_q)
    grad_tok = gres[...] + norm_grad(r_.gn[...], n1[...], inv_one, vector(0), 0, 1)
    r_.o_grad[...] = grad_tok[0:T].astype(BF16)
    put_part(r_.rs_s, 0, vecs[...].T + r_.rterm[...])
    stage_s = core_start(r_.rs_s)
    stage_v = half_start(r_.rs_v, stage_v)
    stage_s = y_start(r_.rs_s, stage_s)
    stage_o = x_start(r_.rs_o, stage_o)

    weight_grads(1)
    stage_v = z_start(r_.rs_v, stage_v)
    weight_grads(1)
    stage_k = half_start(r_.rs_k, stage_k)
    rows_wait(r_.obuf, r_.oland, r_.o_sem)
    flat_out = r_.oland[...].reshape(SB, LW)
    for i in range(q):
        cut = slice(i * LW, (i + 1) * LW)
        total = resid[:, cut]
        for k in range(2):
            total = total + pair_gate[k] * dot(r_.place[k, i], flat_out)
        r_.o_rows[:, cut] = total[0:T].astype(BF16)

    stage_k = z_start(r_.rs_k, stage_k)
    finish(r_.rs_o, stage_o, r_.o_out)
    rows_drain(r_.rbuf, r_.rland, r_.r_sem)
    weight_grads(1)
    stage_v = x_start(r_.rs_v, stage_v)
    stage_q = half_start(r_.rs_q, stage_q)
    stage_s = half_start(r_.rs_s, stage_s)
    stage_k = x_start(r_.rs_k, stage_k)
    stage_q = z_start(r_.rs_q, stage_q)
    stage_s = z_start(r_.rs_s, stage_s)
    finish(r_.rs_v, stage_v, r_.o_proj, 2 * D)
    weight_grads(len(pieces) - len(kept))
    total_grad = jnp.sum(r_.gbrow[...].astype(F32), axis=0, keepdims=True)
    total_grad = total_grad + jnp.sum(r_.yo[...].astype(F32), axis=0, keepdims=True)
    bias[0:1, 0:D] = total_grad
    r_.o_downb[...] = bias[0:1, pl.ds(pl.multiple_of(mine * (D // R), LANES), D // R)]
    rows_drain(r_.obuf, r_.oland, r_.o_sem)
    for copy in cot_copies + hid_copies:
        copy.wait_send()
    stage_q = x_start(r_.rs_q, stage_q)
    stage_s = x_start(r_.rs_s, stage_s)
    for copy in kept[-depth:]:
        copy.wait()
    for copy in pending:
        copy.wait_send()
    finish(r_.rs_k, stage_k, r_.o_proj, D)
    finish(r_.rs_q, stage_q, r_.o_proj)
    finish(r_.rs_s, stage_s, turned)
    r_.o_small[...] = turned[...].T[0 : r_.o_small.shape[0], 0:K]


def call_block(plan, *arrays):
    S, R, TP, FF, E = plan.S, plan.R, plan.TP, plan.FF, plan.E
    K, q, BR, LW, SB, N, Z, Y, part = (
        plan.K, plan.q, plan.BR, plan.LW, plan.SB, plan.N, plan.Z, plan.Y, plan.part,
    )
    vmem = pl.BlockSpec(memory_space=pltpu.VMEM)
    anyw = pl.BlockSpec(memory_space=pl.ANY)
    outs = dict(
        o_rows=((plan.T, D), BF16, vmem),
        o_grad=((plan.T, D), BF16, vmem),
        o_proj=((K, 3 * D), F32, vmem),
        o_out=((K, D), F32, vmem),
        o_small=((-(-(E + VECTORS) // 8) * 8, K), F32, vmem),
        o_up=((D, part), BF16, anyw),
        o_upb=((1, part), F32, vmem),
        o_down=((part, D), BF16, anyw),
        o_downb=((1, D // R), F32, vmem),
    )

    def landing(wide):
        part_wide = wide // 2 if wide // 2 % LANES == 0 else wide
        return (
            pltpu.VMEM((2, Y, Z, K, wide), BF16),
            pltpu.VMEM((Y, Z, K, wide), BF16),
            pltpu.VMEM((max(Y - 1, 1), Z, K, wide), BF16),
            pltpu.VMEM((max(Z - 1, 1), K, part_wide), BF16),
            pltpu.VMEM((max(R - 1, 1), K, part_wide), BF16),
            pltpu.VMEM((Z, K, part_wide), BF16),
            pltpu.SemaphoreType.DMA((2 * (Y + Z + R) + 2,)),
        )

    def pairs_of(*extent):
        return pltpu.SemaphoreType.DMA(extent)

    rows = pltpu.VMEM((S, BR, LW), BF16)
    far_rows = pltpu.VMEM((R - 1, S, BR, LW), BF16)
    wide_rows = pltpu.VMEM((TP, D), F32)
    half_rows = pltpu.VMEM((TP, D), BF16)
    slot_rows = pltpu.VMEM((N, D), BF16)
    scratch = dict(
        up=pltpu.VMEM((D, FF), BF16),
        down=pltpu.VMEM((FF, D), BF16),
        wf_in=pltpu.VMEM((D, 3 * D), BF16),
        wf_out=pltpu.VMEM((D, D), BF16),
        smf=pltpu.VMEM((D, LANES), BF16),
        smt=pltpu.VMEM((LANES, D), F32),
        turned=pltpu.VMEM((LANES, LANES), F32),
        small=pltpu.VMEM((K, LANES), BF16),
        pairs_at=pltpu.VMEM((LANES, -(-TP // LANES) * LANES), F32),
        place=pltpu.VMEM((2, q, TP, SB), BF16),
        unroll=pltpu.VMEM((q, N, SB), BF16),
        cotf=wide_rows, n1=wide_rows, n2=wide_rows, resid=wide_rows, gres=wide_rows,
        gn=wide_rows,
        tmpb=half_rows, act1=half_rows, hid=half_rows, ctx=half_rows,
        bias=pltpu.VMEM((8, 3 * D), F32),
        qkv=pltpu.VMEM((TP, 3 * D), BF16),
        gm=pltpu.VMEM((TP, 3 * D), BF16),
        probs=pltpu.VMEM((HEADS, TP, TP), F32),
        cbuf=rows, cland=rows, hbuf=rows, hland=rows, rland=rows, oland=rows,
        coth=far_rows, hoth=far_rows,
        yrow=slot_rows, xrow=slot_rows, gbrow=slot_rows,
        xo=slot_rows,
        ga=pltpu.VMEM((N, FF), BF16),
        act=pltpu.VMEM((N, FF), BF16),
        gp=pltpu.VMEM((N, FF), BF16),
        act_o=pltpu.VMEM((N, part), BF16),
        gp_o=pltpu.VMEM((N, part), BF16),
        stage=pltpu.VMEM((1, N, D), F32),
        ggate=pltpu.VMEM((N, LANES), F32),
        gatec=pltpu.VMEM((N, LANES), F32),
        rterm=pltpu.VMEM((D, LANES), F32),
        vecs=pltpu.VMEM((LANES, D), F32),
        rs_o=landing(D), rs_v=landing(D), rs_k=landing(D), rs_q=landing(D), rs_s=landing(LANES),
        load_sem=pairs_of(2),
        ag_send=pairs_of(5, 3 + Y, S),
        ag_recv=pairs_of(5, S),
        c_sem=pairs_of(2, S),
        h_sem=pairs_of(2, S),
        r_sem=pairs_of(2, S),
        o_sem=pairs_of(2, S),
        cx_sem=pairs_of(2, R),
        hx_sem=pairs_of(2, R),
        keep_sem=pairs_of(2 * (part // D) + 2 * part // D),
    )
    return pl.pallas_call(
        functools.partial(block_kernel, plan, list(outs)),
        out_shape=[jax.ShapeDtypeStruct(o[0], o[1]) for o in outs.values()],
        in_specs=[vmem] * (9 + VECTORS) + [anyw] * 2,
        out_specs=[o[2] for o in outs.values()],
        scratch_shapes=scratch,
        compiler_params=pltpu.CompilerParams(
            collective_id=0, has_side_effects=True, vmem_limit_bytes=60 * 1024 * 1024
        ),
        cost_estimate=pl.CostEstimate(
            flops=12 * N * D * FF, bytes_accessed=4 * D * FF, transcendentals=2 * N * FF
        ),
    )(*arrays)


def outputs_kernel(plan, count, *refs):
    srcs, small, rest = refs[:count], refs[count], refs[count + 1 :]
    dsts, vectors, router = rest[:count], rest[count : count + VECTORS], rest[count + VECTORS]
    lands, wides, sems = rest[count + VECTORS + 1 : 2 * count + VECTORS + 1], rest[-3:-1], rest[-1]
    steps = []
    for n, (src, land, dst) in enumerate(zip(srcs, lands, dsts)):
        cuts = 6 if n < 2 else 1
        rows = src.shape[0] // cuts
        wide = wides[n] if n < 2 else land
        for cut in range(cuts):
            part = pl.ds(cut * rows, rows)
            at = len(steps)
            fetch = pltpu.make_async_copy(src.at[part], land.at[part], sems.at[0, at])
            fetch.start()
            store = pltpu.make_async_copy(wide.at[part], dst.at[part], sems.at[1, at])
            steps.append((fetch, land, wide, part, store))
    for i, vector in enumerate(vectors):
        vector[...] = small[plan.E + i : plan.E + i + 1, :].reshape(plan.K)
    router[...] = small[0 : plan.E, :]
    for fetch, land, wide, part, store in steps:
        fetch.wait()
        if wide is not land:
            wide[part, :] = land[part, :].astype(F32)
        store.start()
    for step in steps:
        step[-1].wait()


def call_outputs(plan, arrays, small):
    vmem = pl.BlockSpec(memory_space=pltpu.VMEM)
    anyw = pl.BlockSpec(memory_space=pl.ANY)
    count = len(arrays)
    return pl.pallas_call(
        functools.partial(outputs_kernel, plan, count),
        out_shape=[jax.ShapeDtypeStruct(a.shape, F32 if n < 2 else a.dtype) for n, a in enumerate(arrays)]
        + [jax.ShapeDtypeStruct((plan.K,), F32)] * VECTORS
        + [jax.ShapeDtypeStruct((plan.E, plan.K), F32)],
        in_specs=[anyw] * count + [vmem],
        out_specs=[anyw] * count + [vmem] * (VECTORS + 1),
        scratch_shapes=[pltpu.VMEM(a.shape, a.dtype) for a in arrays]
        + [pltpu.VMEM(a.shape, F32) for a in arrays[:2]]
        + [pltpu.SemaphoreType.DMA((2, 12 + count))],
        compiler_params=pltpu.CompilerParams(vmem_limit_bytes=60 * 1024 * 1024),
    )(*arrays, small)


def body(
    tokens, cotangent, norm1_gain, norm1_bias, proj_in, query_bias, value_bias, proj_out, out_bias,
    norm2_gain, norm2_bias, router, up_weight, up_bias, down_weight, down_bias, expert_ids, slot_ids,
):
    shards, replicas = lax.axis_size("shard"), lax.axis_size("replica")
    rows = tokens.shape[0] * tokens.shape[1]
    plan = Plan(shards, replicas, rows, up_weight.shape[2], up_weight.shape[0])
    if plan.part % D or plan.N < D // 2 or up_weight.shape[0] != 1 or tokens.shape[0] != 1:
        return plain_body(
            tokens, cotangent, norm1_gain, norm1_bias, proj_in, query_bias, value_bias, proj_out,
            out_bias, norm2_gain, norm2_bias, router, up_weight, up_bias, down_weight, down_bias,
            expert_ids, slot_ids,
        )
    (o_rows, o_grad, o_proj, o_out, o_small, o_up, o_upb, o_down, o_downb) = call_block(
        plan, tokens.reshape(rows, D), cotangent.reshape(rows, D), proj_in, proj_out, router.T,
        expert_ids.T, slot_ids.T, up_bias, down_bias, norm1_gain, norm1_bias, query_bias, value_bias,
        out_bias, norm2_gain, norm2_bias, up_weight[0], down_weight[0],
    )
    (o_up, o_down, o_rows, o_grad, o_proj, o_out, o_upb, o_downb, *vec, o_router) = call_outputs(
        plan, [o_up, o_down, o_rows, o_grad, o_proj, o_out, o_upb, o_downb], o_small
    )
    return (
        o_rows.reshape(tokens.shape),
        o_grad.reshape(tokens.shape),
        vec[0], vec[1], o_proj, vec[2], vec[3], o_out, vec[4], vec[5], vec[6], o_router.T,
        o_up[None], o_upb, o_down[None], o_downb,
    )


def fits_kernel(mesh):
    shards, replicas = mesh.shape["shard"], mesh.shape["replica"]
    return shards % 2 == 0 and D % shards == 0 and (D // shards) % 16 == 0 and replicas == 2


def solution(mesh):
    in_specs = (
        P(("replica", "shard"), None, None),
        P(("replica", "shard"), None, None),
        P("shard"),
        P("shard"),
        P("shard", None),
        P("shard"),
        P("shard"),
        P("shard", None),
        P("shard"),
        P("shard"),
        P("shard"),
        P("shard", None),
        P("shard", None, None),
        P("shard", None),
        P("shard", None, None),
        P("shard", None),
        P(("replica", "shard"), None),
        P(("replica", "shard"), None),
    )
    out_specs = (
        P(("replica", "shard"), None, None),
        P(("replica", "shard"), None, None),
        P("shard"),
        P("shard"),
        P("shard", None),
        P("shard"),
        P("shard"),
        P("shard", None),
        P("shard"),
        P("shard"),
        P("shard"),
        P("shard", None),
        P("shard", None, "replica"),
        P("shard", "replica"),
        P("shard", "replica", None),
        P("shard", "replica"),
    )
    chosen = body if fits_kernel(mesh) else plain_body
    return jax.shard_map(chosen, mesh=mesh, in_specs=in_specs, out_specs=out_specs, check_vma=False)
```
